128 devices in a mesh: dp: 2 (over core), seq: 4 (over x), tensor: 16 (over y, z).
Axes of the slice: x: 4, y: 4, z: 4, core: 2. Of those that a mesh axis runs over, the one named last changes fastest.
Arguments:
- tokens: bfloat16 [16384, 4096], P(('dp', 'seq', 'tensor')), may hold values from -6 to 6
- cotangent: bfloat16 [16384, 14336], P(('dp', 'seq', 'tensor')), may hold values from -0.046875 to 0.046875
- master: bfloat16 [8, 336, 128, 128], P(None, 'tensor'), as said below
- block_ids: int32 [8, 336], P(None, 'tensor'), may hold values from 0 to 223, as said below
- live_count: int32 [8, 16], P(None, 'tensor'), may hold values from 1 to 21, as said below
Outputs:
- outputs: bfloat16 [16384, 14336], P(('dp', 'seq', 'tensor'))
- w_grad: float32 [8, 336, 128, 128], P(('dp', 'seq'), 'tensor')
The draws below stay inside these ranges and needn't reach their ends.
Inputs may be any that keep to these rules, and one draw needn't show every extreme that they name: Within each group t the 168 entries block_ids[:, t * 21 : (t + 1) * 21] are distinct. `live_count`: in every group one owner uses all 21 slots. `master`: in every block one entry has the largest magnitude, and no entry of a block, divided by that magnitude over 7, lies within 0.1 of a half-integer.
All inputs are finite; a program needn't handle non-finite values. Where the reference program divides by a largest or mean magnitude, that divisor is 1e-20 or more.
Results may differ from the reference program's by a relative error of at most 0.005.
Values may be sent and summed in bfloat16 or wider, within the bound.
A program may use at most 192 MiB of HBM per device.

```python
import math
import jax
import jax.numpy as jnp
from jax import lax

D = 4096
FF = 14336
BS = 128
SLOTS = 21
TGROUPS = 16
OWNERS = 8
ROW_BLOCKS = 32
COL_BLOCKS = 7
TOKENS = 16384


def draw_master(key, part):
    subkeys = jax.random.split(key, 5)
    shape = (OWNERS, TGROUPS * SLOTS, BS, BS)
    block_shape = (OWNERS, TGROUPS * SLOTS, 1, 1)
    integer_part = jax.random.randint(subkeys[0], shape, -6, 7).astype(jnp.float32)
    fraction = jax.random.uniform(subkeys[1], shape, jnp.float32, -0.3, 0.3)
    scales = jnp.exp(jax.random.uniform(subkeys[2], block_shape, jnp.float32, math.log(0.0015), math.log(0.015)))
    peak_spot = jax.random.randint(subkeys[3], block_shape, 0, BS * BS)
    peak_sign = (2 * jax.random.randint(subkeys[4], block_shape, 0, 2) - 1).astype(jnp.float32)
    position = lax.broadcasted_iota(jnp.int32, (1, 1, BS, BS), 2) * BS + lax.broadcasted_iota(jnp.int32, (1, 1, BS, BS), 3)
    values = jnp.where(position == peak_spot, 7.0 * peak_sign, integer_part + fraction) * scales
    return values.astype(jnp.bfloat16)


def draw_block_ids(key, part):
    subkeys = jax.random.split(key, TGROUPS)
    orders = jax.vmap(lambda one_key: jax.random.permutation(one_key, ROW_BLOCKS * COL_BLOCKS))(subkeys)
    chosen = orders[:, :OWNERS * SLOTS].astype(jnp.int32)
    return chosen.reshape(TGROUPS, OWNERS, SLOTS).transpose(1, 0, 2).reshape(OWNERS, TGROUPS * SLOTS)


def draw_live_count(key, part):
    subkeys = jax.random.split(key, 2)
    lowest = max(1, 2 * SLOTS // 5)
    counts = jax.random.randint(subkeys[0], (OWNERS, TGROUPS), lowest, SLOTS + 1)
    fullest = jax.random.randint(subkeys[1], (1, TGROUPS), 0, OWNERS)
    owner_row = lax.broadcasted_iota(jnp.int32, (OWNERS, TGROUPS), 0)
    return jnp.where(owner_row == fullest, SLOTS, counts).astype(jnp.int32)


def steps_of(own_key, dims, shards, low, largest):
    factor_of = 1.0
    for dim, blocks in shards:
        steps = jax.random.uniform(jax.random.fold_in(jax.random.fold_in(own_key, 6), dim), (blocks,), jnp.float32, low / len(shards), largest / len(shards))
        factor_of = factor_of * jnp.repeat(jnp.exp(steps), dims[dim] // blocks).reshape((-1,) + (1,) * (len(dims) - 1 - dim))
    return factor_of


def bell_draw(own_key, extent, spread, limit, cuts=(), kind=jnp.bfloat16):
    values = jax.random.normal(own_key, extent, jnp.float32) * spread
    if len(cuts) > 0:
        values = steps_of(own_key, extent, cuts, -0.22, 0.18) * values
    return jnp.clip(values, min=-limit, max=limit).astype(kind)


def setup_inputs(seed: int = 0) -> dict:
    seeds = jax.random.split(jax.random.key(seed), 6)
    return {
        "tokens": bell_draw(seeds[0], (TOKENS, D), 1.0, 6.0, ((0, 128),)),
        "cotangent": bell_draw(seeds[1], (TOKENS, FF), (TOKENS ** -0.5), 0.046875, ((0, 128),)),
        "master": draw_master(jax.random.fold_in(seeds[5], 71), 0),
        "block_ids": draw_block_ids(jax.random.fold_in(seeds[5], 71), 0),
        "live_count": draw_live_count(jax.random.fold_in(seeds[5], 71), 0),
    }


def fake_quant(master, live_mask):
    master_wide = master.astype(jnp.float32)
    block_peak = jnp.max(jnp.abs(master_wide), axis=(-2, -1), keepdims=True) + 1e-6
    levels = jnp.floor(master_wide * (7.0 / block_peak) + 0.5)
    return (levels * (block_peak / 7.0) * live_mask[..., None, None]).astype(jnp.bfloat16)


def reference(tokens, cotangent, master, block_ids, live_count):
    live_mask = (jnp.arange(SLOTS, dtype=jnp.int32)[None, None, :] < live_count[:, :, None]).astype(jnp.float32)
    live_mask = live_mask.reshape(OWNERS, TGROUPS * SLOTS)
    quantized = fake_quant(master, live_mask)
    per_group = quantized.reshape(OWNERS, TGROUPS, SLOTS, BS, BS).transpose(1, 0, 2, 3, 4).reshape(TGROUPS, OWNERS * SLOTS, BS, BS)
    slot_ids = block_ids.reshape(OWNERS, TGROUPS, SLOTS).transpose(1, 0, 2).reshape(TGROUPS, OWNERS * SLOTS).astype(jnp.int32)
    group_index = jnp.arange(TGROUPS, dtype=jnp.int32)[:, None]
    weight = jnp.zeros((TGROUPS, ROW_BLOCKS * COL_BLOCKS, BS, BS), jnp.bfloat16)
    weight = weight.at[group_index, slot_ids].set(per_group)
    weight = weight.reshape(TGROUPS, ROW_BLOCKS, COL_BLOCKS, BS, BS).transpose(1, 3, 0, 2, 4).reshape(D, FF)
    outputs = jnp.dot(tokens, weight, preferred_element_type=jnp.float32).astype(jnp.bfloat16)
    full_grad = jnp.dot(tokens.T, cotangent, preferred_element_type=jnp.float32)
    grid_blocks = full_grad.reshape(ROW_BLOCKS, BS, TGROUPS, COL_BLOCKS, BS).transpose(2, 0, 3, 1, 4)
    grid_blocks = grid_blocks.reshape(TGROUPS, ROW_BLOCKS * COL_BLOCKS, BS, BS)
    picked = grid_blocks[group_index, slot_ids]
    picked = picked.reshape(TGROUPS, OWNERS, SLOTS, BS, BS).transpose(1, 0, 2, 3, 4).reshape(OWNERS, TGROUPS * SLOTS, BS, BS)
    w_grad = picked * live_mask[..., None, None]
    return outputs, w_grad
```

```python
import functools

import jax
import jax.numpy as jnp
from jax import lax
from jax.experimental import pallas as pl
from jax.experimental.pallas import tpu as pltpu
from jax.sharding import PartitionSpec as P

BS = 128
ROWS = 32
COLS = 7
OWN = 8
SLOTS = 21
NSLOT = OWN * SLOTS
QTR = NSLOT // 4
HALF = QTR // 2
LO, HI = 11, 10
WID = COLS * BS
TOK = 128
MESH = pl.DeviceIdType.MESH
F32 = jnp.float32
BF16 = jnp.bfloat16


class Names:
    def __init__(self):
        self.n = 0
        self.at = {}

    def get(self, key, width=1):
        if key not in self.at:
            self.at[key] = self.n
            self.n += width
        return self.at[key]


def fake_quant(master, live_mask):
    master_wide = master.astype(jnp.float32)
    block_peak = jnp.max(jnp.abs(master_wide), axis=(-2, -1), keepdims=True) + 1e-06
    levels = jnp.floor(master_wide * (7.0 / block_peak) + 0.5)
    return (levels * (block_peak / 7.0) * live_mask[..., None, None]).astype(jnp.bfloat16)


def make_kernel(names_s, names_r, names_l):
    def kernel(
        tok_hbm, cot_hbm, q_hbm, tab_hbm,
        out_hbm, wg_hbm, wc_hbm,
        tok_v, cb, crel, gw, wst, ob, orel, gs, ra1, ra2, ry1, ry2, rz1, rz2, rb1, rb2, fin,
        tabv, tabs, ssem, rsem, lsem,
    ):
        k = lax.axis_index("dp")
        x = lax.axis_index("seq")
        t_me = lax.axis_index("tensor")
        y, z = t_me // 4, t_me % 4
        xp, xm, xo = (x + 1) % 4, (x + 3) % 4, (x + 2) % 4
        yp, ym, yo = (y + 1) % 4, (y + 3) % 4, (y + 2) % 4
        zp, zm, zo = (z + 1) % 4, (z + 3) % 4, (z + 2) % 4
        kk = 1 - k

        def dev(k_=None, x_=None, y_=None, z_=None):
            kd = k if k_ is None else k_
            xd = x if x_ is None else x_
            yd = y if y_ is None else y_
            zd = z if z_ is None else z_
            return (kd, xd, yd * 4 + zd)

        partner = dev(k_=kk)
        devs = {
            "x+": dev(x_=xp), "x-": dev(x_=xm), "y+": dev(y_=yp), "y-": dev(y_=ym), "y2": dev(y_=yo),
            "z+": dev(z_=zp), "z-": dev(z_=zm), "p": partner,
            "z+0": dev(k_=0, z_=zp), "z+1": dev(k_=1, z_=zp), "z-0": dev(k_=0, z_=zm), "z-1": dev(k_=1, z_=zm),
        }

        def remote(key, src, dst, to, skey=None, rkey=None, roff=None, rwidth=1):
            si = names_s.get(skey or key)
            ri = names_r.get(rkey or key, rwidth)
            if roff is not None:
                ri = ri + roff
            return pltpu.make_async_remote_copy(
                src_ref=src, dst_ref=dst, send_sem=ssem.at[si], recv_sem=rsem.at[ri],
                device_id=devs[to], device_id_type=MESH,
            )

        def local(key, src, dst):
            return pltpu.make_async_copy(src, dst, lsem.at[names_l.get(key)])

        def slot(z_, k_):
            return pl.ds(pl.multiple_of((z_ * 2 + k_) * TOK, TOK), TOK)

        def part(z_, k_, lo):
            return pl.ds(pl.multiple_of((z_ * 2 + k_) * TOK + lo, 64), 64)

        def cols(group_y, group_z):
            return pl.ds(pl.multiple_of((group_y * 4 + group_z) * WID, 128), WID)

        peers = [partner, devs["x+"], devs["x-"], devs["y+"], devs["y-"], devs["y2"],
                 devs["z+0"], devs["z+1"], devs["z-0"], devs["z-1"]]
        barrier = pltpu.get_barrier_semaphore()
        for peer in peers:
            pl.semaphore_signal(barrier, inc=1, device_id=peer, device_id_type=MESH)
        pl.semaphore_wait(barrier, len(peers))

        d = [(y + 4 - (2 * k + j)) % 4 for j in (0, 1)]
        tok2 = tok_hbm

        t_own = local("t", tok2, tok_v.at[slot(z, k)])
        T0 = remote("T0", tok2, tok_v.at[slot(z, k)], "z+")
        T1 = remote("T1", tok2, tok_v.at[slot(z, k)], "z-")
        T2 = remote("T2", tok2, tok_v.at[slot(z, k)], "p")
        T0r = remote("T0", tok2, tok_v.at[slot(zm, k)], "z+")
        T1r = remote("T1", tok2, tok_v.at[slot(zp, k)], "z-")
        T2r = remote("T2", tok2, tok_v.at[slot(z, kk)], "p")
        T3 = remote("T3", tok_v.at[slot(zm, k)], tok_v.at[slot(zm, k)], "p")
        T4 = remote("T4", tok_v.at[slot(zp, k)], tok_v.at[slot(zp, k)], "p")
        T3r = remote("T3", tok_v.at[slot(zm, kk)], tok_v.at[slot(zm, kk)], "p")
        T4r = remote("T4", tok_v.at[slot(zp, kk)], tok_v.at[slot(zp, kk)], "p")
        T5 = remote("T5", tok_v.at[part(zm, k, 0)], tok_v.at[part(zm, k, 0)], "z+")
        T6 = remote("T6", tok_v.at[part(zp, k, 64)], tok_v.at[part(zp, k, 64)], "z-")
        T5r = remote("T5", tok_v.at[part(zo, k, 0)], tok_v.at[part(zo, k, 0)], "z+")
        T6r = remote("T6", tok_v.at[part(zo, k, 64)], tok_v.at[part(zo, k, 64)], "z-")
        T7 = remote("T7", tok_v.at[part(zo, k, 0)], tok_v.at[part(zo, k, 0)], "p")
        T8 = remote("T8", tok_v.at[part(zo, k, 64)], tok_v.at[part(zo, k, 64)], "p")
        T7r = remote("T7", tok_v.at[part(zo, kk, 0)], tok_v.at[part(zo, kk, 0)], "p")
        T8r = remote("T8", tok_v.at[part(zo, kk, 64)], tok_v.at[part(zo, kk, 64)], "p")

        def cot(group_y, group_z):
            return cot_hbm.at[:, cols(group_y, group_z)]

        c_own = [local(f"c{j}", cot(2 * k + j, z), cb.at[j, slot(z, k)]) for j in (0, 1)]
        c_sends = []
        for j in (0, 1):
            row = []
            for k_ in (0, 1):
                row.append(remote(f"C1{j}{k_}", cot(2 * k_ + j, zp), cb.at[j, slot(z, k)], f"z+{k_}",
                                  rkey=f"C1r{j}", roff=k, rwidth=2))
                row.append(remote(f"C2{j}{k_}", cot(2 * k_ + j, zm), cb.at[j, slot(z, k)], f"z-{k_}",
                                  rkey=f"C2r{j}", roff=k, rwidth=2))
            row.append(remote(f"C3{j}", cot(j, zo), crel.at[0, j], "z+"))
            row.append(remote(f"C4{j}", cot(2 + j, zo), crel.at[1, j], "z-"))
            row.append(remote(f"C0{j}", cot(2 * kk + j, z), cb.at[j, slot(z, k)], "p"))
            c_sends.append(row)
        C3r = [remote(f"C3{j}", cot(j, zo), crel.at[0, j], "z+") for j in (0, 1)]
        C4r = [remote(f"C4{j}", cot(2 + j, zo), crel.at[1, j], "z-") for j in (0, 1)]
        C5 = [remote(f"C5{j}", crel.at[0, j], cb.at[j, slot(zm, k)], "z+0", rkey=f"C5r{j}", roff=k, rwidth=2) for j in (0, 1)]
        C6 = [remote(f"C6{j}", crel.at[1, j], cb.at[j, slot(zp, k)], "z-1", rkey=f"C5r{j}", roff=k, rwidth=2) for j in (0, 1)]

        def c_recvs(j):
            out = [remote(f"C0{j}", cot(j, z), cb.at[j, slot(z, kk)], "p")]
            for i in (0, 1):
                out.append(remote(f"C1{j}0", cot(j, z), cb.at[j, slot(zm, i)], "z+", rkey=f"C1r{j}", roff=i, rwidth=2))
                out.append(remote(f"C2{j}0", cot(j, z), cb.at[j, slot(zp, i)], "z-", rkey=f"C2r{j}", roff=i, rwidth=2))
                out.append(remote(f"C5{j}", cot(j, z), cb.at[j, slot(zo, i)], "z+", rkey=f"C5r{j}", roff=i, rwidth=2))
            return out

        def wq(j, q):
            return wc_hbm.at[j, pl.ds(q * QTR, QTR)]

        def wlo(j, q):
            return wc_hbm.at[j, pl.ds(q * QTR, HALF)]

        def whi(j, q):
            return wc_hbm.at[j, pl.ds(q * QTR + HALF, HALF)]

        q_mine = q_hbm.at[pl.ds(x * QTR, QTR)]
        W0 = [remote(f"W0{j}", q_mine, wq(j, x), "y+") for j in (0, 1)]
        W1 = [remote(f"W1{j}", q_mine, wq(j, x), "y-") for j in (0, 1)]
        W2 = [remote(f"W2{j}", wlo(j, x), wlo(j, x), "y+") for j in (0, 1)]
        W3 = [remote(f"W3{j}", whi(j, x), whi(j, x), "y-") for j in (0, 1)]
        W4 = [remote(f"W4{j}", wq(j, x), wq(j, x), "x+") for j in (0, 1)]
        W5 = [remote(f"W5{j}", wq(j, x), wq(j, x), "x-") for j in (0, 1)]
        W4r = [remote(f"W4{j}", wq(j, xm), wq(j, xm), "x+") for j in (0, 1)]
        W5r = [remote(f"W5{j}", wq(j, xp), wq(j, xp), "x-") for j in (0, 1)]
        W6 = [remote(f"W6{j}", wlo(j, xm), wlo(j, xm), "x+") for j in (0, 1)]
        W7 = [remote(f"W7{j}", whi(j, xp), whi(j, xp), "x-") for j in (0, 1)]
        W6r = [remote(f"W6{j}", wlo(j, xo), wlo(j, xo), "x+") for j in (0, 1)]
        W7r = [remote(f"W7{j}", whi(j, xo), whi(j, xo), "x-") for j in (0, 1)]
        V = [[remote(f"V{j}{i}", tab_hbm, tabv.at[j], to) for i, to in enumerate(("y+", "y-", "y2"))] for j in (0, 1)]

        def tab_start():
            for j in (0, 1):
                @pl.when(d[j] == 0)
                def _(j=j):
                    for copy in V[j]:
                        copy.start()
                    local(f"v{j}", tab_hbm, tabv.at[j]).start()

        def tab_finish():
            for j in (0, 1):
                @pl.when(d[j] == 0)
                def _(j=j):
                    local(f"v{j}", tab_hbm, tabv.at[j]).wait()

                for i, dist in enumerate((1, 3, 2)):
                    @pl.when(d[j] == dist)
                    def _(j=j, i=i):
                        V[j][i].wait_recv()
            cp = local("tab", tabv, tabs)
            cp.start()
            cp.wait()

        def w_first():
            for j in (0, 1):
                @pl.when(d[j] == 0)
                def _(j=j):
                    W0[j].start()
                    W1[j].start()

        def w_second():
            for j in (0, 1):
                @pl.when(d[j] == 1)
                def _(j=j):
                    W0[j].wait_recv()
                    W2[j].start()
                    W4[j].start()
                    W5[j].start()

                @pl.when(d[j] == 3)
                def _(j=j):
                    W1[j].wait_recv()
                    W3[j].start()
                    W4[j].start()
                    W5[j].start()

        def w_third():
            for j in (0, 1):
                @pl.when(d[j] == 2)
                def _(j=j):
                    W2[j].wait_recv()
                    W3[j].wait_recv()
                    W4[j].start()
                    W5[j].start()

        def w_fourth():
            for j in (0, 1):
                @pl.when(d[j] != 0)
                def _(j=j):
                    W4r[j].wait_recv()
                    W6[j].start()
                    W5r[j].wait_recv()
                    W7[j].start()

        def w_load(j):
            @pl.when(d[j] != 0)
            def _():
                W6r[j].wait_recv()
                W7r[j].wait_recv()
                cp = local("w", wc_hbm.at[j], wst.at[pl.ds(0, NSLOT)])
                cp.start()
                cp.wait()

            @pl.when(d[j] == 0)
            def _():
                cp = local("w", q_hbm, wst.at[pl.ds(0, NSLOT)])
                cp.start()
                cp.wait()

        def grads(j):
            @pl.loop(0, 16)
            def _(r):
                rows = pl.ds(pl.multiple_of(r * 256, 256), 256)
                g = lax.dot_general(tok_v[:, rows], cb[j], (((0,), (0,)), ((), ())), preferred_element_type=F32)
                g = g.astype(BF16)
                for h in (0, 1):
                    for c in range(COLS):
                        gw[(r * 2 + h) * COLS + c] = g[h * BS:(h + 1) * BS, c * BS:(c + 1) * BS]

        def pick(j):
            for o in range(OWN):
                @pl.loop(0, SLOTS)
                def _(s, o=o):
                    gs[j, o, s] = gw[tabs[j, 2 + o // 4, (o % 4) * 32 + s]]

        def assemble(j):
            @pl.loop(0, ROWS)
            def _(r):
                for c in range(COLS):
                    gw[r * COLS + c] = wst[tabs[j, r // 16, (r % 16) * 8 + c]]

        def forward(j):
            @pl.loop(0, 4)
            def _(m):
                rows = pl.ds(pl.multiple_of(m * 256, 256), 256)
                w = jnp.concatenate(
                    [jnp.concatenate([gw[r * COLS + c] for c in range(COLS)], axis=1) for r in range(ROWS)], axis=0
                )
                o = jnp.dot(tok_v[rows, :], w, preferred_element_type=F32)
                ob[j, rows, :] = o.astype(BF16)

        o_own = [local(f"o{j}", ob.at[j, slot(z, k)], out_hbm.at[:, cols(2 * k + j, z)]) for j in (0, 1)]
        o_sends = []
        for j in (0, 1):
            dst = out_hbm.at[:, cols(2 * k + j, z)]
            row = []
            row.append(remote(f"O3{j}", ob.at[j, slot(zo, 0)], orel.at[0, j], "z+"))
            row.append(remote(f"O4{j}", ob.at[j, slot(zo, 1)], orel.at[1, j], "z-"))
            for i in (0, 1):
                row.append(remote(f"O1{j}{i}", ob.at[j, slot(zp, i)], dst, f"z+{i}", rkey=f"O1r{j}", roff=k, rwidth=2))
                row.append(remote(f"O2{j}{i}", ob.at[j, slot(zm, i)], dst, f"z-{i}", rkey=f"O2r{j}", roff=k, rwidth=2))
            row.append(remote(f"O0{j}", ob.at[j, slot(z, kk)], dst, "p"))
            o_sends.append(row)
        O3r = [remote(f"O3{j}", orel.at[0, j], orel.at[0, j], "z+") for j in (0, 1)]
        O4r = [remote(f"O4{j}", orel.at[1, j], orel.at[1, j], "z-") for j in (0, 1)]
        O5 = [remote(f"O5{j}", orel.at[0, j], out_hbm.at[:, cols(2 * k + j, zm)], "z+0", rkey=f"O5r{j}", roff=k, rwidth=2) for j in (0, 1)]
        O6 = [remote(f"O6{j}", orel.at[1, j], out_hbm.at[:, cols(2 * k + j, zp)], "z-1", rkey=f"O5r{j}", roff=k, rwidth=2) for j in (0, 1)]

        def o_recvs(j):
            src = ob.at[j, slot(z, 0)]
            out = [remote(f"O0{j}", src, out_hbm.at[:, cols(2 * kk + j, z)], "p")]
            for i in (0, 1):
                out.append(remote(f"O1{j}0", src, out_hbm.at[:, cols(2 * i + j, zm)], "z+", rkey=f"O1r{j}", roff=i, rwidth=2))
                out.append(remote(f"O2{j}0", src, out_hbm.at[:, cols(2 * i + j, zp)], "z-", rkey=f"O2r{j}", roff=i, rwidth=2))
                out.append(remote(f"O5{j}", src, out_hbm.at[:, cols(2 * i + j, zo)], "z+", rkey=f"O5r{j}", roff=i, rwidth=2))
            return out

        def add1(dst, src, n):
            @pl.loop(0, n)
            def _(i):
                dst[i] = (dst[i].astype(F32) + src[i].astype(F32)).astype(BF16)

        def add2(dst, a, b, n):
            @pl.loop(0, n)
            def _(i):
                dst[i] = (dst[i].astype(F32) + a[i].astype(F32) + b[i].astype(F32)).astype(BF16)

        def sum3(out, dst, a, b, n):
            @pl.loop(0, n)
            def _(i):
                out[i] = dst[i].astype(F32) + a[i].astype(F32) + b[i].astype(F32)

        lo, hi = pl.ds(0, LO), pl.ds(LO, HI)

        class XStage:
            def __init__(self, name, j, base, first, second):
                self.j, self.base = j, base
                self.first, self.second = first, second
                self.c0 = remote(f"{name}0", gs.at[j, base + xo, lo], first.at[0], "x+")
                self.c1 = remote(f"{name}1", gs.at[j, base + xo, hi], first.at[1, pl.ds(0, HI)], "x-")
                self.c2 = remote(f"{name}2", gs.at[j, base + xp], second.at[0], "x+")
                self.c3 = remote(f"{name}3", gs.at[j, base + xm], second.at[1], "x-")

            def start(self):
                self.c0.start()
                self.c1.start()

            def middle(self):
                self.c0.wait_recv()
                add1(gs.at[self.j, self.base + xp, lo], self.first.at[0], LO)
                self.c2.start()
                self.c1.wait_recv()
                add1(gs.at[self.j, self.base + xm, hi], self.first.at[1], HI)
                self.c3.start()

            def arrive(self):
                self.c2.wait_recv()
                self.c3.wait_recv()

            def sends(self):
                return [self.c0, self.c1, self.c2, self.c3]

        class YStage:
            def __init__(self, name, j, whole, low, high, low_dst, high_dst, second):
                self.j = j
                self.c0 = remote(f"{name}0", low, low_dst, "y+")
                self.c1 = remote(f"{name}1", high, high_dst, "y-")
                self.c2 = remote(f"{name}2", whole, second.at[0], "y+")
                self.c3 = remote(f"{name}3", whole, second.at[1], "y-")
                self.low, self.high, self.low_dst, self.high_dst = low, high, low_dst, high_dst

            def start(self):
                @pl.when(d[self.j] == 2)
                def _():
                    self.c0.start()
                    self.c1.start()

            def middle(self, n_low, n_high):
                @pl.when(d[self.j] == 3)
                def _():
                    self.c0.wait_recv()
                    add1(self.low, self.low_dst, n_low)
                    self.c2.start()

                @pl.when(d[self.j] == 1)
                def _():
                    self.c1.wait_recv()
                    add1(self.high, self.high_dst, n_high)
                    self.c3.start()

            def arrive(self):
                self.c2.wait_recv()
                self.c3.wait_recv()

            def wait_sends(self):
                @pl.when(d[self.j] == 2)
                def _():
                    self.c0.wait_send()
                    self.c1.wait_send()

                @pl.when(d[self.j] == 3)
                def _():
                    self.c2.wait_send()

                @pl.when(d[self.j] == 1)
                def _():
                    self.c3.wait_send()

        AX = [XStage(f"A{j}", j, 0, ra1.at[j], ra2.at[j]) for j in (0, 1)]
        AY = [YStage(f"Y{j}", j, gs.at[j, x], gs.at[j, x, lo], gs.at[j, x, hi], ry1, ry1.at[pl.ds(0, HI)], ry2) for j in (0, 1)]
        gs84 = [gs.at[j, pl.ds(4, 4)] for j in (0, 1)]
        BY = [YStage(f"Z{j}", j, gs84[j], gs.at[j, pl.ds(4, 2)], gs.at[j, pl.ds(6, 2)], rz1, rz1, rz2) for j in (0, 1)]
        BX = [XStage(f"B{j}", j, 4, rb1, rb2) for j in (0, 1)]

        def ax_end(j):
            AX[j].arrive()
            add2(gs.at[j, x], ra2.at[j, 0], ra2.at[j, 1], SLOTS)
            AY[j].start()

        def add_nested(dst, srcs, n):
            for o in range(n):
                if len(srcs) == 1:
                    add1(dst.at[o], srcs[0].at[o], SLOTS)
                else:
                    add2(dst.at[o], srcs[0].at[o], srcs[1].at[o], SLOTS)

        def by_middle(j):
            s = BY[j]

            @pl.when(d[j] == 3)
            def _():
                s.c0.wait_recv()
                add_nested(s.low, [rz1], 2)
                s.c2.start()

            @pl.when(d[j] == 1)
            def _():
                s.c1.wait_recv()
                add_nested(s.high, [rz1], 2)
                s.c3.start()

        def by_end(j):
            @pl.when(d[j] == 0)
            def _():
                BY[j].arrive()
                add_nested(gs84[j], [rz2.at[0], rz2.at[1]], 4)
                BX[j].start()

        def bx_middle(j):
            @pl.when(d[j] == 0)
            def _():
                BX[j].middle()

        g_own = local("g", fin.at[k], wg_hbm)
        G = remote("G", fin.at[kk], wg_hbm, "p")

        def finals(j):
            @pl.when(d[j] == 0)
            def _():
                AY[j].arrive()
                sum3(fin.at[0], gs.at[j, x], ry2.at[0], ry2.at[1], SLOTS)
                BX[j].arrive()
                sum3(fin.at[1], gs.at[j, 4 + x], rb2.at[0], rb2.at[1], SLOTS)
                G.start()
                g_own.start()

        t_own.start()
        for copy in (T0, T1, T2):
            copy.start()
        tab_start()
        w_first()
        for copy in c_own:
            copy.start()
        for copy in c_sends[0]:
            copy.start()
        wst[NSLOT] = jnp.zeros((BS, BS), BF16)
        tab_finish()
        w_second()
        w_third()
        T0r.wait_recv()
        T5.start()
        T3.start()
        T1r.wait_recv()
        T6.start()
        T4.start()
        for copy in c_sends[1]:
            copy.start()
        C3r[0].wait_recv()
        C5[0].start()
        C4r[0].wait_recv()
        C6[0].start()
        T5r.wait_recv()
        T7.start()
        T6r.wait_recv()
        T8.start()
        t_own.wait()
        for copy in (T2r, T3r, T4r, T7r, T8r):
            copy.wait_recv()
        c_own[0].wait()
        for copy in c_recvs(0):
            copy.wait_recv()
        grads(0)
        pick(0)
        AX[0].start()
        BY[0].start()
        C3r[1].wait_recv()
        C5[1].start()
        C4r[1].wait_recv()
        C6[1].start()
        w_fourth()
        c_own[1].wait()
        for copy in c_recvs(1):
            copy.wait_recv()
        grads(1)
        pick(1)
        AX[1].start()
        BY[1].start()
        AX[0].middle()
        by_middle(0)
        w_load(0)
        assemble(0)
        forward(0)
        o_own[0].start()
        for copy in o_sends[0]:
            copy.start()
        AX[1].middle()
        by_middle(1)
        ax_end(0)
        w_load(1)
        assemble(1)
        forward(1)
        o_own[1].start()
        for copy in o_sends[1]:
            copy.start()
        by_end(0)
        by_end(1)
        ax_end(1)
        AY[0].middle(LO, HI)
        AY[1].middle(LO, HI)
        O3r[0].wait_recv()
        O5[0].start()
        O4r[0].wait_recv()
        O6[0].start()
        bx_middle(0)
        bx_middle(1)
        O3r[1].wait_recv()
        O5[1].start()
        O4r[1].wait_recv()
        O6[1].start()
        finals(0)
        finals(1)

        for j in (0, 1):
            for copy in o_recvs(j):
                copy.wait_recv()
            o_own[j].wait()

        own_final = (y // 2) == k

        @pl.when(own_final)
        def _():
            g_own.wait()
            G.wait_send()

        @pl.when(jnp.logical_not(own_final))
        def _():
            G.wait_recv()

        for copy in (T0, T1, T2, T3, T4, T5, T6, T7, T8):
            copy.wait_send()
        for j in (0, 1):
            for copy in c_sends[j] + [C5[j], C6[j]] + o_sends[j] + [O5[j], O6[j]] + AX[j].sends():
                copy.wait_send()
            AY[j].wait_sends()
            BY[j].wait_sends()

            @pl.when(d[j] == 0)
            def _(j=j):
                for copy in [W0[j], W1[j]] + V[j] + BX[j].sends():
                    copy.wait_send()

            @pl.when(d[j] == 1)
            def _(j=j):
                W2[j].wait_send()

            @pl.when(d[j] == 3)
            def _(j=j):
                W3[j].wait_send()

            @pl.when(d[j] != 0)
            def _(j=j):
                for copy in (W4[j], W5[j], W6[j], W7[j]):
                    copy.wait_send()

    return kernel


def tables(slot_ids):
    numbers = jnp.arange(ROWS * 8, dtype=jnp.int32)
    block = jnp.where(numbers % 8 < COLS, (numbers // 8) * COLS + numbers % 8, -1)
    match = (slot_ids[:, None] == block[None, :]).astype(jnp.int32)
    index = jnp.sum(match * (jnp.arange(NSLOT, dtype=jnp.int32)[:, None] - NSLOT), axis=0) + NSLOT
    pad = ((0, 0), (0, 32 - SLOTS))
    ids = slot_ids.reshape(OWN, SLOTS)
    ids = jnp.pad(ids, pad).reshape(2, 128)
    return jnp.concatenate([index.reshape(2, 128), ids, jnp.zeros((4, 128), jnp.int32)], axis=0)


def shards(tokens, cotangent, master, block_ids, live_count):
    owners, slots = block_ids.shape
    live_mask = (jnp.arange(slots, dtype=jnp.int32)[None, :] < live_count).astype(jnp.float32)
    quantized = fake_quant(master, live_mask).reshape(owners * slots, BS, BS)
    table = tables(block_ids.reshape(owners * slots))
    vmem = pltpu.VMEM
    blk = (BS, BS)
    anyspec = pl.BlockSpec(memory_space=pl.ANY)
    outputs, w_grad, _ = pl.pallas_call(
        make_kernel(Names(), Names(), Names()),
        out_shape=(
            jax.ShapeDtypeStruct(cotangent.shape, BF16),
            jax.ShapeDtypeStruct((slots,) + blk, F32),
            jax.ShapeDtypeStruct((2, NSLOT) + blk, BF16),
        ),
        in_specs=[anyspec] * 4,
        out_specs=(anyspec,) * 3,
        scratch_shapes=[
            vmem((8 * TOK, ROWS * BS), BF16),
            vmem((2, 8 * TOK, WID), BF16),
            vmem((2, 2, TOK, WID), BF16),
            vmem((ROWS * COLS,) + blk, BF16),
            vmem((NSLOT + 1,) + blk, BF16),
            vmem((2, 8 * TOK, WID), BF16),
            vmem((2, 2, TOK, WID), BF16),
            vmem((2, OWN, SLOTS) + blk, BF16),
            vmem((2, 2, LO) + blk, BF16),
            vmem((2, 2, SLOTS) + blk, BF16),
            vmem((LO,) + blk, BF16),
            vmem((2, SLOTS) + blk, BF16),
            vmem((2, SLOTS) + blk, BF16),
            vmem((2, 4, SLOTS) + blk, BF16),
            vmem((2, LO) + blk, BF16),
            vmem((2, SLOTS) + blk, BF16),
            vmem((2, SLOTS) + blk, F32),
            vmem((2, 8, 128), jnp.int32),
            pltpu.SMEM((2, 8, 128), jnp.int32),
            pltpu.SemaphoreType.DMA((112,)),
            pltpu.SemaphoreType.DMA((112,)),
            pltpu.SemaphoreType.DMA((16,)),
        ],
        compiler_params=pltpu.CompilerParams(
            collective_id=0, has_side_effects=True, vmem_limit_bytes=66 * 1024 * 1000
        ),
    )(tokens, cotangent, quantized, table)
    owner = lax.axis_index("dp") * lax.axis_size("seq") + lax.axis_index("seq")
    count = lax.dynamic_slice(live_count, (owner, 0), (1, 1))
    mine = jnp.arange(slots, dtype=jnp.int32)[None, :, None, None] < count[:, :, None, None]
    return (outputs, jnp.where(mine, w_grad[None], 0.0))


def solution(mesh):
    return jax.shard_map(
        shards,
        mesh=mesh,
        in_specs=(
            P(("dp", "seq", "tensor"), None),
            P(("dp", "seq", "tensor"), None),
            P(None, "tensor", None, None),
            P(None, "tensor"),
            P(None, "tensor"),
        ),
        out_specs=(P(("dp", "seq", "tensor"), None), P(("dp", "seq"), "tensor", None, None)),
        check_vma=False,
    )
```

```python
import functools

import jax
import jax.numpy as jnp
from jax import lax
from jax.experimental import pallas as pl
from jax.experimental.pallas import tpu as pltpu
from jax.sharding import PartitionSpec as P

BS = 128
ROWS = 32
COLS = 7
OWN = 8
SLOTS = 21
NSLOT = OWN * SLOTS
QTR = 28
HALF = QTR // 2
YLO = 4 * QTR
YN = NSLOT - YLO
YH = YN // 2
LO, HI = 11, 10
WID = COLS * BS
TOK = 128
MESH = pl.DeviceIdType.MESH
F32 = jnp.float32
BF16 = jnp.bfloat16


class Names:
    def __init__(self):
        self.n = 0
        self.at = {}

    def get(self, key, width=1):
        if key not in self.at:
            self.at[key] = self.n
            self.n += width
        return self.at[key]


def make_kernel(names_s, names_r, names_l):
    def kernel(
        tok_hbm, cot_hbm, q_hbm, tab_hbm,
        out_hbm, wg_hbm, wc_hbm,
        tok_v, cb, crel, gw, wst, ob, orel, gs, ra1, ra2, ry1, ry2, rz1, rz2, rb1, rb2, fin,
        tabv, tabs, ssem, rsem, lsem,
    ):
        k = lax.axis_index("dp")
        x = lax.axis_index("seq")
        t_me = lax.axis_index("tensor")
        y, z = t_me // 4, t_me % 4
        xp, xm, xo = (x + 1) % 4, (x + 3) % 4, (x + 2) % 4
        yp, ym, yo = (y + 1) % 4, (y + 3) % 4, (y + 2) % 4
        zp, zm, zo = (z + 1) % 4, (z + 3) % 4, (z + 2) % 4
        kk = 1 - k

        def dev(k_=None, x_=None, y_=None, z_=None):
            kd = k if k_ is None else k_
            xd = x if x_ is None else x_
            yd = y if y_ is None else y_
            zd = z if z_ is None else z_
            return (kd, xd, yd * 4 + zd)

        partner = dev(k_=kk)
        devs = {
            "x+": dev(x_=xp), "x-": dev(x_=xm), "y+": dev(y_=yp), "y-": dev(y_=ym), "y2": dev(y_=yo),
            "z+": dev(z_=zp), "z-": dev(z_=zm), "p": partner,
            "z+0": dev(k_=0, z_=zp), "z+1": dev(k_=1, z_=zp), "z-0": dev(k_=0, z_=zm), "z-1": dev(k_=1, z_=zm),
        }

        def remote(key, src, dst, to, skey=None, rkey=None, roff=None, rwidth=1):
            si = names_s.get(skey or key)
            ri = names_r.get(rkey or key, rwidth)
            if roff is not None:
                ri = ri + roff
            return pltpu.make_async_remote_copy(
                src_ref=src, dst_ref=dst, send_sem=ssem.at[si], recv_sem=rsem.at[ri],
                device_id=devs[to], device_id_type=MESH,
            )

        def local(key, src, dst):
            return pltpu.make_async_copy(src, dst, lsem.at[names_l.get(key)])

        def slot(z_, k_):
            return pl.ds(pl.multiple_of((z_ * 2 + k_) * TOK, TOK), TOK)

        def part(z_, k_, lo):
            return pl.ds(pl.multiple_of((z_ * 2 + k_) * TOK + lo, 64), 64)

        def cols(group_y, group_z):
            return pl.ds(pl.multiple_of((group_y * 4 + group_z) * WID, 128), WID)

        peers = [partner, devs["x+"], devs["x-"], devs["y+"], devs["y-"], devs["y2"],
                 devs["z+0"], devs["z+1"], devs["z-0"], devs["z-1"]]
        barrier = pltpu.get_barrier_semaphore()
        for peer in peers:
            pl.semaphore_signal(barrier, inc=1, device_id=peer, device_id_type=MESH)
        pl.semaphore_wait(barrier, len(peers))

        d = [(y + 4 - (2 * k + j)) % 4 for j in (0, 1)]
        tok2 = tok_hbm

        t_own = local("t", tok2, tok_v.at[slot(z, k)])
        T0 = remote("T0", tok2, tok_v.at[slot(z, k)], "z+")
        T1 = remote("T1", tok2, tok_v.at[slot(z, k)], "z-")
        T2 = remote("T2", tok2, tok_v.at[slot(z, k)], "p")
        T0r = remote("T0", tok2, tok_v.at[slot(zm, k)], "z+")
        T1r = remote("T1", tok2, tok_v.at[slot(zp, k)], "z-")
        T2r = remote("T2", tok2, tok_v.at[slot(z, kk)], "p")
        T3 = remote("T3", tok_v.at[slot(zm, k)], tok_v.at[slot(zm, k)], "p")
        T4 = remote("T4", tok_v.at[slot(zp, k)], tok_v.at[slot(zp, k)], "p")
        T3r = remote("T3", tok_v.at[slot(zm, kk)], tok_v.at[slot(zm, kk)], "p")
        T4r = remote("T4", tok_v.at[slot(zp, kk)], tok_v.at[slot(zp, kk)], "p")
        T5 = remote("T5", tok_v.at[part(zm, k, 0)], tok_v.at[part(zm, k, 0)], "z+")
        T6 = remote("T6", tok_v.at[part(zp, k, 64)], tok_v.at[part(zp, k, 64)], "z-")
        T5r = remote("T5", tok_v.at[part(zo, k, 0)], tok_v.at[part(zo, k, 0)], "z+")
        T6r = remote("T6", tok_v.at[part(zo, k, 64)], tok_v.at[part(zo, k, 64)], "z-")
        T7 = remote("T7", tok_v.at[part(zo, k, 0)], tok_v.at[part(zo, k, 0)], "p")
        T8 = remote("T8", tok_v.at[part(zo, k, 64)], tok_v.at[part(zo, k, 64)], "p")
        T7r = remote("T7", tok_v.at[part(zo, kk, 0)], tok_v.at[part(zo, kk, 0)], "p")
        T8r = remote("T8", tok_v.at[part(zo, kk, 64)], tok_v.at[part(zo, kk, 64)], "p")

        def cot(group_y, group_z):
            return cot_hbm.at[:, cols(group_y, group_z)]

        c_own = [local(f"c{j}", cot(2 * k + j, z), cb.at[j, slot(z, k)]) for j in (0, 1)]
        c_sends = []
        for j in (0, 1):
            row = []
            row.append(remote(f"C3{j}", cot(j, zo), crel.at[0, j], "z+"))
            row.append(remote(f"C4{j}", cot(2 + j, zo), crel.at[1, j], "z-"))
            for k_ in (0, 1):
                row.append(remote(f"C1{j}{k_}", cot(2 * k_ + j, zp), cb.at[j, slot(z, k)], f"z+{k_}",
                                  rkey=f"C1r{j}", roff=k, rwidth=2))
                row.append(remote(f"C2{j}{k_}", cot(2 * k_ + j, zm), cb.at[j, slot(z, k)], f"z-{k_}",
                                  rkey=f"C2r{j}", roff=k, rwidth=2))
            row.append(remote(f"C0{j}", cot(2 * kk + j, z), cb.at[j, slot(z, k)], "p"))
            c_sends.append(row)
        C3r = [remote(f"C3{j}", cot(j, zo), crel.at[0, j], "z+") for j in (0, 1)]
        C4r = [remote(f"C4{j}", cot(2 + j, zo), crel.at[1, j], "z-") for j in (0, 1)]
        C5 = [remote(f"C5{j}", crel.at[0, j], cb.at[j, slot(zm, k)], "z+0", rkey=f"C5r{j}", roff=k, rwidth=2) for j in (0, 1)]
        C6 = [remote(f"C6{j}", crel.at[1, j], cb.at[j, slot(zp, k)], "z-1", rkey=f"C5r{j}", roff=k, rwidth=2) for j in (0, 1)]

        def c_recvs(j):
            out = [remote(f"C0{j}", cot(j, z), cb.at[j, slot(z, kk)], "p")]
            for i in (0, 1):
                out.append(remote(f"C1{j}0", cot(j, z), cb.at[j, slot(zm, i)], "z+", rkey=f"C1r{j}", roff=i, rwidth=2))
                out.append(remote(f"C2{j}0", cot(j, z), cb.at[j, slot(zp, i)], "z-", rkey=f"C2r{j}", roff=i, rwidth=2))
                out.append(remote(f"C5{j}", cot(j, z), cb.at[j, slot(zo, i)], "z+", rkey=f"C5r{j}", roff=i, rwidth=2))
            return out

        def wq(j, q):
            return wc_hbm.at[j, pl.ds(q * QTR, QTR)]

        def wlo(j, q):
            return wc_hbm.at[j, pl.ds(q * QTR, HALF)]

        def whi(j, q):
            return wc_hbm.at[j, pl.ds(q * QTR + HALF, HALF)]

        def wu(j, lo=0, n=YN):
            return wc_hbm.at[j, pl.ds(YLO + lo, n)]

        JS = (0, 1)
        W0 = [remote(f"W0{j}", wq(j, x), wq(j, x), "y+") for j in JS]
        W1 = [remote(f"W1{j}", wq(j, x), wq(j, x), "y-") for j in JS]
        W2 = [remote(f"W2{j}", wlo(j, x), wlo(j, x), "y+") for j in JS]
        W3 = [remote(f"W3{j}", whi(j, x), whi(j, x), "y-") for j in JS]
        W4 = [remote(f"W4{j}", wq(j, x), wq(j, x), "x+") for j in JS]
        W5 = [remote(f"W5{j}", wq(j, x), wq(j, x), "x-") for j in JS]
        W4r = [remote(f"W4{j}", wq(j, xm), wq(j, xm), "x+") for j in JS]
        W5r = [remote(f"W5{j}", wq(j, xp), wq(j, xp), "x-") for j in JS]
        W6 = [remote(f"W6{j}", wlo(j, xm), wlo(j, xm), "x+") for j in JS]
        W7 = [remote(f"W7{j}", whi(j, xp), whi(j, xp), "x-") for j in JS]
        W6r = [remote(f"W6{j}", wlo(j, xo), wlo(j, xo), "x+") for j in JS]
        W7r = [remote(f"W7{j}", whi(j, xo), whi(j, xo), "x-") for j in JS]
        U0 = [remote(f"WU0{j}", wu(j), wu(j), "y+") for j in JS]
        U1 = [remote(f"WU1{j}", wu(j), wu(j), "y-") for j in JS]
        U2 = [remote(f"WU2{j}", wu(j, 0, YH), wu(j, 0, YH), "y+") for j in JS]
        U3 = [remote(f"WU3{j}", wu(j, YH, YH), wu(j, YH, YH), "y-") for j in JS]
        V = [[remote(f"V{j}{i}", tab_hbm, tabv.at[j], to) for i, to in enumerate(("y+", "y-", "y2"))] for j in (0, 1)]

        def tab_start():
            for j in (0, 1):
                @pl.when(d[j] == 0)
                def _(j=j):
                    for copy in V[j]:
                        copy.start()
                    local(f"v{j}", tab_hbm, tabv.at[j]).start()

        def tab_finish():
            for j in (0, 1):
                @pl.when(d[j] == 0)
                def _(j=j):
                    local(f"v{j}", tab_hbm, tabv.at[j]).wait()

                for i, dist in enumerate((1, 3, 2)):
                    @pl.when(d[j] == dist)
                    def _(j=j, i=i):
                        V[j][i].wait_recv()
            cp = local("tab", tabv, tabs)
            cp.start()
            cp.wait()

        def quantize(j, start, n):
            @pl.loop(0, n // 4)
            def _(i):
                rows = pl.ds(start + i * 4, 4)
                wide = wst[rows].astype(F32)
                peak = jnp.max(jnp.abs(wide), axis=(1, 2), keepdims=True) + 1e-06
                levels = jnp.floor(wide * (7.0 / peak) + 0.5)
                wst[rows] = (levels * (peak / 7.0)).astype(BF16)

            cp = local("qw", wst.at[pl.ds(start, n)], wc_hbm.at[j, pl.ds(start, n)])
            cp.start()
            cp.wait()

        def w_first():
            for j in (0, 1):
                @pl.when(d[j] == 0)
                def _(j=j):
                    cp = local("q", q_hbm, wst.at[pl.ds(0, NSLOT)])
                    cp.start()
                    cp.wait()
                    quantize(j, x * QTR, QTR)
                    W0[j].start()
                    W1[j].start()
                    quantize(j, YLO, YN)
                    U0[j].start()
                    U1[j].start()
                    for q in (xp, xo, xm):
                        quantize(j, q * QTR, QTR)

        def w_second():
            for j in (0, 1):
                @pl.when(d[j] == 1)
                def _(j=j):
                    W0[j].wait_recv()
                    W2[j].start()
                    W4[j].start()
                    W5[j].start()

                @pl.when(d[j] == 3)
                def _(j=j):
                    W1[j].wait_recv()
                    W3[j].start()
                    W4[j].start()
                    W5[j].start()

        def w_third():
            for j in (0, 1):
                @pl.when(d[j] == 2)
                def _(j=j):
                    W2[j].wait_recv()
                    W3[j].wait_recv()
                    W4[j].start()
                    W5[j].start()

        def w_relay():
            for j in (0, 1):
                @pl.when(d[j] == 1)
                def _(j=j):
                    U0[j].wait_recv()
                    U2[j].start()

                @pl.when(d[j] == 3)
                def _(j=j):
                    U1[j].wait_recv()
                    U3[j].start()

        def w_fourth():
            for j in (0, 1):
                @pl.when(d[j] != 0)
                def _(j=j):
                    W4r[j].wait_recv()
                    W6[j].start()
                    W5r[j].wait_recv()
                    W7[j].start()

        def w_load(j):
            @pl.when(d[j] != 0)
            def _():
                W6r[j].wait_recv()
                W7r[j].wait_recv()

            @pl.when(d[j] == 2)
            def _():
                U2[j].wait_recv()
                U3[j].wait_recv()

            cp = local("w", wc_hbm.at[j], wst.at[pl.ds(0, NSLOT)])
            cp.start()
            cp.wait()

        def grads(j):
            @pl.loop(0, 16)
            def _(r):
                rows = pl.ds(pl.multiple_of(r * 256, 256), 256)
                g = lax.dot_general(tok_v[:, rows], cb[j], (((0,), (0,)), ((), ())), preferred_element_type=F32)
                g = g.astype(BF16)
                for h in (0, 1):
                    for c in range(COLS):
                        gw[(r * 2 + h) * COLS + c] = g[h * BS:(h + 1) * BS, c * BS:(c + 1) * BS]

        def pick(j):
            for o in range(OWN):
                @pl.loop(0, SLOTS)
                def _(s, o=o):
                    gs[j, o, s] = gw[tabs[j, 2 + o // 4, (o % 4) * 32 + s]]

        def assemble(j):
            @pl.loop(0, ROWS)
            def _(r):
                for c in range(COLS):
                    gw[r * COLS + c] = wst[tabs[j, r // 16, (r % 16) * 8 + c]]

        def forward(j, hooks):
            @pl.loop(0, 4)
            def _(m):
                zz = (z + jnp.where(m == 0, 2, jnp.where(m == 1, 1, jnp.where(m == 2, 3, 0)))) % 4
                rows = pl.ds(pl.multiple_of(zz * 256, 256), 256)
                w = jnp.concatenate(
                    [jnp.concatenate([gw[r * COLS + c] for c in range(COLS)], axis=1) for r in range(ROWS)], axis=0
                )
                o = jnp.dot(tok_v[rows, :], w, preferred_element_type=F32)
                ob[j, rows, :] = o.astype(BF16)
                for at, steps in hooks.items():
                    @pl.when(m == at)
                    def _(steps=steps):
                        for step in steps:
                            step()

        o_own = [local(f"o{j}", ob.at[j, slot(z, k)], out_hbm.at[:, cols(2 * k + j, z)]) for j in (0, 1)]
        o_sends = []
        for j in (0, 1):
            dst = out_hbm.at[:, cols(2 * k + j, z)]
            row = []
            row.append(remote(f"O3{j}", ob.at[j, slot(zo, 0)], orel.at[0, j], "z+"))
            row.append(remote(f"O4{j}", ob.at[j, slot(zo, 1)], orel.at[1, j], "z-"))
            for i in (0, 1):
                row.append(remote(f"O1{j}{i}", ob.at[j, slot(zp, i)], dst, f"z+{i}", rkey=f"O1r{j}", roff=k, rwidth=2))
            for i in (0, 1):
                row.append(remote(f"O2{j}{i}", ob.at[j, slot(zm, i)], dst, f"z-{i}", rkey=f"O2r{j}", roff=k, rwidth=2))
            row.append(remote(f"O0{j}", ob.at[j, slot(z, kk)], dst, "p"))
            o_sends.append(row)
        O3r = [remote(f"O3{j}", orel.at[0, j], orel.at[0, j], "z+") for j in (0, 1)]
        O4r = [remote(f"O4{j}", orel.at[1, j], orel.at[1, j], "z-") for j in (0, 1)]
        O5 = [remote(f"O5{j}", orel.at[0, j], out_hbm.at[:, cols(2 * k + j, zm)], "z+0", rkey=f"O5r{j}", roff=k, rwidth=2) for j in (0, 1)]
        O6 = [remote(f"O6{j}", orel.at[1, j], out_hbm.at[:, cols(2 * k + j, zp)], "z-1", rkey=f"O5r{j}", roff=k, rwidth=2) for j in (0, 1)]

        def o_recvs(j):
            src = ob.at[j, slot(z, 0)]
            out = [remote(f"O0{j}", src, out_hbm.at[:, cols(2 * kk + j, z)], "p")]
            for i in (0, 1):
                out.append(remote(f"O1{j}0", src, out_hbm.at[:, cols(2 * i + j, zm)], "z+", rkey=f"O1r{j}", roff=i, rwidth=2))
                out.append(remote(f"O2{j}0", src, out_hbm.at[:, cols(2 * i + j, zp)], "z-", rkey=f"O2r{j}", roff=i, rwidth=2))
                out.append(remote(f"O5{j}", src, out_hbm.at[:, cols(2 * i + j, zo)], "z+", rkey=f"O5r{j}", roff=i, rwidth=2))
            return out

        def add1(dst, src, n):
            @pl.loop(0, n)
            def _(i):
                dst[i] = (dst[i].astype(F32) + src[i].astype(F32)).astype(BF16)

        def add2(dst, a, b, n):
            @pl.loop(0, n)
            def _(i):
                dst[i] = (dst[i].astype(F32) + a[i].astype(F32) + b[i].astype(F32)).astype(BF16)

        def sum3(out, dst, a, b, n):
            @pl.loop(0, n)
            def _(i):
                out[i] = dst[i].astype(F32) + a[i].astype(F32) + b[i].astype(F32)

        lo, hi = pl.ds(0, LO), pl.ds(LO, HI)

        class XStage:
            def __init__(self, name, j, base, first, second):
                self.j, self.base = j, base
                self.first = first
                self.c0 = remote(f"{name}0", gs.at[j, base + xo, lo], first.at[0], "x+")
                self.c1 = remote(f"{name}1", gs.at[j, base + xo, hi], first.at[1, pl.ds(0, HI)], "x-")
                self.c2l = remote(f"{name}2l", gs.at[j, base + xp, lo], second.at[0, lo], "x+")
                self.c2h = remote(f"{name}2h", gs.at[j, base + xp, hi], second.at[0, hi], "x+")
                self.c3l = remote(f"{name}3l", gs.at[j, base + xm, lo], second.at[1, lo], "x-")
                self.c3h = remote(f"{name}3h", gs.at[j, base + xm, hi], second.at[1, hi], "x-")

            def start(self):
                for copy in (self.c0, self.c1, self.c2h, self.c3l):
                    copy.start()

            def middle(self):
                self.c0.wait_recv()
                add1(gs.at[self.j, self.base + xp, lo], self.first.at[0], LO)
                self.c2l.start()
                self.c1.wait_recv()
                add1(gs.at[self.j, self.base + xm, hi], self.first.at[1], HI)
                self.c3h.start()

            def arrive(self):
                for copy in (self.c2h, self.c3l, self.c2l, self.c3h):
                    copy.wait_recv()

            def sends(self):
                return [self.c0, self.c1, self.c2l, self.c2h, self.c3l, self.c3h]

        class YStage:
            def __init__(self, name, j, src, low, high, relay, high_relay, second, add):
                self.j, self.add, self.relay = j, add, relay
                self.low, self.high = src.at[low], src.at[high]
                self.c0 = remote(f"{name}0", self.low, relay, "y+")
                self.c1 = remote(f"{name}1", self.high, high_relay, "y-")
                self.c2l = remote(f"{name}2l", self.low, second.at[0].at[low], "y+")
                self.c2h = remote(f"{name}2h", self.high, second.at[0].at[high], "y+")
                self.c3l = remote(f"{name}3l", self.low, second.at[1].at[low], "y-")
                self.c3h = remote(f"{name}3h", self.high, second.at[1].at[high], "y-")

            def start(self):
                @pl.when(d[self.j] == 2)
                def _():
                    self.c0.start()
                    self.c1.start()

                @pl.when(d[self.j] == 3)
                def _():
                    self.c2h.start()

                @pl.when(d[self.j] == 1)
                def _():
                    self.c3l.start()

            def middle(self):
                @pl.when(d[self.j] == 3)
                def _():
                    self.c0.wait_recv()
                    self.add(self.low, self.relay, 0)
                    self.c2l.start()

                @pl.when(d[self.j] == 1)
                def _():
                    self.c1.wait_recv()
                    self.add(self.high, self.relay, 1)
                    self.c3h.start()

            def arrive(self):
                for copy in (self.c2h, self.c3l, self.c2l, self.c3h):
                    copy.wait_recv()

            def wait_sends(self):
                @pl.when(d[self.j] == 2)
                def _():
                    self.c0.wait_send()
                    self.c1.wait_send()

                @pl.when(d[self.j] == 3)
                def _():
                    self.c2h.wait_send()
                    self.c2l.wait_send()

                @pl.when(d[self.j] == 1)
                def _():
                    self.c3l.wait_send()
                    self.c3h.wait_send()

        AX = [XStage(f"A{j}", j, 0, ra1.at[j], ra2.at[j]) for j in (0, 1)]
        def add_ay(dst, src, half):
            add1(dst, src, (LO, HI)[half])

        def add_by(dst, src, half):
            for o in (0, 1):
                add1(dst.at[o], src.at[o], SLOTS)

        AY = [YStage(f"Y{j}", j, gs.at[j, x], lo, hi, ry1, ry1.at[pl.ds(0, HI)], ry2, add_ay) for j in (0, 1)]
        gs84 = [gs.at[j, pl.ds(4, 4)] for j in (0, 1)]
        BY = [YStage(f"Z{j}", j, gs84[j], pl.ds(0, 2), pl.ds(2, 2), rz1, rz1, rz2, add_by) for j in (0, 1)]
        BX = [XStage(f"B{j}", j, 4, rb1, rb2) for j in (0, 1)]

        def ax_end(j):
            AX[j].arrive()
            add2(gs.at[j, x], ra2.at[j, 0], ra2.at[j, 1], SLOTS)
            AY[j].start()

        def by_end(j):
            @pl.when(d[j] == 0)
            def _():
                BY[j].arrive()
                for o in range(4):
                    add2(gs84[j].at[o], rz2.at[0, o], rz2.at[1, o], SLOTS)
                BX[j].start()

        def bx_middle(j):
            @pl.when(d[j] == 0)
            def _():
                BX[j].middle()

        g_own = local("g", fin.at[k], wg_hbm)
        G = remote("G", fin.at[kk], wg_hbm, "p")

        def finals(j):
            @pl.when(d[j] == 0)
            def _():
                AY[j].arrive()
                sum3(fin.at[0], gs.at[j, x], ry2.at[0], ry2.at[1], SLOTS)
                BX[j].arrive()
                sum3(fin.at[1], gs.at[j, 4 + x], rb2.at[0], rb2.at[1], SLOTS)
                G.start()
                g_own.start()

        def o_start(j, *which):
            def go():
                for i in which:
                    if i < 0:
                        o_own[j].start()
                    else:
                        o_sends[j][i].start()
            return go

        def o_hooks(j):
            return {0: [o_start(j, 0, 1)], 1: [o_start(j, 2, 3)], 2: [o_start(j, 4, 5)], 3: [o_start(j, 6, -1)]}

        def o_relay(j):
            O3r[j].wait_recv()
            O5[j].start()
            O4r[j].wait_recv()
            O6[j].start()

        def c_relay(j):
            C3r[j].wait_recv()
            C5[j].start()
            C4r[j].wait_recv()
            C6[j].start()

        def reduce_start(j):
            AX[j].start()
            BY[j].start()

        t_own.start()
        for copy in (T0, T1, T2):
            copy.start()
        tab_start()
        for copy in c_sends[0] + c_own:
            copy.start()
        w_first()
        wst[NSLOT] = jnp.zeros((BS, BS), BF16)
        tab_finish()
        w_second()
        w_third()
        T0r.wait_recv()
        T5.start()
        T3.start()
        T1r.wait_recv()
        T6.start()
        T4.start()
        c_relay(0)
        for copy in c_sends[1]:
            copy.start()
        w_relay()
        w_fourth()
        T5r.wait_recv()
        T7.start()
        T6r.wait_recv()
        T8.start()
        t_own.wait()
        for copy in (T2r, T3r, T4r, T7r, T8r):
            copy.wait_recv()
        c_own[0].wait()
        for copy in c_recvs(0):
            copy.wait_recv()
        grads(0)
        pick(0)
        reduce_start(0)
        c_relay(1)
        w_load(0)
        assemble(0)
        hooks = o_hooks(0)
        hooks[2] += [AX[0].middle, BY[0].middle]
        forward(0, hooks)
        o_relay(0)
        c_own[1].wait()
        for copy in c_recvs(1):
            copy.wait_recv()
        grads(1)
        pick(1)
        reduce_start(1)
        ax_end(0)
        w_load(1)
        assemble(1)
        hooks = o_hooks(1)
        hooks[1] += [lambda: by_end(0)]
        hooks[2] += [AX[1].middle, BY[1].middle, AY[0].middle]
        forward(1, hooks)
        bx_middle(0)
        ax_end(1)
        o_relay(1)
        by_end(1)
        AY[1].middle()
        finals(0)
        bx_middle(1)
        finals(1)

        for j in (0, 1):
            for copy in o_recvs(j):
                copy.wait_recv()
            o_own[j].wait()

        own_final = (y // 2) == k

        @pl.when(own_final)
        def _():
            g_own.wait()
            G.wait_send()

        @pl.when(jnp.logical_not(own_final))
        def _():
            G.wait_recv()

        for copy in (T0, T1, T2, T3, T4, T5, T6, T7, T8):
            copy.wait_send()
        for j in (0, 1):
            for copy in c_sends[j] + [C5[j], C6[j]] + o_sends[j] + [O5[j], O6[j]] + AX[j].sends():
                copy.wait_send()
            AY[j].wait_sends()
            BY[j].wait_sends()

            @pl.when(d[j] == 0)
            def _(j=j):
                for copy in [W0[j], W1[j], U0[j], U1[j]] + V[j] + BX[j].sends():
                    copy.wait_send()

            @pl.when(d[j] == 1)
            def _(j=j):
                W2[j].wait_send()
                U2[j].wait_send()

            @pl.when(d[j] == 3)
            def _(j=j):
                W3[j].wait_send()
                U3[j].wait_send()

            @pl.when(d[j] != 0)
            def _(j=j):
                for copy in (W4[j], W5[j], W6[j], W7[j]):
                    copy.wait_send()

    return kernel


def tables(slot_ids, live):
    numbers = jnp.arange(ROWS * 8, dtype=jnp.int32)
    block = jnp.where(numbers % 8 < COLS, (numbers // 8) * COLS + numbers % 8, -1)
    match = ((slot_ids[:, None] == block[None, :]) & live[:, None]).astype(jnp.int32)
    index = jnp.sum(match * (jnp.arange(NSLOT, dtype=jnp.int32)[:, None] - NSLOT), axis=0) + NSLOT
    pad = ((0, 0), (0, 32 - SLOTS))
    ids = slot_ids.reshape(OWN, SLOTS)
    ids = jnp.pad(ids, pad).reshape(2, 128)
    return jnp.concatenate([index.reshape(2, 128), ids, jnp.zeros((4, 128), jnp.int32)], axis=0)


def shards(tokens, cotangent, master, block_ids, live_count):
    owners, slots = block_ids.shape
    live = jnp.arange(slots, dtype=jnp.int32)[None, :] < live_count
    table = tables(block_ids.reshape(owners * slots), live.reshape(owners * slots))
    vmem = pltpu.VMEM
    blk = (BS, BS)
    anyspec = pl.BlockSpec(memory_space=pl.ANY)
    outputs, w_grad, _ = pl.pallas_call(
        make_kernel(Names(), Names(), Names()),
        out_shape=(
            jax.ShapeDtypeStruct(cotangent.shape, BF16),
            jax.ShapeDtypeStruct((slots,) + blk, F32),
            jax.ShapeDtypeStruct((2, NSLOT) + blk, BF16),
        ),
        in_specs=[anyspec] * 4,
        out_specs=(anyspec,) * 3,
        scratch_shapes=[
            vmem((8 * TOK, ROWS * BS), BF16),
            vmem((2, 8 * TOK, WID), BF16),
            vmem((2, 2, TOK, WID), BF16),
            vmem((ROWS * COLS,) + blk, BF16),
            vmem((NSLOT + 1,) + blk, BF16),
            vmem((2, 8 * TOK, WID), BF16),
            vmem((2, 2, TOK, WID), BF16),
            vmem((2, OWN, SLOTS) + blk, BF16),
            vmem((2, 2, LO) + blk, BF16),
            vmem((2, 2, SLOTS) + blk, BF16),
            vmem((LO,) + blk, BF16),
            vmem((2, SLOTS) + blk, BF16),
            vmem((2, SLOTS) + blk, BF16),
            vmem((2, 4, SLOTS) + blk, BF16),
            vmem((2, LO) + blk, BF16),
            vmem((2, SLOTS) + blk, BF16),
            vmem((2, SLOTS) + blk, F32),
            vmem((2, 8, 128), jnp.int32),
            pltpu.SMEM((2, 8, 128), jnp.int32),
            pltpu.SemaphoreType.DMA((144,)),
            pltpu.SemaphoreType.DMA((144,)),
            pltpu.SemaphoreType.DMA((16,)),
        ],
        compiler_params=pltpu.CompilerParams(
            collective_id=0, has_side_effects=True, vmem_limit_bytes=66 * 1024 * 1000
        ),
    )(tokens, cotangent, master.reshape(owners * slots, BS, BS), table)
    owner = lax.axis_index("dp") * lax.axis_size("seq") + lax.axis_index("seq")
    count = lax.dynamic_slice(live_count, (owner, 0), (1, 1))
    mine = jnp.arange(slots, dtype=jnp.int32)[None, :, None, None] < count[:, :, None, None]
    return (outputs, jnp.where(mine, w_grad[None], 0.0))


def solution(mesh):
    return jax.shard_map(
        shards,
        mesh=mesh,
        in_specs=(
            P(("dp", "seq", "tensor"), None),
            P(("dp", "seq", "tensor"), None),
            P(None, "tensor", None, None),
            P(None, "tensor"),
            P(None, "tensor"),
        ),
        out_specs=(P(("dp", "seq", "tensor"), None), P(("dp", "seq"), "tensor", None, None)),
        check_vma=False,
    )
```

```python
import functools

import jax
import jax.numpy as jnp
from jax import lax
from jax.experimental import pallas as pl
from jax.experimental.pallas import tpu as pltpu
from jax.sharding import PartitionSpec as P

BS = 128
ROWS = 32
COLS = 7
OWN = 8
SLOTS = 21
NSLOT = OWN * SLOTS
QTR = 28
HALF = QTR // 2
YLO = 4 * QTR
YN = NSLOT - YLO
YH = YN // 2
LO, HI = 11, 10
WID = COLS * BS
TOK = 128
MESH = pl.DeviceIdType.MESH
F32 = jnp.float32
BF16 = jnp.bfloat16


class Names:
    def __init__(self):
        self.n = 0
        self.at = {}

    def get(self, key, width=1):
        if key not in self.at:
            self.at[key] = self.n
            self.n += width
        return self.at[key]


def make_kernel(names_s, names_r, names_l):
    def kernel(
        tok_hbm, cot_hbm, q_hbm, tab_hbm,
        out_hbm, wg_hbm, wc_hbm,
        tok_v, cb, crel, gw, wst, ob, orel, gs, ra1, ra2, ry1, ry2, rz1, rz2, rb1, rb2, fin,
        tabv, tabs, ssem, rsem, lsem,
    ):
        k = lax.axis_index("dp")
        x = lax.axis_index("seq")
        t_me = lax.axis_index("tensor")
        y, z = t_me // 4, t_me % 4
        xp, xm, xo = (x + 1) % 4, (x + 3) % 4, (x + 2) % 4
        yp, ym, yo = (y + 1) % 4, (y + 3) % 4, (y + 2) % 4
        zp, zm, zo = (z + 1) % 4, (z + 3) % 4, (z + 2) % 4
        kk = 1 - k

        def dev(k_=None, x_=None, y_=None, z_=None):
            kd = k if k_ is None else k_
            xd = x if x_ is None else x_
            yd = y if y_ is None else y_
            zd = z if z_ is None else z_
            return (kd, xd, yd * 4 + zd)

        partner = dev(k_=kk)
        devs = {
            "x+": dev(x_=xp), "x-": dev(x_=xm), "y+": dev(y_=yp), "y-": dev(y_=ym), "y2": dev(y_=yo),
            "z+": dev(z_=zp), "z-": dev(z_=zm), "p": partner,
            "z+0": dev(k_=0, z_=zp), "z+1": dev(k_=1, z_=zp), "z-0": dev(k_=0, z_=zm), "z-1": dev(k_=1, z_=zm),
        }

        def remote(key, src, dst, to, skey=None, rkey=None, roff=None, rwidth=1):
            si = names_s.get(skey or key)
            ri = names_r.get(rkey or key, rwidth)
            if roff is not None:
                ri = ri + roff
            assert max(si, names_r.n) < 184
            return pltpu.make_async_remote_copy(
                src_ref=src, dst_ref=dst, send_sem=ssem.at[si], recv_sem=rsem.at[ri],
                device_id=devs[to], device_id_type=MESH,
            )

        def local(key, src, dst):
            return pltpu.make_async_copy(src, dst, lsem.at[names_l.get(key)])

        def slot(z_, k_):
            return pl.ds(pl.multiple_of((z_ * 2 + k_) * TOK, TOK), TOK)

        def part(z_, k_, lo):
            return pl.ds(pl.multiple_of((z_ * 2 + k_) * TOK + lo, 64), 64)

        def cols(group_y, group_z):
            return pl.ds(pl.multiple_of((group_y * 4 + group_z) * WID, 128), WID)

        peers = [partner, devs["x+"], devs["x-"], devs["y+"], devs["y-"], devs["y2"],
                 devs["z+0"], devs["z+1"], devs["z-0"], devs["z-1"]]
        barrier = pltpu.get_barrier_semaphore()
        for peer in peers:
            pl.semaphore_signal(barrier, inc=1, device_id=peer, device_id_type=MESH)
        pl.semaphore_wait(barrier, len(peers))

        d = [(y + 4 - (2 * k + j)) % 4 for j in (0, 1)]
        tok2 = tok_hbm

        t_own = local("t", tok2, tok_v.at[slot(z, k)])
        T0 = remote("T0", tok2, tok_v.at[slot(z, k)], "z+")
        T1 = remote("T1", tok2, tok_v.at[slot(z, k)], "z-")
        T2 = remote("T2", tok2, tok_v.at[slot(z, k)], "p")
        T0r = remote("T0", tok2, tok_v.at[slot(zm, k)], "z+")
        T1r = remote("T1", tok2, tok_v.at[slot(zp, k)], "z-")
        T2r = remote("T2", tok2, tok_v.at[slot(z, kk)], "p")
        T3 = remote("T3", tok_v.at[slot(zm, k)], tok_v.at[slot(zm, k)], "p")
        T4 = remote("T4", tok_v.at[slot(zp, k)], tok_v.at[slot(zp, k)], "p")
        T3r = remote("T3", tok_v.at[slot(zm, kk)], tok_v.at[slot(zm, kk)], "p")
        T4r = remote("T4", tok_v.at[slot(zp, kk)], tok_v.at[slot(zp, kk)], "p")
        T5 = remote("T5", tok_v.at[part(zm, k, 0)], tok_v.at[part(zm, k, 0)], "z+")
        T6 = remote("T6", tok_v.at[part(zp, k, 64)], tok_v.at[part(zp, k, 64)], "z-")
        T5r = remote("T5", tok_v.at[part(zo, k, 0)], tok_v.at[part(zo, k, 0)], "z+")
        T6r = remote("T6", tok_v.at[part(zo, k, 64)], tok_v.at[part(zo, k, 64)], "z-")
        T7 = remote("T7", tok_v.at[part(zo, k, 0)], tok_v.at[part(zo, k, 0)], "p")
        T8 = remote("T8", tok_v.at[part(zo, k, 64)], tok_v.at[part(zo, k, 64)], "p")
        T7r = remote("T7", tok_v.at[part(zo, kk, 0)], tok_v.at[part(zo, kk, 0)], "p")
        T8r = remote("T8", tok_v.at[part(zo, kk, 64)], tok_v.at[part(zo, kk, 64)], "p")

        def cot(group_y, group_z):
            return cot_hbm.at[:, cols(group_y, group_z)]

        c_own = [local(f"c{j}", cot(2 * k + j, z), cb.at[j, slot(z, k)]) for j in (0, 1)]
        c_sends = []
        for j in (0, 1):
            row = []
            row.append(remote(f"C3{j}", cot(j, zo), crel.at[0, j], "z+"))
            row.append(remote(f"C4{j}", cot(2 + j, zo), crel.at[1, j], "z-"))
            for k_ in (0, 1):
                row.append(remote(f"C1{j}{k_}", cot(2 * k_ + j, zp), cb.at[j, slot(z, k)], f"z+{k_}",
                                  rkey=f"C1r{j}", roff=k, rwidth=2))
                row.append(remote(f"C2{j}{k_}", cot(2 * k_ + j, zm), cb.at[j, slot(z, k)], f"z-{k_}",
                                  rkey=f"C2r{j}", roff=k, rwidth=2))
            row.append(remote(f"C0{j}", cot(2 * kk + j, z), cb.at[j, slot(z, k)], "p"))
            c_sends.append(row)
        C3r = [remote(f"C3{j}", cot(j, zo), crel.at[0, j], "z+") for j in (0, 1)]
        C4r = [remote(f"C4{j}", cot(2 + j, zo), crel.at[1, j], "z-") for j in (0, 1)]
        C5 = [remote(f"C5{j}", crel.at[0, j], cb.at[j, slot(zm, k)], "z+0", rkey=f"C5r{j}", roff=k, rwidth=2) for j in (0, 1)]
        C6 = [remote(f"C6{j}", crel.at[1, j], cb.at[j, slot(zp, k)], "z-1", rkey=f"C5r{j}", roff=k, rwidth=2) for j in (0, 1)]

        def c_recvs(j):
            out = [remote(f"C0{j}", cot(j, z), cb.at[j, slot(z, kk)], "p")]
            for i in (0, 1):
                out.append(remote(f"C1{j}0", cot(j, z), cb.at[j, slot(zm, i)], "z+", rkey=f"C1r{j}", roff=i, rwidth=2))
                out.append(remote(f"C2{j}0", cot(j, z), cb.at[j, slot(zp, i)], "z-", rkey=f"C2r{j}", roff=i, rwidth=2))
                out.append(remote(f"C5{j}", cot(j, z), cb.at[j, slot(zo, i)], "z+", rkey=f"C5r{j}", roff=i, rwidth=2))
            return out

        def wq(j, q):
            return wc_hbm.at[j, pl.ds(q * QTR, QTR)]

        def wlo(j, q):
            return wc_hbm.at[j, pl.ds(q * QTR, HALF)]

        def whi(j, q):
            return wc_hbm.at[j, pl.ds(q * QTR + HALF, HALF)]

        def wu(j, lo=0, n=YN):
            return wc_hbm.at[j, pl.ds(YLO + lo, n)]

        JS = (0, 1)
        W0 = [remote(f"W0{j}", wq(j, x), wq(j, x), "y+") for j in JS]
        W1 = [remote(f"W1{j}", wq(j, x), wq(j, x), "y-") for j in JS]
        W2 = [remote(f"W2{j}", wlo(j, x), wlo(j, x), "y+") for j in JS]
        W3 = [remote(f"W3{j}", whi(j, x), whi(j, x), "y-") for j in JS]
        W4 = [remote(f"W4{j}", wq(j, x), wq(j, x), "x+") for j in JS]
        W5 = [remote(f"W5{j}", wq(j, x), wq(j, x), "x-") for j in JS]
        W4r = [remote(f"W4{j}", wq(j, xm), wq(j, xm), "x+") for j in JS]
        W5r = [remote(f"W5{j}", wq(j, xp), wq(j, xp), "x-") for j in JS]
        W6 = [remote(f"W6{j}", wlo(j, xm), wlo(j, xm), "x+") for j in JS]
        W7 = [remote(f"W7{j}", whi(j, xp), whi(j, xp), "x-") for j in JS]
        W6r = [remote(f"W6{j}", wlo(j, xo), wlo(j, xo), "x+") for j in JS]
        W7r = [remote(f"W7{j}", whi(j, xo), whi(j, xo), "x-") for j in JS]
        U0 = [remote(f"WU0{j}", wu(j), wu(j), "y+") for j in JS]
        U1 = [remote(f"WU1{j}", wu(j), wu(j), "y-") for j in JS]
        U2 = [remote(f"WU2{j}", wu(j, 0, YH), wu(j, 0, YH), "y+") for j in JS]
        U3 = [remote(f"WU3{j}", wu(j, YH, YH), wu(j, YH, YH), "y-") for j in JS]
        V = [[remote(f"V{j}{i}", tab_hbm, tabv.at[j], to) for i, to in enumerate(("y+", "y-", "y2"))] for j in (0, 1)]

        def tab_start():
            for j in (0, 1):
                @pl.when(d[j] == 0)
                def _(j=j):
                    for copy in V[j]:
                        copy.start()
                    local(f"v{j}", tab_hbm, tabv.at[j]).start()

        def tab_finish():
            for j in (0, 1):
                @pl.when(d[j] == 0)
                def _(j=j):
                    local(f"v{j}", tab_hbm, tabv.at[j]).wait()

                for i, dist in enumerate((1, 3, 2)):
                    @pl.when(d[j] == dist)
                    def _(j=j, i=i):
                        V[j][i].wait_recv()
            cp = local("tab", tabv, tabs)
            cp.start()
            cp.wait()

        def quantize(j, start, n):
            @pl.loop(0, n // 4)
            def _(i):
                rows = pl.ds(start + i * 4, 4)
                wide = wst[rows].astype(F32)
                peak = jnp.max(jnp.abs(wide), axis=(1, 2), keepdims=True) + 1e-06
                levels = jnp.floor(wide * (7.0 / peak) + 0.5)
                wst[rows] = (levels * (peak / 7.0)).astype(BF16)

            cp = local("qw", wst.at[pl.ds(start, n)], wc_hbm.at[j, pl.ds(start, n)])
            cp.start()
            cp.wait()

        def w_first():
            for j in (0, 1):
                @pl.when(d[j] == 0)
                def _(j=j):
                    cp = local("q", q_hbm, wst.at[pl.ds(0, NSLOT)])
                    cp.start()
                    cp.wait()
                    quantize(j, x * QTR, QTR)
                    W0[j].start()
                    W1[j].start()
                    quantize(j, YLO, YN)
                    U0[j].start()
                    U1[j].start()
                    for q in (xp, xo, xm):
                        quantize(j, q * QTR, QTR)

        def w_second():
            for j in (0, 1):
                @pl.when(d[j] == 1)
                def _(j=j):
                    W0[j].wait_recv()
                    W2[j].start()
                    W4[j].start()
                    W5[j].start()

                @pl.when(d[j] == 3)
                def _(j=j):
                    W1[j].wait_recv()
                    W3[j].start()
                    W4[j].start()
                    W5[j].start()

        def w_third():
            for j in (0, 1):
                @pl.when(d[j] == 2)
                def _(j=j):
                    W2[j].wait_recv()
                    W3[j].wait_recv()
                    W4[j].start()
                    W5[j].start()

        def w_relay():
            for j in (0, 1):
                @pl.when(d[j] == 1)
                def _(j=j):
                    U0[j].wait_recv()
                    U2[j].start()

                @pl.when(d[j] == 3)
                def _(j=j):
                    U1[j].wait_recv()
                    U3[j].start()

        def w_fourth():
            for j in (0, 1):
                @pl.when(d[j] != 0)
                def _(j=j):
                    W4r[j].wait_recv()
                    W6[j].start()
                    W5r[j].wait_recv()
                    W7[j].start()

        def w_load(j):
            @pl.when(d[j] != 0)
            def _():
                W6r[j].wait_recv()
                W7r[j].wait_recv()

            @pl.when(d[j] == 2)
            def _():
                U2[j].wait_recv()
                U3[j].wait_recv()

            cp = local("w", wc_hbm.at[j], wst.at[pl.ds(0, NSLOT)])
            cp.start()
            cp.wait()

        def grads(j, hooks):
            @pl.loop(0, 16)
            def _(r):
                rows = pl.ds(pl.multiple_of(r * 256, 256), 256)
                g = lax.dot_general(tok_v[:, rows], cb[j], (((0,), (0,)), ((), ())), preferred_element_type=F32)
                g = g.astype(BF16)
                for h in (0, 1):
                    for c in range(COLS):
                        gw[(r * 2 + h) * COLS + c] = g[h * BS:(h + 1) * BS, c * BS:(c + 1) * BS]
                for at, steps in hooks.items():
                    @pl.when(r == at)
                    def _(steps=steps):
                        for step in steps:
                            step()

        def pick(j):
            for o in range(OWN):
                @pl.loop(0, SLOTS)
                def _(s, o=o):
                    gs[j, o, s] = gw[tabs[j, 2 + o // 4, (o % 4) * 32 + s]]

        def assemble(j):
            @pl.loop(0, ROWS)
            def _(r):
                for c in range(COLS):
                    gw[r * COLS + c] = wst[tabs[j, r // 16, (r % 16) * 8 + c]]

        def forward(j, hooks):
            @pl.loop(0, 4)
            def _(m):
                zz = (z + jnp.where(m == 0, 2, jnp.where(m == 1, 1, jnp.where(m == 2, 3, 0)))) % 4
                rows = pl.ds(pl.multiple_of(zz * 256, 256), 256)
                w = jnp.concatenate(
                    [jnp.concatenate([gw[r * COLS + c] for c in range(COLS)], axis=1) for r in range(ROWS)], axis=0
                )
                o = jnp.dot(tok_v[rows, :], w, preferred_element_type=F32)
                ob[j, rows, :] = o.astype(BF16)
                for at, steps in hooks.items():
                    @pl.when(m == at)
                    def _(steps=steps):
                        for step in steps:
                            step()

        o_own = [local(f"o{j}", ob.at[j, slot(z, k)], out_hbm.at[:, cols(2 * k + j, z)]) for j in (0, 1)]
        o_sends = []
        for j in (0, 1):
            dst = out_hbm.at[:, cols(2 * k + j, z)]
            row = []
            row.append(remote(f"O3{j}", ob.at[j, slot(zo, 0)], orel.at[0, j], "z+"))
            row.append(remote(f"O4{j}", ob.at[j, slot(zo, 1)], orel.at[1, j], "z-"))
            for i in (0, 1):
                row.append(remote(f"O1{j}{i}", ob.at[j, slot(zp, i)], dst, f"z+{i}", rkey=f"O1r{j}", roff=k, rwidth=2))
            for i in (0, 1):
                row.append(remote(f"O2{j}{i}", ob.at[j, slot(zm, i)], dst, f"z-{i}", rkey=f"O2r{j}", roff=k, rwidth=2))
            row.append(remote(f"O0{j}", ob.at[j, slot(z, kk)], dst, "p"))
            o_sends.append(row)
        O3r = [remote(f"O3{j}", orel.at[0, j], orel.at[0, j], "z+") for j in (0, 1)]
        O4r = [remote(f"O4{j}", orel.at[1, j], orel.at[1, j], "z-") for j in (0, 1)]
        O5 = [remote(f"O5{j}", orel.at[0, j], out_hbm.at[:, cols(2 * k + j, zm)], "z+0", rkey=f"O5r{j}", roff=k, rwidth=2) for j in (0, 1)]
        O6 = [remote(f"O6{j}", orel.at[1, j], out_hbm.at[:, cols(2 * k + j, zp)], "z-1", rkey=f"O5r{j}", roff=k, rwidth=2) for j in (0, 1)]

        def o_recvs(j):
            src = ob.at[j, slot(z, 0)]
            out = [remote(f"O0{j}", src, out_hbm.at[:, cols(2 * kk + j, z)], "p")]
            for i in (0, 1):
                out.append(remote(f"O1{j}0", src, out_hbm.at[:, cols(2 * i + j, zm)], "z+", rkey=f"O1r{j}", roff=i, rwidth=2))
                out.append(remote(f"O2{j}0", src, out_hbm.at[:, cols(2 * i + j, zp)], "z-", rkey=f"O2r{j}", roff=i, rwidth=2))
                out.append(remote(f"O5{j}", src, out_hbm.at[:, cols(2 * i + j, zo)], "z+", rkey=f"O5r{j}", roff=i, rwidth=2))
            return out

        def add1(dst, src, n):
            @pl.loop(0, n)
            def _(i):
                dst[i] = (dst[i].astype(F32) + src[i].astype(F32)).astype(BF16)

        def add2(dst, a, b, n):
            @pl.loop(0, n)
            def _(i):
                dst[i] = (dst[i].astype(F32) + a[i].astype(F32) + b[i].astype(F32)).astype(BF16)

        def sum3(out, dst, a, b, n):
            @pl.loop(0, n)
            def _(i):
                out[i] = dst[i].astype(F32) + a[i].astype(F32) + b[i].astype(F32)

        lo, hi = pl.ds(0, LO), pl.ds(LO, HI)

        class XStage:
            def __init__(self, name, j, base, first, second):
                self.j, self.base = j, base
                self.first = first
                self.c0 = remote(f"{name}0", gs.at[j, base + xo, lo], first.at[0], "x+")
                self.c1 = remote(f"{name}1", gs.at[j, base + xo, hi], first.at[1, pl.ds(0, HI)], "x-")
                self.c2l = remote(f"{name}2l", gs.at[j, base + xp, lo], second.at[0, lo], "x+")
                self.c2h = remote(f"{name}2h", gs.at[j, base + xp, hi], second.at[0, hi], "x+")
                self.c3l = remote(f"{name}3l", gs.at[j, base + xm, lo], second.at[1, lo], "x-")
                self.c3h = remote(f"{name}3h", gs.at[j, base + xm, hi], second.at[1, hi], "x-")

            def start(self, which=(0, 1, 2)):
                for i in which:
                    for copy in ((self.c0, self.c1), (self.c2h,), (self.c3l,))[i]:
                        copy.start()

            def middle(self):
                self.c0.wait_recv()
                add1(gs.at[self.j, self.base + xp, lo], self.first.at[0], LO)
                self.c2l.start()
                self.c1.wait_recv()
                add1(gs.at[self.j, self.base + xm, hi], self.first.at[1], HI)
                self.c3h.start()

            def arrive(self):
                for copy in (self.c2h, self.c3l, self.c2l, self.c3h):
                    copy.wait_recv()

            def sends(self):
                return [self.c0, self.c1, self.c2l, self.c2h, self.c3l, self.c3h]

        class YStage:
            def __init__(self, name, j, src, low, high, relay, high_relay, second, add):
                self.j, self.add, self.relay = j, add, relay
                self.low, self.high = src.at[low], src.at[high]
                self.c0 = remote(f"{name}0", self.low, relay, "y+")
                self.c1 = remote(f"{name}1", self.high, high_relay, "y-")
                self.c2l = remote(f"{name}2l", self.low, second.at[0].at[low], "y+")
                self.c2h = remote(f"{name}2h", self.high, second.at[0].at[high], "y+")
                self.c3l = remote(f"{name}3l", self.low, second.at[1].at[low], "y-")
                self.c3h = remote(f"{name}3h", self.high, second.at[1].at[high], "y-")

            def start(self):
                @pl.when(d[self.j] == 2)
                def _():
                    self.c0.start()
                    self.c1.start()

                @pl.when(d[self.j] == 3)
                def _():
                    self.c2h.start()

                @pl.when(d[self.j] == 1)
                def _():
                    self.c3l.start()

            def middle(self):
                @pl.when(d[self.j] == 3)
                def _():
                    self.c0.wait_recv()
                    self.add(self.low, self.relay, 0)
                    self.c2l.start()

                @pl.when(d[self.j] == 1)
                def _():
                    self.c1.wait_recv()
                    self.add(self.high, self.relay, 1)
                    self.c3h.start()

            def arrive(self):
                for copy in (self.c2h, self.c3l, self.c2l, self.c3h):
                    copy.wait_recv()

            def wait_sends(self):
                @pl.when(d[self.j] == 2)
                def _():
                    self.c0.wait_send()
                    self.c1.wait_send()

                @pl.when(d[self.j] == 3)
                def _():
                    self.c2h.wait_send()
                    self.c2l.wait_send()

                @pl.when(d[self.j] == 1)
                def _():
                    self.c3l.wait_send()
                    self.c3h.wait_send()

        AX = [XStage(f"A{j}", j, 0, ra1.at[j], ra2.at[j]) for j in (0, 1)]
        def add_ay(dst, src, half):
            add1(dst, src, (LO, HI)[half])

        AY = [YStage(f"Y{j}", j, gs.at[j, x], lo, hi, ry1, ry1.at[pl.ds(0, HI)], ry2, add_ay) for j in (0, 1)]
        order = (xo, xp, xm, x)
        BY = [
            [YStage(f"Z{j}{i}", j, gs.at[j, 4 + q], lo, hi, rz1.at[i], rz1.at[i, pl.ds(0, HI)], rz2.at[i], add_ay)
             for i, q in enumerate(order)]
            for j in (0, 1)
        ]
        BX = [XStage(f"B{j}", j, 4, rb1, rb2) for j in (0, 1)]

        def ax_end(j):
            AX[j].arrive()
            add2(gs.at[j, x], ra2.at[j, 0], ra2.at[j, 1], SLOTS)
            AY[j].start()

        def by_end(j, i):
            def go():
                @pl.when(d[j] == 0)
                def _():
                    BY[j][i].arrive()
                    add2(gs.at[j, 4 + order[i]], rz2.at[i, 0], rz2.at[i, 1], SLOTS)
                    if i < 3:
                        BX[j].start((i,))
            return go

        def bx_middle(j):
            @pl.when(d[j] == 0)
            def _():
                BX[j].middle()

        g_own = local("g", fin.at[k], wg_hbm)
        G = remote("G", fin.at[kk], wg_hbm, "p")

        def finals(j):
            @pl.when(d[j] == 0)
            def _():
                AY[j].arrive()
                sum3(fin.at[0], gs.at[j, x], ry2.at[0], ry2.at[1], SLOTS)
                BX[j].arrive()
                sum3(fin.at[1], gs.at[j, 4 + x], rb2.at[0], rb2.at[1], SLOTS)
                G.start()
                g_own.start()

        def o_start(j, *which):
            def go():
                for i in which:
                    if i < 0:
                        o_own[j].start()
                    else:
                        o_sends[j][i].start()
            return go

        def o_hooks(j):
            return {0: [o_start(j, 0, 1)], 1: [o_start(j, 2, 3)], 2: [o_start(j, 4, 5)], 3: [o_start(j, 6, -1)]}

        def o_relay(j):
            O3r[j].wait_recv()
            O5[j].start()
            O4r[j].wait_recv()
            O6[j].start()

        def c_relay(j):
            C3r[j].wait_recv()
            C5[j].start()
            C4r[j].wait_recv()
            C6[j].start()

        def reduce_start(j):
            AX[j].start()
            for i in range(4):
                BY[j][i].start()

        t_own.start()
        for copy in (T0, T1, T2):
            copy.start()
        tab_start()
        for copy in c_sends[0] + c_own:
            copy.start()
        w_first()
        wst[NSLOT] = jnp.zeros((BS, BS), BF16)
        tab_finish()
        w_second()
        w_third()
        T0r.wait_recv()
        T5.start()
        T3.start()
        T1r.wait_recv()
        T6.start()
        T4.start()
        c_relay(0)
        for copy in c_sends[1]:
            copy.start()
        w_relay()
        w_fourth()
        T5r.wait_recv()
        T7.start()
        T6r.wait_recv()
        T8.start()
        t_own.wait()
        for copy in (T2r, T3r, T4r, T7r, T8r):
            copy.wait_recv()
        c_own[0].wait()
        for copy in c_recvs(0):
            copy.wait_recv()
        grads(0, {})
        pick(0)
        reduce_start(0)
        c_relay(1)
        c_own[1].wait()
        for copy in c_recvs(1):
            copy.wait_recv()
        grads(1, {8: [BY[0][0].middle, BY[0][1].middle], 12: [AX[0].middle]})
        pick(1)
        reduce_start(1)
        BY[0][2].middle()
        BY[0][3].middle()
        w_load(0)
        assemble(0)
        hooks = o_hooks(0)
        hooks[1] += [lambda: ax_end(0)]
        hooks[2] += [by_end(0, 0)]
        hooks[3] += [AX[1].middle, AY[0].middle]
        forward(0, hooks)
        w_load(1)
        assemble(1)
        o_relay(0)
        hooks = o_hooks(1)
        hooks[0] += [by_end(0, 1), by_end(0, 2), by_end(0, 3)]
        hooks[1] += [BY[1][0].middle]
        hooks[2] += [BY[1][1].middle, lambda: bx_middle(0)]
        hooks[3] += [BY[1][2].middle]
        forward(1, hooks)
        ax_end(1)
        BY[1][3].middle()
        by_end(1, 0)()
        by_end(1, 1)()
        o_relay(1)
        by_end(1, 2)()
        AY[1].middle()
        bx_middle(1)
        by_end(1, 3)()
        finals(0)
        finals(1)

        for j in (0, 1):
            for copy in o_recvs(j):
                copy.wait_recv()
            o_own[j].wait()

        own_final = (y // 2) == k

        @pl.when(own_final)
        def _():
            g_own.wait()
            G.wait_send()

        @pl.when(jnp.logical_not(own_final))
        def _():
            G.wait_recv()

        for copy in (T0, T1, T2, T3, T4, T5, T6, T7, T8):
            copy.wait_send()
        for j in (0, 1):
            for copy in c_sends[j] + [C5[j], C6[j]] + o_sends[j] + [O5[j], O6[j]] + AX[j].sends():
                copy.wait_send()
            AY[j].wait_sends()
            for i in range(4):
                BY[j][i].wait_sends()

            @pl.when(d[j] == 0)
            def _(j=j):
                for copy in [W0[j], W1[j], U0[j], U1[j]] + V[j] + BX[j].sends():
                    copy.wait_send()

            @pl.when(d[j] == 1)
            def _(j=j):
                W2[j].wait_send()
                U2[j].wait_send()

            @pl.when(d[j] == 3)
            def _(j=j):
                W3[j].wait_send()
                U3[j].wait_send()

            @pl.when(d[j] != 0)
            def _(j=j):
                for copy in (W4[j], W5[j], W6[j], W7[j]):
                    copy.wait_send()

    return kernel


def tables(slot_ids, live):
    numbers = jnp.arange(ROWS * 8, dtype=jnp.int32)
    block = jnp.where(numbers % 8 < COLS, (numbers // 8) * COLS + numbers % 8, -1)
    match = ((slot_ids[:, None] == block[None, :]) & live[:, None]).astype(jnp.int32)
    index = jnp.sum(match * (jnp.arange(NSLOT, dtype=jnp.int32)[:, None] - NSLOT), axis=0) + NSLOT
    pad = ((0, 0), (0, 32 - SLOTS))
    ids = slot_ids.reshape(OWN, SLOTS)
    ids = jnp.pad(ids, pad).reshape(2, 128)
    return jnp.concatenate([index.reshape(2, 128), ids, jnp.zeros((4, 128), jnp.int32)], axis=0)


def shards(tokens, cotangent, master, block_ids, live_count):
    owners, slots = block_ids.shape
    live = jnp.arange(slots, dtype=jnp.int32)[None, :] < live_count
    table = tables(block_ids.reshape(owners * slots), live.reshape(owners * slots))
    vmem = pltpu.VMEM
    blk = (BS, BS)
    anyspec = pl.BlockSpec(memory_space=pl.ANY)
    outputs, w_grad, _ = pl.pallas_call(
        make_kernel(Names(), Names(), Names()),
        out_shape=(
            jax.ShapeDtypeStruct(cotangent.shape, BF16),
            jax.ShapeDtypeStruct((slots,) + blk, F32),
            jax.ShapeDtypeStruct((2, NSLOT) + blk, BF16),
        ),
        in_specs=[anyspec] * 4,
        out_specs=(anyspec,) * 3,
        scratch_shapes=[
            vmem((8 * TOK, ROWS * BS), BF16),
            vmem((2, 8 * TOK, WID), BF16),
            vmem((2, 2, TOK, WID), BF16),
            vmem((ROWS * COLS,) + blk, BF16),
            vmem((NSLOT + 1,) + blk, BF16),
            vmem((2, 8 * TOK, WID), BF16),
            vmem((2, 2, TOK, WID), BF16),
            vmem((2, OWN, SLOTS) + blk, BF16),
            vmem((2, 2, LO) + blk, BF16),
            vmem((2, 2, SLOTS) + blk, BF16),
            vmem((LO,) + blk, BF16),
            vmem((2, SLOTS) + blk, BF16),
            vmem((4, LO) + blk, BF16),
            vmem((4, 2, SLOTS) + blk, BF16),
            vmem((2, LO) + blk, BF16),
            vmem((2, SLOTS) + blk, BF16),
            vmem((2, SLOTS) + blk, F32),
            vmem((2, 8, 128), jnp.int32),
            pltpu.SMEM((2, 8, 128), jnp.int32),
            pltpu.SemaphoreType.DMA((184,)),
            pltpu.SemaphoreType.DMA((184,)),
            pltpu.SemaphoreType.DMA((16,)),
        ],
        compiler_params=pltpu.CompilerParams(
            collective_id=0, has_side_effects=True, vmem_limit_bytes=66 * 1024 * 1000
        ),
    )(tokens, cotangent, master.reshape(owners * slots, BS, BS), table)
    def finish_body(count_ref, o_ref, g_ref, o_out, g_out):
        o_out[...] = o_ref[...]
        own = count_ref[lax.axis_index("dp") * 4 + lax.axis_index("seq"), 0]
        first = pl.program_id(0) * 3
        for i in range(3):
            keep = (first + i < own).astype(F32)
            g_out[i] = g_ref[i] * keep

    return finish(finish_body, live_count, outputs, w_grad)


def finish(body, live_count, outputs, w_grad):
    steps = 7
    wide = outputs.shape[1] // steps
    each = SLOTS // steps
    outputs, w_grad = pl.pallas_call(
        body,
        grid=(steps,),
        out_shape=(
            jax.ShapeDtypeStruct(outputs.shape, outputs.dtype),
            jax.ShapeDtypeStruct(w_grad.shape, w_grad.dtype),
        ),
        in_specs=[
            pl.BlockSpec(memory_space=pltpu.SMEM),
            pl.BlockSpec((outputs.shape[0], wide), lambda i: (0, i)),
            pl.BlockSpec((each, BS, BS), lambda i: (i, 0, 0)),
        ],
        out_specs=(
            pl.BlockSpec((outputs.shape[0], wide), lambda i: (0, i)),
            pl.BlockSpec((each, BS, BS), lambda i: (i, 0, 0)),
        ),
    )(live_count, outputs, w_grad)
    return outputs, w_grad[None]


def solution(mesh):
    return jax.shard_map(
        shards,
        mesh=mesh,
        in_specs=(
            P(("dp", "seq", "tensor"), None),
            P(("dp", "seq", "tensor"), None),
            P(None, "tensor", None, None),
            P(None, "tensor"),
            P(None, "tensor"),
        ),
        out_specs=(P(("dp", "seq", "tensor"), None), P(("dp", "seq"), "tensor", None, None)),
        check_vma=False,
    )
```

```python
import functools

import jax
import jax.numpy as jnp
from jax import lax
from jax.experimental import pallas as pl
from jax.experimental.pallas import tpu as pltpu
from jax.sharding import PartitionSpec as P

BS = 128
ROWS = 32
COLS = 7
OWN = 8
SLOTS = 21
NSLOT = OWN * SLOTS
QTR = 28
HALF = QTR // 2
YLO = 4 * QTR
YN = NSLOT - YLO
YH = YN // 2
LO, HI = 11, 10
WID = COLS * BS
TOK = 128
MESH = pl.DeviceIdType.MESH
F32 = jnp.float32
BF16 = jnp.bfloat16


class Names:
    def __init__(self):
        self.n = 0
        self.at = {}

    def get(self, key, width=1):
        if key not in self.at:
            self.at[key] = self.n
            self.n += width
        return self.at[key]


def make_kernel(names_s, names_r, names_l):
    def kernel(
        tok_hbm, cot_hbm, q_hbm, tab_hbm,
        out_hbm, wg_hbm, wc_hbm,
        tok_v, cb, crel, gw, wst, ob, orel, gs, ra1, ra2, ry1, ry2, rz1, rz2, rb1, rb2, fin,
        tabv, tabs, ssem, rsem, lsem,
    ):
        k = lax.axis_index("dp")
        x = lax.axis_index("seq")
        t_me = lax.axis_index("tensor")
        y, z = t_me // 4, t_me % 4
        xp, xm, xo = (x + 1) % 4, (x + 3) % 4, (x + 2) % 4
        yp, ym, yo = (y + 1) % 4, (y + 3) % 4, (y + 2) % 4
        zp, zm, zo = (z + 1) % 4, (z + 3) % 4, (z + 2) % 4
        kk = 1 - k

        def dev(k_=None, x_=None, y_=None, z_=None):
            kd = k if k_ is None else k_
            xd = x if x_ is None else x_
            yd = y if y_ is None else y_
            zd = z if z_ is None else z_
            return (kd, xd, yd * 4 + zd)

        partner = dev(k_=kk)
        devs = {
            "x+": dev(x_=xp), "x-": dev(x_=xm), "y+": dev(y_=yp), "y-": dev(y_=ym), "y2": dev(y_=yo),
            "z+": dev(z_=zp), "z-": dev(z_=zm), "p": partner,
            "z+0": dev(k_=0, z_=zp), "z+1": dev(k_=1, z_=zp), "z-0": dev(k_=0, z_=zm), "z-1": dev(k_=1, z_=zm),
        }

        def remote(key, src, dst, to, skey=None, rkey=None, roff=None, rwidth=1):
            si = names_s.get(skey or key)
            ri = names_r.get(rkey or key, rwidth)
            if roff is not None:
                ri = ri + roff
            assert max(si, names_r.n) < 184
            return pltpu.make_async_remote_copy(
                src_ref=src, dst_ref=dst, send_sem=ssem.at[si], recv_sem=rsem.at[ri],
                device_id=devs[to], device_id_type=MESH,
            )

        def local(key, src, dst):
            return pltpu.make_async_copy(src, dst, lsem.at[names_l.get(key)])

        def slot(z_, k_):
            return pl.ds(pl.multiple_of((z_ * 2 + k_) * TOK, TOK), TOK)

        def part(z_, k_, lo):
            return pl.ds(pl.multiple_of((z_ * 2 + k_) * TOK + lo, 64), 64)

        def cols(group_y, group_z):
            return pl.ds(pl.multiple_of((group_y * 4 + group_z) * WID, 128), WID)

        peers = [partner, devs["x+"], devs["x-"], devs["y+"], devs["y-"], devs["y2"],
                 devs["z+0"], devs["z+1"], devs["z-0"], devs["z-1"]]
        barrier = pltpu.get_barrier_semaphore()
        for peer in peers:
            pl.semaphore_signal(barrier, inc=1, device_id=peer, device_id_type=MESH)
        pl.semaphore_wait(barrier, len(peers))

        d = [(y + 4 - (2 * k + j)) % 4 for j in (0, 1)]
        tok2 = tok_hbm

        t_own = local("t", tok2, tok_v.at[slot(z, k)])
        T0 = remote("T0", tok2, tok_v.at[slot(z, k)], "z+")
        T1 = remote("T1", tok2, tok_v.at[slot(z, k)], "z-")
        T2 = remote("T2", tok2, tok_v.at[slot(z, k)], "p")
        T0r = remote("T0", tok2, tok_v.at[slot(zm, k)], "z+")
        T1r = remote("T1", tok2, tok_v.at[slot(zp, k)], "z-")
        T2r = remote("T2", tok2, tok_v.at[slot(z, kk)], "p")
        T3 = remote("T3", tok_v.at[slot(zm, k)], tok_v.at[slot(zm, k)], "p")
        T4 = remote("T4", tok_v.at[slot(zp, k)], tok_v.at[slot(zp, k)], "p")
        T3r = remote("T3", tok_v.at[slot(zm, kk)], tok_v.at[slot(zm, kk)], "p")
        T4r = remote("T4", tok_v.at[slot(zp, kk)], tok_v.at[slot(zp, kk)], "p")
        T5 = remote("T5", tok_v.at[part(zm, k, 0)], tok_v.at[part(zm, k, 0)], "z+")
        T6 = remote("T6", tok_v.at[part(zp, k, 64)], tok_v.at[part(zp, k, 64)], "z-")
        T5r = remote("T5", tok_v.at[part(zo, k, 0)], tok_v.at[part(zo, k, 0)], "z+")
        T6r = remote("T6", tok_v.at[part(zo, k, 64)], tok_v.at[part(zo, k, 64)], "z-")
        T7 = remote("T7", tok_v.at[part(zo, k, 0)], tok_v.at[part(zo, k, 0)], "p")
        T8 = remote("T8", tok_v.at[part(zo, k, 64)], tok_v.at[part(zo, k, 64)], "p")
        T7r = remote("T7", tok_v.at[part(zo, kk, 0)], tok_v.at[part(zo, kk, 0)], "p")
        T8r = remote("T8", tok_v.at[part(zo, kk, 64)], tok_v.at[part(zo, kk, 64)], "p")

        def cot(group_y, group_z):
            return cot_hbm.at[:, cols(group_y, group_z)]

        c_own = [local(f"c{j}", cot(2 * k + j, z), cb.at[j, slot(z, k)]) for j in (0, 1)]
        c_sends = []
        for j in (0, 1):
            row = []
            row.append(remote(f"C3{j}", cot(j, zo), crel.at[0, j], "z+"))
            row.append(remote(f"C4{j}", cot(2 + j, zo), crel.at[1, j], "z-"))
            for k_ in (0, 1):
                row.append(remote(f"C1{j}{k_}", cot(2 * k_ + j, zp), cb.at[j, slot(z, k)], f"z+{k_}",
                                  rkey=f"C1r{j}", roff=k, rwidth=2))
                row.append(remote(f"C2{j}{k_}", cot(2 * k_ + j, zm), cb.at[j, slot(z, k)], f"z-{k_}",
                                  rkey=f"C2r{j}", roff=k, rwidth=2))
            row.append(remote(f"C0{j}", cot(2 * kk + j, z), cb.at[j, slot(z, k)], "p"))
            c_sends.append(row)
        C3r = [remote(f"C3{j}", cot(j, zo), crel.at[0, j], "z+") for j in (0, 1)]
        C4r = [remote(f"C4{j}", cot(2 + j, zo), crel.at[1, j], "z-") for j in (0, 1)]
        C5 = [remote(f"C5{j}", crel.at[0, j], cb.at[j, slot(zm, k)], "z+0", rkey=f"C5r{j}", roff=k, rwidth=2) for j in (0, 1)]
        C6 = [remote(f"C6{j}", crel.at[1, j], cb.at[j, slot(zp, k)], "z-1", rkey=f"C5r{j}", roff=k, rwidth=2) for j in (0, 1)]

        def c_recvs(j):
            out = [remote(f"C0{j}", cot(j, z), cb.at[j, slot(z, kk)], "p")]
            for i in (0, 1):
                out.append(remote(f"C1{j}0", cot(j, z), cb.at[j, slot(zm, i)], "z+", rkey=f"C1r{j}", roff=i, rwidth=2))
                out.append(remote(f"C2{j}0", cot(j, z), cb.at[j, slot(zp, i)], "z-", rkey=f"C2r{j}", roff=i, rwidth=2))
                out.append(remote(f"C5{j}", cot(j, z), cb.at[j, slot(zo, i)], "z+", rkey=f"C5r{j}", roff=i, rwidth=2))
            return out

        def wq(j, q):
            return wc_hbm.at[j, pl.ds(q * QTR, QTR)]

        def wlo(j, q):
            return wc_hbm.at[j, pl.ds(q * QTR, HALF)]

        def whi(j, q):
            return wc_hbm.at[j, pl.ds(q * QTR + HALF, HALF)]

        def wu(j, lo=0, n=YN):
            return wc_hbm.at[j, pl.ds(YLO + lo, n)]

        JS = (0, 1)
        W0 = [remote(f"W0{j}", wq(j, x), wq(j, x), "y+") for j in JS]
        W1 = [remote(f"W1{j}", wq(j, x), wq(j, x), "y-") for j in JS]
        W2 = [remote(f"W2{j}", wlo(j, x), wlo(j, x), "y+") for j in JS]
        W3 = [remote(f"W3{j}", whi(j, x), whi(j, x), "y-") for j in JS]
        W4 = [remote(f"W4{j}", wq(j, x), wq(j, x), "x+") for j in JS]
        W5 = [remote(f"W5{j}", wq(j, x), wq(j, x), "x-") for j in JS]
        W4r = [remote(f"W4{j}", wq(j, xm), wq(j, xm), "x+") for j in JS]
        W5r = [remote(f"W5{j}", wq(j, xp), wq(j, xp), "x-") for j in JS]
        W6 = [remote(f"W6{j}", wlo(j, xm), wlo(j, xm), "x+") for j in JS]
        W7 = [remote(f"W7{j}", whi(j, xp), whi(j, xp), "x-") for j in JS]
        W6r = [remote(f"W6{j}", wlo(j, xo), wlo(j, xo), "x+") for j in JS]
        W7r = [remote(f"W7{j}", whi(j, xo), whi(j, xo), "x-") for j in JS]
        U0 = [remote(f"WU0{j}", wu(j), wu(j), "y+") for j in JS]
        U1 = [remote(f"WU1{j}", wu(j), wu(j), "y-") for j in JS]
        U2 = [remote(f"WU2{j}", wu(j, 0, YH), wu(j, 0, YH), "y+") for j in JS]
        U3 = [remote(f"WU3{j}", wu(j, YH, YH), wu(j, YH, YH), "y-") for j in JS]
        V = [[remote(f"V{j}{i}", tab_hbm, tabv.at[j], to) for i, to in enumerate(("y+", "y-", "y2"))] for j in (0, 1)]

        def tab_start():
            for j in (0, 1):
                @pl.when(d[j] == 0)
                def _(j=j):
                    for copy in V[j]:
                        copy.start()
                    local(f"v{j}", tab_hbm, tabv.at[j]).start()

        def tab_finish():
            for j in (0, 1):
                @pl.when(d[j] == 0)
                def _(j=j):
                    local(f"v{j}", tab_hbm, tabv.at[j]).wait()

                for i, dist in enumerate((1, 3, 2)):
                    @pl.when(d[j] == dist)
                    def _(j=j, i=i):
                        V[j][i].wait_recv()
            cp = local("tab", tabv, tabs)
            cp.start()
            cp.wait()

        def quantize(j, start, n):
            @pl.loop(0, n // 4)
            def _(i):
                rows = pl.ds(start + i * 4, 4)
                wide = wst[rows].astype(F32)
                peak = jnp.max(jnp.abs(wide), axis=(1, 2), keepdims=True) + 1e-06
                levels = jnp.floor(wide * (7.0 / peak) + 0.5)
                wst[rows] = (levels * (peak / 7.0)).astype(BF16)

            cp = local("qw", wst.at[pl.ds(start, n)], wc_hbm.at[j, pl.ds(start, n)])
            cp.start()
            cp.wait()

        def w_first():
            for j in (0, 1):
                @pl.when(d[j] == 0)
                def _(j=j):
                    cp = local("q", q_hbm, wst.at[pl.ds(0, NSLOT)])
                    cp.start()
                    cp.wait()
                    quantize(j, x * QTR, QTR)
                    W0[j].start()
                    W1[j].start()
                    quantize(j, YLO, YN)
                    U0[j].start()
                    U1[j].start()
                    for q in (xp, xo, xm):
                        quantize(j, q * QTR, QTR)

        def w_second():
            for j in (0, 1):
                @pl.when(d[j] == 1)
                def _(j=j):
                    W0[j].wait_recv()
                    W2[j].start()
                    W4[j].start()
                    W5[j].start()

                @pl.when(d[j] == 3)
                def _(j=j):
                    W1[j].wait_recv()
                    W3[j].start()
                    W4[j].start()
                    W5[j].start()

        def w_third():
            for j in (0, 1):
                @pl.when(d[j] == 2)
                def _(j=j):
                    W2[j].wait_recv()
                    W3[j].wait_recv()
                    W4[j].start()
                    W5[j].start()

        def w_relay():
            for j in (0, 1):
                @pl.when(d[j] == 1)
                def _(j=j):
                    U0[j].wait_recv()
                    U2[j].start()

                @pl.when(d[j] == 3)
                def _(j=j):
                    U1[j].wait_recv()
                    U3[j].start()

        def w_fourth():
            for j in (0, 1):
                @pl.when(d[j] != 0)
                def _(j=j):
                    W4r[j].wait_recv()
                    W6[j].start()
                    W5r[j].wait_recv()
                    W7[j].start()

        def w_load(j):
            @pl.when(d[j] != 0)
            def _():
                W6r[j].wait_recv()
                W7r[j].wait_recv()

            @pl.when(d[j] == 2)
            def _():
                U2[j].wait_recv()
                U3[j].wait_recv()

            local("w", wc_hbm.at[j], wst.at[pl.ds(0, NSLOT)]).start()

        def w_ready(j):
            local("w", wc_hbm.at[j], wst.at[pl.ds(0, NSLOT)]).wait()

        def grads(j, hooks):
            @pl.loop(0, 16)
            def _(r):
                rows = pl.ds(pl.multiple_of(r * 256, 256), 256)
                g = lax.dot_general(tok_v[:, rows], cb[j], (((0,), (0,)), ((), ())), preferred_element_type=F32)
                g = g.astype(BF16)
                for h in (0, 1):
                    for c in range(COLS):
                        gw[(r * 2 + h) * COLS + c] = g[h * BS:(h + 1) * BS, c * BS:(c + 1) * BS]
                for at, steps in hooks.items():
                    @pl.when(r == at)
                    def _(steps=steps):
                        for step in steps:
                            step()

        def pick(j):
            for o in range(OWN):
                @pl.loop(0, SLOTS)
                def _(s, o=o):
                    gs[j, o, s] = gw[tabs[j, 2 + o // 4, (o % 4) * 32 + s]]

        def assemble(j):
            @pl.loop(0, ROWS)
            def _(r):
                for c in range(COLS):
                    gw[r * COLS + c] = wst[tabs[j, r // 16, (r % 16) * 8 + c]]

        def forward(j, lo_m, hi_m, hooks):
            @pl.loop(lo_m, hi_m)
            def _(m):
                zz = (z + jnp.where(m == 0, 2, jnp.where(m == 1, 1, jnp.where(m == 2, 3, 0)))) % 4
                rows = pl.ds(pl.multiple_of(zz * 256, 256), 256)
                w = jnp.concatenate(
                    [jnp.concatenate([gw[r * COLS + c] for c in range(COLS)], axis=1) for r in range(ROWS)], axis=0
                )
                o = jnp.dot(tok_v[rows, :], w, preferred_element_type=F32)
                ob[j, rows, :] = o.astype(BF16)
                for at, steps in hooks.items():
                    @pl.when(m == at)
                    def _(steps=steps):
                        for step in steps:
                            step()

        o_own = [local(f"o{j}", ob.at[j, slot(z, k)], out_hbm.at[:, cols(2 * k + j, z)]) for j in (0, 1)]
        o_sends = []
        for j in (0, 1):
            dst = out_hbm.at[:, cols(2 * k + j, z)]
            row = []
            row.append(remote(f"O3{j}", ob.at[j, slot(zo, 0)], orel.at[0, j], "z+"))
            row.append(remote(f"O4{j}", ob.at[j, slot(zo, 1)], orel.at[1, j], "z-"))
            for i in (0, 1):
                row.append(remote(f"O1{j}{i}", ob.at[j, slot(zp, i)], dst, f"z+{i}", rkey=f"O1r{j}", roff=k, rwidth=2))
            for i in (0, 1):
                row.append(remote(f"O2{j}{i}", ob.at[j, slot(zm, i)], dst, f"z-{i}", rkey=f"O2r{j}", roff=k, rwidth=2))
            row.append(remote(f"O0{j}", ob.at[j, slot(z, kk)], dst, "p"))
            o_sends.append(row)
        O3r = [remote(f"O3{j}", orel.at[0, j], orel.at[0, j], "z+") for j in (0, 1)]
        O4r = [remote(f"O4{j}", orel.at[1, j], orel.at[1, j], "z-") for j in (0, 1)]
        O5 = [remote(f"O5{j}", orel.at[0, j], out_hbm.at[:, cols(2 * k + j, zm)], "z+0", rkey=f"O5r{j}", roff=k, rwidth=2) for j in (0, 1)]
        O6 = [remote(f"O6{j}", orel.at[1, j], out_hbm.at[:, cols(2 * k + j, zp)], "z-1", rkey=f"O5r{j}", roff=k, rwidth=2) for j in (0, 1)]

        def o_recvs(j):
            src = ob.at[j, slot(z, 0)]
            out = [remote(f"O0{j}", src, out_hbm.at[:, cols(2 * kk + j, z)], "p")]
            for i in (0, 1):
                out.append(remote(f"O1{j}0", src, out_hbm.at[:, cols(2 * i + j, zm)], "z+", rkey=f"O1r{j}", roff=i, rwidth=2))
                out.append(remote(f"O2{j}0", src, out_hbm.at[:, cols(2 * i + j, zp)], "z-", rkey=f"O2r{j}", roff=i, rwidth=2))
                out.append(remote(f"O5{j}", src, out_hbm.at[:, cols(2 * i + j, zo)], "z+", rkey=f"O5r{j}", roff=i, rwidth=2))
            return out

        def add1(dst, src, n):
            @pl.loop(0, n)
            def _(i):
                dst[i] = (dst[i].astype(F32) + src[i].astype(F32)).astype(BF16)

        def add2(dst, a, b, n):
            @pl.loop(0, n)
            def _(i):
                dst[i] = (dst[i].astype(F32) + a[i].astype(F32) + b[i].astype(F32)).astype(BF16)

        def sum3(out, dst, a, b, count):
            @pl.loop(0, SLOTS)
            def _(i):
                live = jnp.minimum(jnp.maximum(count - i, 0), 1).astype(F32)
                out[i] = (dst[i].astype(F32) + a[i].astype(F32) + b[i].astype(F32)) * live

        lo, hi = pl.ds(0, LO), pl.ds(LO, HI)

        class XStage:
            def __init__(self, name, j, base, first, second):
                self.j, self.base = j, base
                self.first = first
                self.c0 = remote(f"{name}0", gs.at[j, base + xo, lo], first.at[0], "x+")
                self.c1 = remote(f"{name}1", gs.at[j, base + xo, hi], first.at[1, pl.ds(0, HI)], "x-")
                self.c2l = remote(f"{name}2l", gs.at[j, base + xp, lo], second.at[0, lo], "x+")
                self.c2h = remote(f"{name}2h", gs.at[j, base + xp, hi], second.at[0, hi], "x+")
                self.c3l = remote(f"{name}3l", gs.at[j, base + xm, lo], second.at[1, lo], "x-")
                self.c3h = remote(f"{name}3h", gs.at[j, base + xm, hi], second.at[1, hi], "x-")

            def start(self, which=(0, 1, 2)):
                for i in which:
                    for copy in ((self.c0, self.c1), (self.c2h,), (self.c3l,))[i]:
                        copy.start()

            def middle(self):
                self.c0.wait_recv()
                add1(gs.at[self.j, self.base + xp, lo], self.first.at[0], LO)
                self.c2l.start()
                self.c1.wait_recv()
                add1(gs.at[self.j, self.base + xm, hi], self.first.at[1], HI)
                self.c3h.start()

            def arrive(self):
                for copy in (self.c2h, self.c3l, self.c2l, self.c3h):
                    copy.wait_recv()

            def sends(self):
                return [self.c0, self.c1, self.c2l, self.c2h, self.c3l, self.c3h]

        class YStage:
            def __init__(self, name, j, src, low, high, relay, high_relay, second, add):
                self.j, self.add, self.relay = j, add, relay
                self.low, self.high = src.at[low], src.at[high]
                self.c0 = remote(f"{name}0", self.low, relay, "y+")
                self.c1 = remote(f"{name}1", self.high, high_relay, "y-")
                self.c2l = remote(f"{name}2l", self.low, second.at[0].at[low], "y+")
                self.c2h = remote(f"{name}2h", self.high, second.at[0].at[high], "y+")
                self.c3l = remote(f"{name}3l", self.low, second.at[1].at[low], "y-")
                self.c3h = remote(f"{name}3h", self.high, second.at[1].at[high], "y-")

            def start(self):
                @pl.when(d[self.j] == 2)
                def _():
                    self.c0.start()
                    self.c1.start()

                @pl.when(d[self.j] == 3)
                def _():
                    self.c2h.start()

                @pl.when(d[self.j] == 1)
                def _():
                    self.c3l.start()

            def middle(self):
                @pl.when(d[self.j] == 3)
                def _():
                    self.c0.wait_recv()
                    self.add(self.low, self.relay, 0)
                    self.c2l.start()

                @pl.when(d[self.j] == 1)
                def _():
                    self.c1.wait_recv()
                    self.add(self.high, self.relay, 1)
                    self.c3h.start()

            def arrive(self):
                for copy in (self.c2h, self.c3l, self.c2l, self.c3h):
                    copy.wait_recv()

            def wait_sends(self):
                @pl.when(d[self.j] == 2)
                def _():
                    self.c0.wait_send()
                    self.c1.wait_send()

                @pl.when(d[self.j] == 3)
                def _():
                    self.c2h.wait_send()
                    self.c2l.wait_send()

                @pl.when(d[self.j] == 1)
                def _():
                    self.c3l.wait_send()
                    self.c3h.wait_send()

        AX = [XStage(f"A{j}", j, 0, ra1.at[j], ra2.at[j]) for j in (0, 1)]
        def add_ay(dst, src, half):
            add1(dst, src, (LO, HI)[half])

        AY = [YStage(f"Y{j}", j, gs.at[j, x], lo, hi, ry1, ry1.at[pl.ds(0, HI)], ry2, add_ay) for j in (0, 1)]
        order = (xo, xp, xm, x)
        BY = [
            [YStage(f"Z{j}{i}", j, gs.at[j, 4 + q], lo, hi, rz1.at[i], rz1.at[i, pl.ds(0, HI)], rz2.at[i], add_ay)
             for i, q in enumerate(order)]
            for j in (0, 1)
        ]
        BX = [XStage(f"B{j}", j, 4, rb1, rb2) for j in (0, 1)]

        def ax_end(j):
            AX[j].arrive()
            add2(gs.at[j, x], ra2.at[j, 0], ra2.at[j, 1], SLOTS)
            AY[j].start()

        def by_end(j, i):
            def go():
                @pl.when(d[j] == 0)
                def _():
                    BY[j][i].arrive()
                    add2(gs.at[j, 4 + order[i]], rz2.at[i, 0], rz2.at[i, 1], SLOTS)
                    if i < 3:
                        BX[j].start((i,))
            return go

        def bx_middle(j):
            @pl.when(d[j] == 0)
            def _():
                BX[j].middle()

        g_own = local("g", fin.at[k], wg_hbm)
        G = remote("G", fin.at[kk], wg_hbm, "p")

        def finals(j):
            @pl.when(d[j] == 0)
            def _():
                AY[j].arrive()
                sum3(fin.at[0], gs.at[j, x], ry2.at[0], ry2.at[1], tabs[j, 4, x])
                BX[j].arrive()
                sum3(fin.at[1], gs.at[j, 4 + x], rb2.at[0], rb2.at[1], tabs[j, 4, 4 + x])
                G.start()
                g_own.start()

        def o_start(j, *which):
            def go():
                for i in which:
                    if i < 0:
                        o_own[j].start()
                    else:
                        o_sends[j][i].start()
            return go

        def o_hooks(j):
            return {0: [o_start(j, 0, 1)], 1: [o_start(j, 2, 3)], 2: [o_start(j, 4, 5)], 3: [o_start(j, 6, -1)]}

        def o_relay(j):
            O3r[j].wait_recv()
            O5[j].start()
            O4r[j].wait_recv()
            O6[j].start()

        def c_relay(j):
            C3r[j].wait_recv()
            C5[j].start()
            C4r[j].wait_recv()
            C6[j].start()

        def reduce_start(j):
            AX[j].start()
            for i in range(4):
                BY[j][i].start()

        t_own.start()
        for copy in (T0, T1, T2):
            copy.start()
        tab_start()
        for copy in c_sends[0] + c_own:
            copy.start()
        w_first()
        wst[NSLOT] = jnp.zeros((BS, BS), BF16)
        tab_finish()
        w_second()
        w_third()
        T0r.wait_recv()
        T5.start()
        T3.start()
        T1r.wait_recv()
        T6.start()
        T4.start()
        c_relay(0)
        for copy in c_sends[1]:
            copy.start()
        w_relay()
        w_fourth()
        T5r.wait_recv()
        T7.start()
        T6r.wait_recv()
        T8.start()
        t_own.wait()
        for copy in (T2r, T3r, T4r, T7r, T8r):
            copy.wait_recv()
        c_own[0].wait()
        for copy in c_recvs(0):
            copy.wait_recv()
        grads(0, {10: [lambda: c_relay(1)], 12: [lambda: w_load(0)]})
        pick(0)
        reduce_start(0)
        w_ready(0)
        assemble(0)
        hooks = o_hooks(0)
        hooks[1] += [BY[0][0].middle, BY[0][1].middle]
        forward(0, 0, 2, hooks)
        c_own[1].wait()
        for copy in c_recvs(1):
            copy.wait_recv()
        grads(1, {4: [AX[0].middle, BY[0][2].middle], 8: [BY[0][3].middle]})
        pick(1)
        reduce_start(1)
        assemble(0)
        w_load(1)
        hooks = o_hooks(0)
        hooks[2] += [lambda: ax_end(0)]
        hooks[3] += [AX[1].middle, BY[1][0].middle]
        forward(0, 2, 4, hooks)
        w_ready(1)
        assemble(1)
        AY[0].middle()
        o_relay(0)
        for i in range(4):
            by_end(0, i)()
        hooks = o_hooks(1)
        hooks[0] += [BY[1][1].middle]
        hooks[1] += [BY[1][2].middle]
        hooks[2] += [BY[1][3].middle, lambda: bx_middle(0)]
        hooks[3] += [lambda: ax_end(1), by_end(1, 0)]
        forward(1, 0, 4, hooks)
        by_end(1, 1)()
        by_end(1, 2)()
        o_relay(1)
        AY[1].middle()
        bx_middle(1)
        by_end(1, 3)()
        finals(0)
        finals(1)

        for j in (0, 1):
            for copy in o_recvs(j):
                copy.wait_recv()
            o_own[j].wait()

        own_final = (y // 2) == k

        @pl.when(own_final)
        def _():
            g_own.wait()
            G.wait_send()

        @pl.when(jnp.logical_not(own_final))
        def _():
            G.wait_recv()

        for copy in (T0, T1, T2, T3, T4, T5, T6, T7, T8):
            copy.wait_send()
        for j in (0, 1):
            for copy in c_sends[j] + [C5[j], C6[j]] + o_sends[j] + [O5[j], O6[j]] + AX[j].sends():
                copy.wait_send()
            AY[j].wait_sends()
            for i in range(4):
                BY[j][i].wait_sends()

            @pl.when(d[j] == 0)
            def _(j=j):
                for copy in [W0[j], W1[j], U0[j], U1[j]] + V[j] + BX[j].sends():
                    copy.wait_send()

            @pl.when(d[j] == 1)
            def _(j=j):
                W2[j].wait_send()
                U2[j].wait_send()

            @pl.when(d[j] == 3)
            def _(j=j):
                W3[j].wait_send()
                U3[j].wait_send()

            @pl.when(d[j] != 0)
            def _(j=j):
                for copy in (W4[j], W5[j], W6[j], W7[j]):
                    copy.wait_send()

    return kernel


def tables(slot_ids, live, counts):
    numbers = jnp.arange(ROWS * 8, dtype=jnp.int32)
    block = jnp.where(numbers % 8 < COLS, (numbers // 8) * COLS + numbers % 8, -1)
    match = ((slot_ids[:, None] == block[None, :]) & live[:, None]).astype(jnp.int32)
    index = jnp.sum(match * (jnp.arange(NSLOT, dtype=jnp.int32)[:, None] - NSLOT), axis=0) + NSLOT
    pad = ((0, 0), (0, 32 - SLOTS))
    ids = slot_ids.reshape(OWN, SLOTS)
    ids = jnp.pad(ids, pad).reshape(2, 128)
    return jnp.concatenate([index.reshape(2, 128), ids, jnp.pad(counts, ((0, 3), (0, 128 - OWN)))], axis=0)


def shards(tokens, cotangent, master, block_ids, live_count):
    owners, slots = block_ids.shape
    live = jnp.arange(slots, dtype=jnp.int32)[None, :] < live_count
    table = tables(block_ids.reshape(owners * slots), live.reshape(owners * slots), live_count.reshape(1, owners))
    vmem = pltpu.VMEM
    blk = (BS, BS)
    anyspec = pl.BlockSpec(memory_space=pl.ANY)
    outputs, w_grad, _ = pl.pallas_call(
        make_kernel(Names(), Names(), Names()),
        out_shape=(
            jax.ShapeDtypeStruct(cotangent.shape, BF16),
            jax.ShapeDtypeStruct((slots,) + blk, F32),
            jax.ShapeDtypeStruct((2, NSLOT) + blk, BF16),
        ),
        in_specs=[anyspec] * 4,
        out_specs=(anyspec,) * 3,
        scratch_shapes=[
            vmem((8 * TOK, ROWS * BS), BF16),
            vmem((2, 8 * TOK, WID), BF16),
            vmem((2, 2, TOK, WID), BF16),
            vmem((ROWS * COLS,) + blk, BF16),
            vmem((NSLOT + 1,) + blk, BF16),
            vmem((2, 8 * TOK, WID), BF16),
            vmem((2, 2, TOK, WID), BF16),
            vmem((2, OWN, SLOTS) + blk, BF16),
            vmem((2, 2, LO) + blk, BF16),
            vmem((2, 2, SLOTS) + blk, BF16),
            vmem((LO,) + blk, BF16),
            vmem((2, SLOTS) + blk, BF16),
            vmem((4, LO) + blk, BF16),
            vmem((4, 2, SLOTS) + blk, BF16),
            vmem((2, LO) + blk, BF16),
            vmem((2, SLOTS) + blk, BF16),
            vmem((2, SLOTS) + blk, F32),
            vmem((2, 8, 128), jnp.int32),
            pltpu.SMEM((2, 8, 128), jnp.int32),
            pltpu.SemaphoreType.DMA((184,)),
            pltpu.SemaphoreType.DMA((184,)),
            pltpu.SemaphoreType.DMA((16,)),
        ],
        compiler_params=pltpu.CompilerParams(
            collective_id=0, has_side_effects=True, vmem_limit_bytes=66 * 1024 * 1000
        ),
    )(tokens, cotangent, master.reshape(owners * slots, BS, BS), table)
    return finish(outputs, w_grad)


def finish(outputs, w_grad):
    n_o, n_g = 8, 3
    rows, each = outputs.shape[0] // n_o, SLOTS // n_g

    def body(o_ref, g_ref, o_out, g_out, o_v, g_v, in_sem, out_sem):
        loads, stores = [], []
        for i in range(n_o):
            part = pl.ds(i * rows, rows)
            loads.append(pltpu.make_async_copy(o_ref.at[part], o_v.at[part], in_sem.at[i]))
            stores.append(pltpu.make_async_copy(o_v.at[part], o_out.at[part], out_sem.at[i]))
        for i in range(n_g):
            part = pl.ds(i * each, each)
            loads.append(pltpu.make_async_copy(g_ref.at[part], g_v.at[part], in_sem.at[n_o + i]))
            stores.append(pltpu.make_async_copy(g_v.at[part], g_out.at[part], out_sem.at[n_o + i]))
        for load in loads:
            load.start()
        for load, store in zip(loads, stores):
            load.wait()
            store.start()
        for store in stores:
            store.wait()

    anyspec = pl.BlockSpec(memory_space=pl.ANY)
    outputs, w_grad = pl.pallas_call(
        body,
        out_shape=(
            jax.ShapeDtypeStruct(outputs.shape, outputs.dtype),
            jax.ShapeDtypeStruct(w_grad.shape, w_grad.dtype),
        ),
        in_specs=[anyspec] * 2,
        out_specs=(anyspec,) * 2,
        scratch_shapes=[
            pltpu.VMEM(outputs.shape, outputs.dtype),
            pltpu.VMEM(w_grad.shape, w_grad.dtype),
            pltpu.SemaphoreType.DMA((n_o + n_g,)),
            pltpu.SemaphoreType.DMA((n_o + n_g,)),
        ],
    )(outputs, w_grad)
    return outputs, w_grad[None]


def solution(mesh):
    return jax.shard_map(
        shards,
        mesh=mesh,
        in_specs=(
            P(("dp", "seq", "tensor"), None),
            P(("dp", "seq", "tensor"), None),
            P(None, "tensor", None, None),
            P(None, "tensor"),
            P(None, "tensor"),
        ),
        out_specs=(P(("dp", "seq", "tensor"), None), P(("dp", "seq"), "tensor", None, None)),
        check_vma=False,
    )
```

```python
import functools

import jax
import jax.numpy as jnp
from jax import lax
from jax.experimental import pallas as pl
from jax.experimental.pallas import tpu as pltpu
from jax.sharding import PartitionSpec as P

BS = 128
CUT = 512
ROWS = 32
COLS = 7
OWN = 8
SLOTS = 21
NSLOT = OWN * SLOTS
QTR = 28
HALF = QTR // 2
YLO = 4 * QTR
YN = NSLOT - YLO
YH = YN // 2
LO, HI = 11, 10
WID = COLS * BS
TOK = 128
MESH = pl.DeviceIdType.MESH
F32 = jnp.float32
BF16 = jnp.bfloat16


class Names:
    def __init__(self):
        self.n = 0
        self.at = {}

    def get(self, key, width=1):
        if key not in self.at:
            self.at[key] = self.n
            self.n += width
        return self.at[key]


def make_kernel(names_s, names_r, names_l):
    def kernel(
        tok_hbm, cot_hbm, q_hbm, tab_hbm,
        out_hbm, wg_hbm, wc_hbm,
        tok_v, cb, crel, gw, wst, ob, orel, gs, ra1, ra2, ry1, ry2, rz1, rz2, rb1, rb2, fin,
        tabv, tabs, ssem, rsem, lsem,
    ):
        k = lax.axis_index("dp")
        x = lax.axis_index("seq")
        t_me = lax.axis_index("tensor")
        y, z = t_me // 4, t_me % 4
        xp, xm, xo = (x + 1) % 4, (x + 3) % 4, (x + 2) % 4
        yp, ym, yo = (y + 1) % 4, (y + 3) % 4, (y + 2) % 4
        zp, zm, zo = (z + 1) % 4, (z + 3) % 4, (z + 2) % 4
        kk = 1 - k

        def dev(k_=None, x_=None, y_=None, z_=None):
            kd = k if k_ is None else k_
            xd = x if x_ is None else x_
            yd = y if y_ is None else y_
            zd = z if z_ is None else z_
            return (kd, xd, yd * 4 + zd)

        partner = dev(k_=kk)
        devs = {
            "x+": dev(x_=xp), "x-": dev(x_=xm), "y+": dev(y_=yp), "y-": dev(y_=ym), "y2": dev(y_=yo),
            "z+": dev(z_=zp), "z-": dev(z_=zm), "p": partner,
            "z+0": dev(k_=0, z_=zp), "z+1": dev(k_=1, z_=zp), "z-0": dev(k_=0, z_=zm), "z-1": dev(k_=1, z_=zm),
        }

        def remote(key, src, dst, to, skey=None, rkey=None, roff=None, rwidth=1):
            si = names_s.get(skey or key)
            ri = names_r.get(rkey or key, rwidth)
            if roff is not None:
                ri = ri + roff
            assert max(si, names_r.n) < 200
            return pltpu.make_async_remote_copy(
                src_ref=src, dst_ref=dst, send_sem=ssem.at[si], recv_sem=rsem.at[ri],
                device_id=devs[to], device_id_type=MESH,
            )

        def local(key, src, dst):
            assert names_l.get(key) < 20
            return pltpu.make_async_copy(src, dst, lsem.at[names_l.get(key)])

        def slot(z_, k_):
            return pl.ds(pl.multiple_of((z_ * 2 + k_) * TOK, TOK), TOK)

        def part(z_, k_, lo):
            return pl.ds(pl.multiple_of((z_ * 2 + k_) * TOK + lo, 64), 64)

        def cols(group_y, group_z):
            return pl.ds(pl.multiple_of((group_y * 4 + group_z) * WID, 128), WID)

        peers = [partner, devs["x+"], devs["x-"], devs["y+"], devs["y-"], devs["y2"],
                 devs["z+0"], devs["z+1"], devs["z-0"], devs["z-1"]]
        barrier = pltpu.get_barrier_semaphore()
        for peer in peers:
            pl.semaphore_signal(barrier, inc=1, device_id=peer, device_id_type=MESH)
        pl.semaphore_wait(barrier, len(peers))

        d = [(y + 4 - (2 * k + j)) % 4 for j in (0, 1)]
        tok2 = tok_hbm

        t_own = local("t", tok2, tok_v.at[slot(z, k)])
        T0 = remote("T0", tok2, tok_v.at[slot(z, k)], "z+")
        T1 = remote("T1", tok2, tok_v.at[slot(z, k)], "z-")
        T2 = remote("T2", tok2, tok_v.at[slot(z, k)], "p")
        T0r = remote("T0", tok2, tok_v.at[slot(zm, k)], "z+")
        T1r = remote("T1", tok2, tok_v.at[slot(zp, k)], "z-")
        T2r = remote("T2", tok2, tok_v.at[slot(z, kk)], "p")
        T3 = remote("T3", tok_v.at[slot(zm, k)], tok_v.at[slot(zm, k)], "p")
        T4 = remote("T4", tok_v.at[slot(zp, k)], tok_v.at[slot(zp, k)], "p")
        T3r = remote("T3", tok_v.at[slot(zm, kk)], tok_v.at[slot(zm, kk)], "p")
        T4r = remote("T4", tok_v.at[slot(zp, kk)], tok_v.at[slot(zp, kk)], "p")
        T5 = remote("T5", tok_v.at[part(zm, k, 0)], tok_v.at[part(zm, k, 0)], "z+")
        T6 = remote("T6", tok_v.at[part(zp, k, 64)], tok_v.at[part(zp, k, 64)], "z-")
        T5r = remote("T5", tok_v.at[part(zo, k, 0)], tok_v.at[part(zo, k, 0)], "z+")
        T6r = remote("T6", tok_v.at[part(zo, k, 64)], tok_v.at[part(zo, k, 64)], "z-")
        T7 = remote("T7", tok_v.at[part(zo, k, 0)], tok_v.at[part(zo, k, 0)], "p")
        T8 = remote("T8", tok_v.at[part(zo, k, 64)], tok_v.at[part(zo, k, 64)], "p")
        T7r = remote("T7", tok_v.at[part(zo, kk, 0)], tok_v.at[part(zo, kk, 0)], "p")
        T8r = remote("T8", tok_v.at[part(zo, kk, 64)], tok_v.at[part(zo, kk, 64)], "p")

        PARTS = ((0, 0, WID), (1, 0, CUT), (1, CUT, WID - CUT))

        def cot(p, group_k, group_z):
            j, c0, n = PARTS[p]
            first = ((group_k * 2 + j) * 4 + group_z) * WID + c0
            return cot_hbm.at[:, pl.ds(pl.multiple_of(first, 128), n)]

        def cbuf(p, z_, k_):
            j, c0, n = PARTS[p]
            return cb.at[j, slot(z_, k_), pl.ds(c0, n)]

        def crelay(p, way):
            j, c0, n = PARTS[p]
            return crel.at[way, j, :, pl.ds(c0, n)]

        PS = (0, 1, 2)
        c_own = [local(f"c{p}", cot(p, k, z), cbuf(p, z, k)) for p in PS]
        c_sends = []
        for p in PS:
            row = [remote(f"C3{p}", cot(p, 0, zo), crelay(p, 0), "z+"), remote(f"C4{p}", cot(p, 1, zo), crelay(p, 1), "z-")]
            for k_ in (0, 1):
                row.append(remote(f"C1{p}{k_}", cot(p, k_, zp), cbuf(p, z, k), f"z+{k_}", rkey=f"C1r{p}", roff=k, rwidth=2))
                row.append(remote(f"C2{p}{k_}", cot(p, k_, zm), cbuf(p, z, k), f"z-{k_}", rkey=f"C2r{p}", roff=k, rwidth=2))
            row.append(remote(f"C0{p}", cot(p, kk, z), cbuf(p, z, k), "p"))
            c_sends.append(row)
        C3r = [remote(f"C3{p}", cot(p, 0, zo), crelay(p, 0), "z+") for p in PS]
        C4r = [remote(f"C4{p}", cot(p, 1, zo), crelay(p, 1), "z-") for p in PS]
        C5 = [remote(f"C5{p}", crelay(p, 0), cbuf(p, zm, k), "z+0", rkey=f"C5r{p}", roff=k, rwidth=2) for p in PS]
        C6 = [remote(f"C6{p}", crelay(p, 1), cbuf(p, zp, k), "z-1", rkey=f"C5r{p}", roff=k, rwidth=2) for p in PS]

        def c_arrive(p):
            src = cot(p, 0, z)
            out = [remote(f"C0{p}", src, cbuf(p, z, kk), "p")]
            for i in (0, 1):
                out.append(remote(f"C1{p}0", src, cbuf(p, zm, i), "z+", rkey=f"C1r{p}", roff=i, rwidth=2))
                out.append(remote(f"C2{p}0", src, cbuf(p, zp, i), "z-", rkey=f"C2r{p}", roff=i, rwidth=2))
                out.append(remote(f"C5{p}", src, cbuf(p, zo, i), "z+", rkey=f"C5r{p}", roff=i, rwidth=2))
            c_own[p].wait()
            for copy in out:
                copy.wait_recv()

        def wq(j, q):
            return wc_hbm.at[j, pl.ds(q * QTR, QTR)]

        def wlo(j, q):
            return wc_hbm.at[j, pl.ds(q * QTR, HALF)]

        def whi(j, q):
            return wc_hbm.at[j, pl.ds(q * QTR + HALF, HALF)]

        def wu(j, lo=0, n=YN):
            return wc_hbm.at[j, pl.ds(YLO + lo, n)]

        JS = (0, 1)
        W0 = [remote(f"W0{j}", wq(j, x), wq(j, x), "y+") for j in JS]
        W1 = [remote(f"W1{j}", wq(j, x), wq(j, x), "y-") for j in JS]
        W2 = [remote(f"W2{j}", wlo(j, x), wlo(j, x), "y+") for j in JS]
        W3 = [remote(f"W3{j}", whi(j, x), whi(j, x), "y-") for j in JS]
        W4 = [remote(f"W4{j}", wq(j, x), wq(j, x), "x+") for j in JS]
        W5 = [remote(f"W5{j}", wq(j, x), wq(j, x), "x-") for j in JS]
        W4r = [remote(f"W4{j}", wq(j, xm), wq(j, xm), "x+") for j in JS]
        W5r = [remote(f"W5{j}", wq(j, xp), wq(j, xp), "x-") for j in JS]
        W6 = [remote(f"W6{j}", wlo(j, xm), wlo(j, xm), "x+") for j in JS]
        W7 = [remote(f"W7{j}", whi(j, xp), whi(j, xp), "x-") for j in JS]
        W6r = [remote(f"W6{j}", wlo(j, xo), wlo(j, xo), "x+") for j in JS]
        W7r = [remote(f"W7{j}", whi(j, xo), whi(j, xo), "x-") for j in JS]
        U0 = [remote(f"WU0{j}", wu(j), wu(j), "y+") for j in JS]
        U1 = [remote(f"WU1{j}", wu(j), wu(j), "y-") for j in JS]
        U2 = [remote(f"WU2{j}", wu(j, 0, YH), wu(j, 0, YH), "y+") for j in JS]
        U3 = [remote(f"WU3{j}", wu(j, YH, YH), wu(j, YH, YH), "y-") for j in JS]
        V = [[remote(f"V{j}{i}", tab_hbm, tabv.at[j], to) for i, to in enumerate(("y+", "y-", "y2"))] for j in (0, 1)]

        def tab_start():
            for j in (0, 1):
                @pl.when(d[j] == 0)
                def _(j=j):
                    for copy in V[j]:
                        copy.start()
                    local(f"v{j}", tab_hbm, tabv.at[j]).start()

        def tab_finish():
            for j in (0, 1):
                @pl.when(d[j] == 0)
                def _(j=j):
                    local(f"v{j}", tab_hbm, tabv.at[j]).wait()

                for i, dist in enumerate((1, 3, 2)):
                    @pl.when(d[j] == dist)
                    def _(j=j, i=i):
                        V[j][i].wait_recv()
            cp = local("tab", tabv, tabs)
            cp.start()
            cp.wait()

        def quantize(j, start, n):
            @pl.loop(0, n // 4)
            def _(i):
                rows = pl.ds(start + i * 4, 4)
                wide = wst[rows].astype(F32)
                peak = jnp.max(jnp.abs(wide), axis=(1, 2), keepdims=True) + 1e-06
                levels = jnp.floor(wide * (7.0 / peak) + 0.5)
                wst[rows] = (levels * (peak / 7.0)).astype(BF16)

            cp = local("qw", wst.at[pl.ds(start, n)], wc_hbm.at[j, pl.ds(start, n)])
            cp.start()
            cp.wait()

        def w_first():
            for j in (0, 1):
                @pl.when(d[j] == 0)
                def _(j=j):
                    cp = local("q", q_hbm, wst.at[pl.ds(0, NSLOT)])
                    cp.start()
                    cp.wait()
                    quantize(j, x * QTR, QTR)
                    W0[j].start()
                    W1[j].start()
                    quantize(j, YLO, YN)
                    U0[j].start()
                    U1[j].start()
                    for q in (xp, xo, xm):
                        quantize(j, q * QTR, QTR)

        def w_second():
            for j in (0, 1):
                @pl.when(d[j] == 1)
                def _(j=j):
                    W0[j].wait_recv()
                    W2[j].start()
                    W4[j].start()
                    W5[j].start()

                @pl.when(d[j] == 3)
                def _(j=j):
                    W1[j].wait_recv()
                    W3[j].start()
                    W4[j].start()
                    W5[j].start()

        def w_third():
            for j in (0, 1):
                @pl.when(d[j] == 2)
                def _(j=j):
                    W2[j].wait_recv()
                    W3[j].wait_recv()
                    W4[j].start()
                    W5[j].start()

        def w_relay():
            for j in (0, 1):
                @pl.when(d[j] == 1)
                def _(j=j):
                    U0[j].wait_recv()
                    U2[j].start()

                @pl.when(d[j] == 3)
                def _(j=j):
                    U1[j].wait_recv()
                    U3[j].start()

        def w_fourth():
            for j in (0, 1):
                @pl.when(d[j] != 0)
                def _(j=j):
                    W4r[j].wait_recv()
                    W6[j].start()
                    W5r[j].wait_recv()
                    W7[j].start()

        def w_load(j):
            @pl.when(d[j] != 0)
            def _():
                W6r[j].wait_recv()
                W7r[j].wait_recv()

            @pl.when(d[j] == 2)
            def _():
                U2[j].wait_recv()
                U3[j].wait_recv()

            local("w", wc_hbm.at[j], wst.at[pl.ds(0, NSLOT)]).start()

        def w_ready(j):
            local("w", wc_hbm.at[j], wst.at[pl.ds(0, NSLOT)]).wait()

        def grads(p, hooks):
            j, c0, n = PARTS[p]

            @pl.loop(0, 16)
            def _(r):
                rows = pl.ds(pl.multiple_of(r * 256, 256), 256)
                g = lax.dot_general(
                    tok_v[:, rows], cb[j, :, c0:c0 + n], (((0,), (0,)), ((), ())), preferred_element_type=F32
                )
                g = g.astype(BF16)
                for h in (0, 1):
                    for c in range(n // BS):
                        gw[(r * 2 + h) * COLS + c0 // BS + c] = g[h * BS:(h + 1) * BS, c * BS:(c + 1) * BS]
                for at, steps in hooks.items():
                    @pl.when(r == at)
                    def _(steps=steps):
                        for step in steps:
                            step()

        def pick(j):
            for o in range(OWN):
                @pl.loop(0, SLOTS)
                def _(s, o=o):
                    gs[j, o, s] = gw[tabs[j, 2 + o // 4, (o % 4) * 32 + s]]

        def assemble(j):
            @pl.loop(0, ROWS)
            def _(r):
                for c in range(COLS):
                    gw[r * COLS + c] = wst[tabs[j, r // 16, (r % 16) * 8 + c]]

        def forward(j, lo_m, hi_m, hooks):
            @pl.loop(lo_m, hi_m)
            def _(m):
                zz = (z + jnp.where(m == 0, 2, jnp.where(m == 1, 1, jnp.where(m == 2, 3, 0)))) % 4
                rows = pl.ds(pl.multiple_of(zz * 256, 256), 256)
                w = jnp.concatenate(
                    [jnp.concatenate([gw[r * COLS + c] for c in range(COLS)], axis=1) for r in range(ROWS)], axis=0
                )
                o = jnp.dot(tok_v[rows, :], w, preferred_element_type=F32)
                ob[j, rows, :] = o.astype(BF16)
                for at, steps in hooks.items():
                    @pl.when(m == at)
                    def _(steps=steps):
                        for step in steps:
                            step()

        o_own = [local(f"o{j}", ob.at[j, slot(z, k)], out_hbm.at[:, cols(2 * k + j, z)]) for j in (0, 1)]
        o_sends = []
        for j in (0, 1):
            dst = out_hbm.at[:, cols(2 * k + j, z)]
            row = []
            row.append(remote(f"O3{j}", ob.at[j, slot(zo, 0)], orel.at[0, j], "z+"))
            row.append(remote(f"O4{j}", ob.at[j, slot(zo, 1)], orel.at[1, j], "z-"))
            for i in (0, 1):
                row.append(remote(f"O1{j}{i}", ob.at[j, slot(zp, i)], dst, f"z+{i}", rkey=f"O1r{j}", roff=k, rwidth=2))
            for i in (0, 1):
                row.append(remote(f"O2{j}{i}", ob.at[j, slot(zm, i)], dst, f"z-{i}", rkey=f"O2r{j}", roff=k, rwidth=2))
            row.append(remote(f"O0{j}", ob.at[j, slot(z, kk)], dst, "p"))
            o_sends.append(row)
        O3r = [remote(f"O3{j}", orel.at[0, j], orel.at[0, j], "z+") for j in (0, 1)]
        O4r = [remote(f"O4{j}", orel.at[1, j], orel.at[1, j], "z-") for j in (0, 1)]
        O5 = [remote(f"O5{j}", orel.at[0, j], out_hbm.at[:, cols(2 * k + j, zm)], "z+0", rkey=f"O5r{j}", roff=k, rwidth=2) for j in (0, 1)]
        O6 = [remote(f"O6{j}", orel.at[1, j], out_hbm.at[:, cols(2 * k + j, zp)], "z-1", rkey=f"O5r{j}", roff=k, rwidth=2) for j in (0, 1)]

        def o_recvs(j):
            src = ob.at[j, slot(z, 0)]
            out = [remote(f"O0{j}", src, out_hbm.at[:, cols(2 * kk + j, z)], "p")]
            for i in (0, 1):
                out.append(remote(f"O1{j}0", src, out_hbm.at[:, cols(2 * i + j, zm)], "z+", rkey=f"O1r{j}", roff=i, rwidth=2))
                out.append(remote(f"O2{j}0", src, out_hbm.at[:, cols(2 * i + j, zp)], "z-", rkey=f"O2r{j}", roff=i, rwidth=2))
                out.append(remote(f"O5{j}", src, out_hbm.at[:, cols(2 * i + j, zo)], "z+", rkey=f"O5r{j}", roff=i, rwidth=2))
            return out

        def add1(dst, src, n):
            @pl.loop(0, n)
            def _(i):
                dst[i] = (dst[i].astype(F32) + src[i].astype(F32)).astype(BF16)

        def add2(dst, a, b, n):
            @pl.loop(0, n)
            def _(i):
                dst[i] = (dst[i].astype(F32) + a[i].astype(F32) + b[i].astype(F32)).astype(BF16)

        def sum3(out, dst, a, b, count):
            @pl.loop(0, SLOTS)
            def _(i):
                live = jnp.minimum(jnp.maximum(count - i, 0), 1).astype(F32)
                out[i] = (dst[i].astype(F32) + a[i].astype(F32) + b[i].astype(F32)) * live

        lo, hi = pl.ds(0, LO), pl.ds(LO, HI)

        class XStage:
            def __init__(self, name, j, base, first, second):
                self.j, self.base = j, base
                self.first = first
                self.c0 = remote(f"{name}0", gs.at[j, base + xo, lo], first.at[0], "x+")
                self.c1 = remote(f"{name}1", gs.at[j, base + xo, hi], first.at[1, pl.ds(0, HI)], "x-")
                self.c2l = remote(f"{name}2l", gs.at[j, base + xp, lo], second.at[0, lo], "x+")
                self.c2h = remote(f"{name}2h", gs.at[j, base + xp, hi], second.at[0, hi], "x+")
                self.c3l = remote(f"{name}3l", gs.at[j, base + xm, lo], second.at[1, lo], "x-")
                self.c3h = remote(f"{name}3h", gs.at[j, base + xm, hi], second.at[1, hi], "x-")

            def start(self, which=(0, 1, 2)):
                for i in which:
                    for copy in ((self.c0, self.c1), (self.c2h,), (self.c3l,))[i]:
                        copy.start()

            def middle(self):
                self.c0.wait_recv()
                add1(gs.at[self.j, self.base + xp, lo], self.first.at[0], LO)
                self.c2l.start()
                self.c1.wait_recv()
                add1(gs.at[self.j, self.base + xm, hi], self.first.at[1], HI)
                self.c3h.start()

            def arrive(self):
                for copy in (self.c2h, self.c3l, self.c2l, self.c3h):
                    copy.wait_recv()

            def sends(self):
                return [self.c0, self.c1, self.c2l, self.c2h, self.c3l, self.c3h]

        class YStage:
            def __init__(self, name, j, src, low, high, relay, high_relay, second, add):
                self.j, self.add, self.relay = j, add, relay
                self.low, self.high = src.at[low], src.at[high]
                self.c0 = remote(f"{name}0", self.low, relay, "y+")
                self.c1 = remote(f"{name}1", self.high, high_relay, "y-")
                self.c2l = remote(f"{name}2l", self.low, second.at[0].at[low], "y+")
                self.c2h = remote(f"{name}2h", self.high, second.at[0].at[high], "y+")
                self.c3l = remote(f"{name}3l", self.low, second.at[1].at[low], "y-")
                self.c3h = remote(f"{name}3h", self.high, second.at[1].at[high], "y-")

            def start(self):
                @pl.when(d[self.j] == 2)
                def _():
                    self.c0.start()
                    self.c1.start()

                @pl.when(d[self.j] == 3)
                def _():
                    self.c2h.start()

                @pl.when(d[self.j] == 1)
                def _():
                    self.c3l.start()

            def middle(self):
                @pl.when(d[self.j] == 3)
                def _():
                    self.c0.wait_recv()
                    self.add(self.low, self.relay, 0)
                    self.c2l.start()

                @pl.when(d[self.j] == 1)
                def _():
                    self.c1.wait_recv()
                    self.add(self.high, self.relay, 1)
                    self.c3h.start()

            def arrive(self):
                for copy in (self.c2h, self.c3l, self.c2l, self.c3h):
                    copy.wait_recv()

            def wait_sends(self):
                @pl.when(d[self.j] == 2)
                def _():
                    self.c0.wait_send()
                    self.c1.wait_send()

                @pl.when(d[self.j] == 3)
                def _():
                    self.c2h.wait_send()
                    self.c2l.wait_send()

                @pl.when(d[self.j] == 1)
                def _():
                    self.c3l.wait_send()
                    self.c3h.wait_send()

        AX = [XStage(f"A{j}", j, 0, ra1.at[j], ra2.at[j]) for j in (0, 1)]
        def add_ay(dst, src, half):
            add1(dst, src, (LO, HI)[half])

        AY = [YStage(f"Y{j}", j, gs.at[j, x], lo, hi, ry1, ry1.at[pl.ds(0, HI)], ry2, add_ay) for j in (0, 1)]
        order = (xo, xp, xm, x)
        BY = [
            [YStage(f"Z{j}{i}", j, gs.at[j, 4 + q], lo, hi, rz1.at[i], rz1.at[i, pl.ds(0, HI)], rz2.at[i], add_ay)
             for i, q in enumerate(order)]
            for j in (0, 1)
        ]
        BX = [XStage(f"B{j}", j, 4, rb1, rb2) for j in (0, 1)]

        def ax_end(j):
            AX[j].arrive()
            add2(gs.at[j, x], ra2.at[j, 0], ra2.at[j, 1], SLOTS)
            AY[j].start()

        def by_end(j, i):
            def go():
                @pl.when(d[j] == 0)
                def _():
                    BY[j][i].arrive()
                    add2(gs.at[j, 4 + order[i]], rz2.at[i, 0], rz2.at[i, 1], SLOTS)
                    if i < 3:
                        BX[j].start((i,))
            return go

        def bx_middle(j):
            @pl.when(d[j] == 0)
            def _():
                BX[j].middle()

        g_own = local("g", fin.at[k], wg_hbm)
        G = remote("G", fin.at[kk], wg_hbm, "p")

        def finals(j):
            @pl.when(d[j] == 0)
            def _():
                AY[j].arrive()
                sum3(fin.at[0], gs.at[j, x], ry2.at[0], ry2.at[1], tabs[j, 4, x])
                BX[j].arrive()
                sum3(fin.at[1], gs.at[j, 4 + x], rb2.at[0], rb2.at[1], tabs[j, 4, 4 + x])
                G.start()
                g_own.start()

        def o_start(j, *which):
            def go():
                for i in which:
                    if i < 0:
                        o_own[j].start()
                    else:
                        o_sends[j][i].start()
            return go

        def o_hooks(j):
            return {0: [o_start(j, 0, 1)], 1: [o_start(j, 2, 3)], 2: [o_start(j, 4, 5)], 3: [o_start(j, 6, -1)]}

        def o_relay(j):
            O3r[j].wait_recv()
            O5[j].start()
            O4r[j].wait_recv()
            O6[j].start()

        def c_relay(j):
            C3r[j].wait_recv()
            C5[j].start()
            C4r[j].wait_recv()
            C6[j].start()

        def reduce_start(j):
            AX[j].start()
            for i in range(4):
                BY[j][i].start()

        t_own.start()
        for copy in (T0, T1, T2):
            copy.start()
        tab_start()
        for copy in c_sends[0] + c_own:
            copy.start()
        w_first()
        wst[NSLOT] = jnp.zeros((BS, BS), BF16)
        tab_finish()
        w_second()
        w_third()
        T0r.wait_recv()
        T5.start()
        T3.start()
        T1r.wait_recv()
        T6.start()
        T4.start()
        c_relay(0)
        for copy in c_sends[1] + c_sends[2]:
            copy.start()
        w_relay()
        w_fourth()
        T5r.wait_recv()
        T7.start()
        T6r.wait_recv()
        T8.start()
        t_own.wait()
        for copy in (T2r, T3r, T4r, T7r, T8r):
            copy.wait_recv()
        c_arrive(0)
        grads(0, {4: [lambda: c_relay(1)], 10: [lambda: c_relay(2)], 13: [lambda: w_load(0)]})
        pick(0)
        reduce_start(0)
        c_arrive(1)
        grads(1, {4: [BY[0][0].middle, BY[0][1].middle], 12: [AX[0].middle, BY[0][2].middle]})
        c_arrive(2)
        grads(2, {0: [BY[0][3].middle]})
        pick(1)
        reduce_start(1)
        w_ready(0)
        assemble(0)
        w_load(1)
        hooks = o_hooks(0)
        hooks[1] += [lambda: ax_end(0)]
        hooks[2] += [AX[1].middle]
        hooks[3] += [BY[1][0].middle]
        forward(0, 0, 4, hooks)
        w_ready(1)
        assemble(1)
        AY[0].middle()
        o_relay(0)
        for i in range(4):
            by_end(0, i)()
        hooks = o_hooks(1)
        hooks[0] += [BY[1][1].middle]
        hooks[1] += [BY[1][2].middle]
        hooks[2] += [BY[1][3].middle, lambda: bx_middle(0)]
        hooks[3] += [lambda: ax_end(1), by_end(1, 0)]
        forward(1, 0, 4, hooks)
        by_end(1, 1)()
        by_end(1, 2)()
        o_relay(1)
        AY[1].middle()
        bx_middle(1)
        by_end(1, 3)()
        finals(0)
        finals(1)

        for j in (0, 1):
            for copy in o_recvs(j):
                copy.wait_recv()
            o_own[j].wait()

        own_final = (y // 2) == k

        @pl.when(own_final)
        def _():
            g_own.wait()
            G.wait_send()

        @pl.when(jnp.logical_not(own_final))
        def _():
            G.wait_recv()

        for copy in [T0, T1, T2, T3, T4, T5, T6, T7, T8] + c_sends[0] + c_sends[1] + c_sends[2] + C5 + C6:
            copy.wait_send()
        for j in (0, 1):
            for copy in o_sends[j] + [O5[j], O6[j]] + AX[j].sends():
                copy.wait_send()
            AY[j].wait_sends()
            for i in range(4):
                BY[j][i].wait_sends()

            @pl.when(d[j] == 0)
            def _(j=j):
                for copy in [W0[j], W1[j], U0[j], U1[j]] + V[j] + BX[j].sends():
                    copy.wait_send()

            @pl.when(d[j] == 1)
            def _(j=j):
                W2[j].wait_send()
                U2[j].wait_send()

            @pl.when(d[j] == 3)
            def _(j=j):
                W3[j].wait_send()
                U3[j].wait_send()

            @pl.when(d[j] != 0)
            def _(j=j):
                for copy in (W4[j], W5[j], W6[j], W7[j]):
                    copy.wait_send()

    return kernel


def tables(slot_ids, live, counts):
    numbers = jnp.arange(ROWS * 8, dtype=jnp.int32)
    block = jnp.where(numbers % 8 < COLS, (numbers // 8) * COLS + numbers % 8, -1)
    match = ((slot_ids[:, None] == block[None, :]) & live[:, None]).astype(jnp.int32)
    index = jnp.sum(match * (jnp.arange(NSLOT, dtype=jnp.int32)[:, None] - NSLOT), axis=0) + NSLOT
    pad = ((0, 0), (0, 32 - SLOTS))
    ids = slot_ids.reshape(OWN, SLOTS)
    ids = jnp.pad(ids, pad).reshape(2, 128)
    return jnp.concatenate([index.reshape(2, 128), ids, jnp.pad(counts, ((0, 3), (0, 128 - OWN)))], axis=0)


def shards(tokens, cotangent, master, block_ids, live_count):
    owners, slots = block_ids.shape
    live = jnp.arange(slots, dtype=jnp.int32)[None, :] < live_count
    table = tables(block_ids.reshape(owners * slots), live.reshape(owners * slots), live_count.reshape(1, owners))
    vmem = pltpu.VMEM
    blk = (BS, BS)
    anyspec = pl.BlockSpec(memory_space=pl.ANY)
    outputs, w_grad, _ = pl.pallas_call(
        make_kernel(Names(), Names(), Names()),
        out_shape=(
            jax.ShapeDtypeStruct(cotangent.shape, BF16),
            jax.ShapeDtypeStruct((slots,) + blk, F32),
            jax.ShapeDtypeStruct((2, NSLOT) + blk, BF16),
        ),
        in_specs=[anyspec] * 4,
        out_specs=(anyspec,) * 3,
        scratch_shapes=[
            vmem((8 * TOK, ROWS * BS), BF16),
            vmem((2, 8 * TOK, WID), BF16),
            vmem((2, 2, TOK, WID), BF16),
            vmem((ROWS * COLS,) + blk, BF16),
            vmem((NSLOT + 1,) + blk, BF16),
            vmem((2, 8 * TOK, WID), BF16),
            vmem((2, 2, TOK, WID), BF16),
            vmem((2, OWN, SLOTS) + blk, BF16),
            vmem((2, 2, LO) + blk, BF16),
            vmem((2, 2, SLOTS) + blk, BF16),
            vmem((LO,) + blk, BF16),
            vmem((2, SLOTS) + blk, BF16),
            vmem((4, LO) + blk, BF16),
            vmem((4, 2, SLOTS) + blk, BF16),
            vmem((2, LO) + blk, BF16),
            vmem((2, SLOTS) + blk, BF16),
            vmem((2, SLOTS) + blk, F32),
            vmem((2, 8, 128), jnp.int32),
            pltpu.SMEM((2, 8, 128), jnp.int32),
            pltpu.SemaphoreType.DMA((200,)),
            pltpu.SemaphoreType.DMA((200,)),
            pltpu.SemaphoreType.DMA((20,)),
        ],
        compiler_params=pltpu.CompilerParams(
            collective_id=0, has_side_effects=True, vmem_limit_bytes=66 * 1024 * 1000
        ),
    )(tokens, cotangent, master.reshape(owners * slots, BS, BS), table)
    return finish(outputs, w_grad)


def finish(outputs, w_grad):
    n_o, n_g = 8, 3
    rows, each = outputs.shape[0] // n_o, SLOTS // n_g

    def body(o_ref, g_ref, o_out, g_out, o_v, g_v, in_sem, out_sem):
        loads, stores = [], []
        for i in range(n_o):
            part = pl.ds(i * rows, rows)
            loads.append(pltpu.make_async_copy(o_ref.at[part], o_v.at[part], in_sem.at[i]))
            stores.append(pltpu.make_async_copy(o_v.at[part], o_out.at[part], out_sem.at[i]))
        for i in range(n_g):
            part = pl.ds(i * each, each)
            loads.append(pltpu.make_async_copy(g_ref.at[part], g_v.at[part], in_sem.at[n_o + i]))
            stores.append(pltpu.make_async_copy(g_v.at[part], g_out.at[part], out_sem.at[n_o + i]))
        for load in loads:
            load.start()
        for load, store in zip(loads, stores):
            load.wait()
            store.start()
        for store in stores:
            store.wait()

    anyspec = pl.BlockSpec(memory_space=pl.ANY)
    outputs, w_grad = pl.pallas_call(
        body,
        out_shape=(
            jax.ShapeDtypeStruct(outputs.shape, outputs.dtype),
            jax.ShapeDtypeStruct(w_grad.shape, w_grad.dtype),
        ),
        in_specs=[anyspec] * 2,
        out_specs=(anyspec,) * 2,
        scratch_shapes=[
            pltpu.VMEM(outputs.shape, outputs.dtype),
            pltpu.VMEM(w_grad.shape, w_grad.dtype),
            pltpu.SemaphoreType.DMA((n_o + n_g,)),
            pltpu.SemaphoreType.DMA((n_o + n_g,)),
        ],
    )(outputs, w_grad)
    return outputs, w_grad[None]


def solution(mesh):
    return jax.shard_map(
        shards,
        mesh=mesh,
        in_specs=(
            P(("dp", "seq", "tensor"), None),
            P(("dp", "seq", "tensor"), None),
            P(None, "tensor", None, None),
            P(None, "tensor"),
            P(None, "tensor"),
        ),
        out_specs=(P(("dp", "seq", "tensor"), None), P(("dp", "seq"), "tensor", None, None)),
        check_vma=False,
    )
```

```python
import functools

import jax
import jax.numpy as jnp
from jax import lax
from jax.experimental import pallas as pl
from jax.experimental.pallas import tpu as pltpu
from jax.sharding import PartitionSpec as P

BS = 128
ROWS = 32
COLS = 7
OWN = 8
SLOTS = 21
NSLOT = OWN * SLOTS
QTR = 28
HALF = QTR // 2
YLO = 4 * QTR
YN = NSLOT - YLO
YH = YN // 2
LO, HI = 11, 10
WID = COLS * BS
TOK = 128
MESH = pl.DeviceIdType.MESH
F32 = jnp.float32
BF16 = jnp.bfloat16


class Names:
    def __init__(self):
        self.n = 0
        self.at = {}

    def get(self, key, width=1):
        if key not in self.at:
            self.at[key] = self.n
            self.n += width
        return self.at[key]


def make_kernel(names_s, names_r, names_l):
    def kernel(
        tok_hbm, cot_hbm, q_hbm, tab_hbm,
        out_hbm, wg_hbm, wc_hbm,
        tok_v, cb, crel, gw, wst, ob, orel, gs, ra1, ra2, ry1, ry2, rz1, rz2, rb1, rb2, fin,
        tabv, tabs, invv, invs, ssem, rsem, lsem,
    ):
        k = lax.axis_index("dp")
        x = lax.axis_index("seq")
        t_me = lax.axis_index("tensor")
        y, z = t_me // 4, t_me % 4
        xp, xm, xo = (x + 1) % 4, (x + 3) % 4, (x + 2) % 4
        yp, ym, yo = (y + 1) % 4, (y + 3) % 4, (y + 2) % 4
        zp, zm, zo = (z + 1) % 4, (z + 3) % 4, (z + 2) % 4
        kk = 1 - k

        def dev(k_=None, x_=None, y_=None, z_=None):
            kd = k if k_ is None else k_
            xd = x if x_ is None else x_
            yd = y if y_ is None else y_
            zd = z if z_ is None else z_
            return (kd, xd, yd * 4 + zd)

        partner = dev(k_=kk)
        devs = {
            "x+": dev(x_=xp), "x-": dev(x_=xm), "y+": dev(y_=yp), "y-": dev(y_=ym), "y2": dev(y_=yo),
            "z+": dev(z_=zp), "z-": dev(z_=zm), "p": partner,
            "z+0": dev(k_=0, z_=zp), "z+1": dev(k_=1, z_=zp), "z-0": dev(k_=0, z_=zm), "z-1": dev(k_=1, z_=zm),
        }

        def remote(key, src, dst, to, skey=None, rkey=None, roff=None, rwidth=1):
            si = names_s.get(skey or key)
            ri = names_r.get(rkey or key, rwidth)
            if roff is not None:
                ri = ri + roff
            assert max(si, names_r.n) < 184
            return pltpu.make_async_remote_copy(
                src_ref=src, dst_ref=dst, send_sem=ssem.at[si], recv_sem=rsem.at[ri],
                device_id=devs[to], device_id_type=MESH,
            )

        def local(key, src, dst):
            return pltpu.make_async_copy(src, dst, lsem.at[names_l.get(key)])

        def slot(z_, k_):
            return pl.ds(pl.multiple_of((z_ * 2 + k_) * TOK, TOK), TOK)

        def part(z_, k_, lo):
            return pl.ds(pl.multiple_of((z_ * 2 + k_) * TOK + lo, 64), 64)

        def cols(group_y, group_z):
            return pl.ds(pl.multiple_of((group_y * 4 + group_z) * WID, 128), WID)

        peers = [partner, devs["x+"], devs["x-"], devs["y+"], devs["y-"], devs["y2"],
                 devs["z+0"], devs["z+1"], devs["z-0"], devs["z-1"]]
        barrier = pltpu.get_barrier_semaphore()
        for peer in peers:
            pl.semaphore_signal(barrier, inc=1, device_id=peer, device_id_type=MESH)
        pl.semaphore_wait(barrier, len(peers))

        d = [(y + 4 - (2 * k + j)) % 4 for j in (0, 1)]
        tok2 = tok_hbm

        t_own = local("t", tok2, tok_v.at[slot(z, k)])
        T0 = remote("T0", tok2, tok_v.at[slot(z, k)], "z+")
        T1 = remote("T1", tok2, tok_v.at[slot(z, k)], "z-")
        T2 = remote("T2", tok2, tok_v.at[slot(z, k)], "p")
        T0r = remote("T0", tok2, tok_v.at[slot(zm, k)], "z+")
        T1r = remote("T1", tok2, tok_v.at[slot(zp, k)], "z-")
        T2r = remote("T2", tok2, tok_v.at[slot(z, kk)], "p")
        T3 = remote("T3", tok_v.at[slot(zm, k)], tok_v.at[slot(zm, k)], "p")
        T4 = remote("T4", tok_v.at[slot(zp, k)], tok_v.at[slot(zp, k)], "p")
        T3r = remote("T3", tok_v.at[slot(zm, kk)], tok_v.at[slot(zm, kk)], "p")
        T4r = remote("T4", tok_v.at[slot(zp, kk)], tok_v.at[slot(zp, kk)], "p")
        T5 = remote("T5", tok_v.at[part(zm, k, 0)], tok_v.at[part(zm, k, 0)], "z+")
        T6 = remote("T6", tok_v.at[part(zp, k, 64)], tok_v.at[part(zp, k, 64)], "z-")
        T5r = remote("T5", tok_v.at[part(zo, k, 0)], tok_v.at[part(zo, k, 0)], "z+")
        T6r = remote("T6", tok_v.at[part(zo, k, 64)], tok_v.at[part(zo, k, 64)], "z-")
        T7 = remote("T7", tok_v.at[part(zo, k, 0)], tok_v.at[part(zo, k, 0)], "p")
        T8 = remote("T8", tok_v.at[part(zo, k, 64)], tok_v.at[part(zo, k, 64)], "p")
        T7r = remote("T7", tok_v.at[part(zo, kk, 0)], tok_v.at[part(zo, kk, 0)], "p")
        T8r = remote("T8", tok_v.at[part(zo, kk, 64)], tok_v.at[part(zo, kk, 64)], "p")

        def cot(group_y, group_z):
            return cot_hbm.at[:, cols(group_y, group_z)]

        c_own = [local(f"c{j}", cot(2 * k + j, z), cb.at[j, slot(z, k)]) for j in (0, 1)]
        c_sends = []
        for j in (0, 1):
            row = []
            row.append(remote(f"C3{j}", cot(j, zo), crel.at[0, j], "z+"))
            row.append(remote(f"C4{j}", cot(2 + j, zo), crel.at[1, j], "z-"))
            for k_ in (0, 1):
                row.append(remote(f"C1{j}{k_}", cot(2 * k_ + j, zp), cb.at[j, slot(z, k)], f"z+{k_}",
                                  rkey=f"C1r{j}", roff=k, rwidth=2))
                row.append(remote(f"C2{j}{k_}", cot(2 * k_ + j, zm), cb.at[j, slot(z, k)], f"z-{k_}",
                                  rkey=f"C2r{j}", roff=k, rwidth=2))
            row.append(remote(f"C0{j}", cot(2 * kk + j, z), cb.at[j, slot(z, k)], "p"))
            c_sends.append(row)
        C3r = [remote(f"C3{j}", cot(j, zo), crel.at[0, j], "z+") for j in (0, 1)]
        C4r = [remote(f"C4{j}", cot(2 + j, zo), crel.at[1, j], "z-") for j in (0, 1)]
        C5 = [remote(f"C5{j}", crel.at[0, j], cb.at[j, slot(zm, k)], "z+0", rkey=f"C5r{j}", roff=k, rwidth=2) for j in (0, 1)]
        C6 = [remote(f"C6{j}", crel.at[1, j], cb.at[j, slot(zp, k)], "z-1", rkey=f"C5r{j}", roff=k, rwidth=2) for j in (0, 1)]

        def c_recvs(j):
            out = [remote(f"C0{j}", cot(j, z), cb.at[j, slot(z, kk)], "p")]
            for i in (0, 1):
                out.append(remote(f"C1{j}0", cot(j, z), cb.at[j, slot(zm, i)], "z+", rkey=f"C1r{j}", roff=i, rwidth=2))
                out.append(remote(f"C2{j}0", cot(j, z), cb.at[j, slot(zp, i)], "z-", rkey=f"C2r{j}", roff=i, rwidth=2))
                out.append(remote(f"C5{j}", cot(j, z), cb.at[j, slot(zo, i)], "z+", rkey=f"C5r{j}", roff=i, rwidth=2))
            return out

        def wq(j, q):
            return wc_hbm.at[j, pl.ds(q * QTR, QTR)]

        def wlo(j, q):
            return wc_hbm.at[j, pl.ds(q * QTR, HALF)]

        def whi(j, q):
            return wc_hbm.at[j, pl.ds(q * QTR + HALF, HALF)]

        def wu(j, lo=0, n=YN):
            return wc_hbm.at[j, pl.ds(YLO + lo, n)]

        JS = (0, 1)
        W0 = [remote(f"W0{j}", wq(j, x), wq(j, x), "y+") for j in JS]
        W1 = [remote(f"W1{j}", wq(j, x), wq(j, x), "y-") for j in JS]
        W2 = [remote(f"W2{j}", wlo(j, x), wlo(j, x), "y+") for j in JS]
        W3 = [remote(f"W3{j}", whi(j, x), whi(j, x), "y-") for j in JS]
        W4 = [remote(f"W4{j}", wq(j, x), wq(j, x), "x+") for j in JS]
        W5 = [remote(f"W5{j}", wq(j, x), wq(j, x), "x-") for j in JS]
        W4r = [remote(f"W4{j}", wq(j, xm), wq(j, xm), "x+") for j in JS]
        W5r = [remote(f"W5{j}", wq(j, xp), wq(j, xp), "x-") for j in JS]
        W6 = [remote(f"W6{j}", wlo(j, xm), wlo(j, xm), "x+") for j in JS]
        W7 = [remote(f"W7{j}", whi(j, xp), whi(j, xp), "x-") for j in JS]
        W6r = [remote(f"W6{j}", wlo(j, xo), wlo(j, xo), "x+") for j in JS]
        W7r = [remote(f"W7{j}", whi(j, xo), whi(j, xo), "x-") for j in JS]
        U0 = [remote(f"WU0{j}", wu(j), wu(j), "y+") for j in JS]
        U1 = [remote(f"WU1{j}", wu(j), wu(j), "y-") for j in JS]
        U2 = [remote(f"WU2{j}", wu(j, 0, YH), wu(j, 0, YH), "y+") for j in JS]
        U3 = [remote(f"WU3{j}", wu(j, YH, YH), wu(j, YH, YH), "y-") for j in JS]
        V = [[remote(f"V{j}{i}", tab_hbm, tabv.at[j], to) for i, to in enumerate(("y+", "y-", "y2"))] for j in (0, 1)]

        def tab_start():
            for j in (0, 1):
                @pl.when(d[j] == 0)
                def _(j=j):
                    for copy in V[j]:
                        copy.start()
                    local(f"v{j}", tab_hbm, tabv.at[j]).start()

        def tab_finish():
            for j in (0, 1):
                @pl.when(d[j] == 0)
                def _(j=j):
                    local(f"v{j}", tab_hbm, tabv.at[j]).wait()

                for i, dist in enumerate((1, 3, 2)):
                    @pl.when(d[j] == dist)
                    def _(j=j, i=i):
                        V[j][i].wait_recv()
            cp = local("tab", tabv, tabs)
            cp.start()
            cp.wait()
            spot = lax.broadcasted_iota(jnp.int32, (8, 128), 0) * 128 + lax.broadcasted_iota(jnp.int32, (8, 128), 1)
            spot = jnp.where((spot & 7) < COLS, (spot >> 3) * COLS + (spot & 7), -1)
            for j in (0, 1):
                def slot_step(s, inv, j=j):
                    for o in range(OWN):
                        named = jnp.where(s < tabs[j, o, SLOTS], tabs[j, o, s], -2)
                        inv = jnp.where(spot == named, o * SLOTS + s, inv)
                    return inv
                invv[j] = lax.fori_loop(0, SLOTS, slot_step, jnp.full((8, 128), NSLOT, jnp.int32))

        def quantize(j, start, n):
            @pl.loop(0, n // 4)
            def _(i):
                rows = pl.ds(start + i * 4, 4)
                wide = wst[rows].astype(F32)
                peak = jnp.max(jnp.abs(wide), axis=(1, 2), keepdims=True) + 1e-06
                levels = jnp.floor(wide * (7.0 / peak) + 0.5)
                wst[rows] = (levels * (peak / 7.0)).astype(BF16)

            cp = local("qw", wst.at[pl.ds(start, n)], wc_hbm.at[j, pl.ds(start, n)])
            cp.start()
            cp.wait()

        def w_first():
            for j in (0, 1):
                @pl.when(d[j] == 0)
                def _(j=j):
                    cp = local("q", q_hbm, wst.at[pl.ds(0, NSLOT)])
                    cp.start()
                    cp.wait()
                    quantize(j, x * QTR, QTR)
                    W0[j].start()
                    W1[j].start()
                    quantize(j, YLO, YN)
                    U0[j].start()
                    U1[j].start()
                    for q in (xp, xo, xm):
                        quantize(j, q * QTR, QTR)

        def w_second():
            for j in (0, 1):
                @pl.when(d[j] == 1)
                def _(j=j):
                    W0[j].wait_recv()
                    W2[j].start()
                    W4[j].start()
                    W5[j].start()

                @pl.when(d[j] == 3)
                def _(j=j):
                    W1[j].wait_recv()
                    W3[j].start()
                    W4[j].start()
                    W5[j].start()

        def w_third():
            for j in (0, 1):
                @pl.when(d[j] == 2)
                def _(j=j):
                    W2[j].wait_recv()
                    W3[j].wait_recv()
                    W4[j].start()
                    W5[j].start()

        def w_relay():
            for j in (0, 1):
                @pl.when(d[j] == 1)
                def _(j=j):
                    U0[j].wait_recv()
                    U2[j].start()

                @pl.when(d[j] == 3)
                def _(j=j):
                    U1[j].wait_recv()
                    U3[j].start()

        def w_fourth():
            for j in (0, 1):
                @pl.when(d[j] != 0)
                def _(j=j):
                    W4r[j].wait_recv()
                    W6[j].start()
                    W5r[j].wait_recv()
                    W7[j].start()

        def w_load(j):
            @pl.when(d[j] != 0)
            def _():
                W6r[j].wait_recv()
                W7r[j].wait_recv()

            @pl.when(d[j] == 2)
            def _():
                U2[j].wait_recv()
                U3[j].wait_recv()

            local("w", wc_hbm.at[j], wst.at[pl.ds(0, NSLOT)]).start()

        def w_ready(j):
            local("w", wc_hbm.at[j], wst.at[pl.ds(0, NSLOT)]).wait()

        def grads(j, hooks):
            @pl.loop(0, 16)
            def _(r):
                rows = pl.ds(pl.multiple_of(r * 256, 256), 256)
                g = lax.dot_general(tok_v[:, rows], cb[j], (((0,), (0,)), ((), ())), preferred_element_type=F32)
                g = g.astype(BF16)
                for h in (0, 1):
                    for c in range(COLS):
                        gw[(r * 2 + h) * COLS + c] = g[h * BS:(h + 1) * BS, c * BS:(c + 1) * BS]
                for at, steps in hooks.items():
                    @pl.when(r == at)
                    def _(steps=steps):
                        for step in steps:
                            step()

        def pick(j, o):
            @pl.loop(0, SLOTS)
            def _(s):
                gs[j, o, s] = gw[tabs[j, o, s]]

        def assemble(j):
            @pl.loop(0, ROWS)
            def _(r):
                for c in range(COLS):
                    gw[r * COLS + c] = wst[invs[j, r // 16, (r % 16) * 8 + c]]

        def forward(j, lo_m, hi_m, hooks):
            @pl.loop(lo_m, hi_m)
            def _(m):
                zz = (z + jnp.where(m == 0, 2, jnp.where(m == 1, 1, jnp.where(m == 2, 3, 0)))) % 4
                rows = pl.ds(pl.multiple_of(zz * 256, 256), 256)
                w = jnp.concatenate(
                    [jnp.concatenate([gw[r * COLS + c] for c in range(COLS)], axis=1) for r in range(ROWS)], axis=0
                )
                o = jnp.dot(tok_v[rows, :], w, preferred_element_type=F32)
                ob[j, rows, :] = o.astype(BF16)
                for at, steps in hooks.items():
                    @pl.when(m == at)
                    def _(steps=steps):
                        for step in steps:
                            step()

        o_own = [local(f"o{j}", ob.at[j, slot(z, k)], out_hbm.at[:, cols(2 * k + j, z)]) for j in (0, 1)]
        o_sends = []
        for j in (0, 1):
            dst = out_hbm.at[:, cols(2 * k + j, z)]
            row = []
            row.append(remote(f"O3{j}", ob.at[j, slot(zo, 0)], orel.at[0, j], "z+"))
            row.append(remote(f"O4{j}", ob.at[j, slot(zo, 1)], orel.at[1, j], "z-"))
            for i in (0, 1):
                row.append(remote(f"O1{j}{i}", ob.at[j, slot(zp, i)], dst, f"z+{i}", rkey=f"O1r{j}", roff=k, rwidth=2))
            for i in (0, 1):
                row.append(remote(f"O2{j}{i}", ob.at[j, slot(zm, i)], dst, f"z-{i}", rkey=f"O2r{j}", roff=k, rwidth=2))
            row.append(remote(f"O0{j}", ob.at[j, slot(z, kk)], dst, "p"))
            o_sends.append(row)
        O3r = [remote(f"O3{j}", orel.at[0, j], orel.at[0, j], "z+") for j in (0, 1)]
        O4r = [remote(f"O4{j}", orel.at[1, j], orel.at[1, j], "z-") for j in (0, 1)]
        O5 = [remote(f"O5{j}", orel.at[0, j], out_hbm.at[:, cols(2 * k + j, zm)], "z+0", rkey=f"O5r{j}", roff=k, rwidth=2) for j in (0, 1)]
        O6 = [remote(f"O6{j}", orel.at[1, j], out_hbm.at[:, cols(2 * k + j, zp)], "z-1", rkey=f"O5r{j}", roff=k, rwidth=2) for j in (0, 1)]

        def o_recvs(j):
            src = ob.at[j, slot(z, 0)]
            out = [remote(f"O0{j}", src, out_hbm.at[:, cols(2 * kk + j, z)], "p")]
            for i in (0, 1):
                out.append(remote(f"O1{j}0", src, out_hbm.at[:, cols(2 * i + j, zm)], "z+", rkey=f"O1r{j}", roff=i, rwidth=2))
                out.append(remote(f"O2{j}0", src, out_hbm.at[:, cols(2 * i + j, zp)], "z-", rkey=f"O2r{j}", roff=i, rwidth=2))
                out.append(remote(f"O5{j}", src, out_hbm.at[:, cols(2 * i + j, zo)], "z+", rkey=f"O5r{j}", roff=i, rwidth=2))
            return out

        def add1(dst, src, n):
            @pl.loop(0, n)
            def _(i):
                dst[i] = (dst[i].astype(F32) + src[i].astype(F32)).astype(BF16)

        def add2(dst, a, b, n):
            @pl.loop(0, n)
            def _(i):
                dst[i] = (dst[i].astype(F32) + a[i].astype(F32) + b[i].astype(F32)).astype(BF16)

        def sum3(out, dst, a, b, count):
            @pl.loop(0, SLOTS)
            def _(i):
                live = jnp.minimum(jnp.maximum(count - i, 0), 1).astype(F32)
                out[i] = (dst[i].astype(F32) + a[i].astype(F32) + b[i].astype(F32)) * live

        lo, hi = pl.ds(0, LO), pl.ds(LO, HI)

        class XStage:
            def __init__(self, name, j, base, first, second):
                self.j, self.base = j, base
                self.first = first
                self.c0 = remote(f"{name}0", gs.at[j, base + xo, lo], first.at[0], "x+")
                self.c1 = remote(f"{name}1", gs.at[j, base + xo, hi], first.at[1, pl.ds(0, HI)], "x-")
                self.c2l = remote(f"{name}2l", gs.at[j, base + xp, lo], second.at[0, lo], "x+")
                self.c2h = remote(f"{name}2h", gs.at[j, base + xp, hi], second.at[0, hi], "x+")
                self.c3l = remote(f"{name}3l", gs.at[j, base + xm, lo], second.at[1, lo], "x-")
                self.c3h = remote(f"{name}3h", gs.at[j, base + xm, hi], second.at[1, hi], "x-")

            def start(self, which=(0, 1, 2)):
                for i in which:
                    for copy in ((self.c0, self.c1), (self.c2h,), (self.c3l,))[i]:
                        copy.start()

            def middle(self):
                self.c0.wait_recv()
                add1(gs.at[self.j, self.base + xp, lo], self.first.at[0], LO)
                self.c2l.start()
                self.c1.wait_recv()
                add1(gs.at[self.j, self.base + xm, hi], self.first.at[1], HI)
                self.c3h.start()

            def arrive(self):
                for copy in (self.c2h, self.c3l, self.c2l, self.c3h):
                    copy.wait_recv()

            def sends(self):
                return [self.c0, self.c1, self.c2l, self.c2h, self.c3l, self.c3h]

        class YStage:
            def __init__(self, name, j, src, low, high, relay, high_relay, second, add):
                self.j, self.add, self.relay = j, add, relay
                self.low, self.high = src.at[low], src.at[high]
                self.c0 = remote(f"{name}0", self.low, relay, "y+")
                self.c1 = remote(f"{name}1", self.high, high_relay, "y-")
                self.c2l = remote(f"{name}2l", self.low, second.at[0].at[low], "y+")
                self.c2h = remote(f"{name}2h", self.high, second.at[0].at[high], "y+")
                self.c3l = remote(f"{name}3l", self.low, second.at[1].at[low], "y-")
                self.c3h = remote(f"{name}3h", self.high, second.at[1].at[high], "y-")

            def start(self):
                @pl.when(d[self.j] == 2)
                def _():
                    self.c0.start()
                    self.c1.start()

                @pl.when(d[self.j] == 3)
                def _():
                    self.c2h.start()

                @pl.when(d[self.j] == 1)
                def _():
                    self.c3l.start()

            def middle(self):
                @pl.when(d[self.j] == 3)
                def _():
                    self.c0.wait_recv()
                    self.add(self.low, self.relay, 0)
                    self.c2l.start()

                @pl.when(d[self.j] == 1)
                def _():
                    self.c1.wait_recv()
                    self.add(self.high, self.relay, 1)
                    self.c3h.start()

            def arrive(self):
                for copy in (self.c2h, self.c3l, self.c2l, self.c3h):
                    copy.wait_recv()

            def wait_sends(self):
                @pl.when(d[self.j] == 2)
                def _():
                    self.c0.wait_send()
                    self.c1.wait_send()

                @pl.when(d[self.j] == 3)
                def _():
                    self.c2h.wait_send()
                    self.c2l.wait_send()

                @pl.when(d[self.j] == 1)
                def _():
                    self.c3l.wait_send()
                    self.c3h.wait_send()

        AX = [XStage(f"A{j}", j, 0, ra1.at[j], ra2.at[j]) for j in (0, 1)]
        def add_ay(dst, src, half):
            add1(dst, src, (LO, HI)[half])

        AY = [YStage(f"Y{j}", j, gs.at[j, x], lo, hi, ry1, ry1.at[pl.ds(0, HI)], ry2, add_ay) for j in (0, 1)]
        order = (xo, xp, xm, x)
        BY = [
            [YStage(f"Z{j}{i}", j, gs.at[j, 4 + q], lo, hi, rz1.at[i], rz1.at[i, pl.ds(0, HI)], rz2.at[i], add_ay)
             for i, q in enumerate(order)]
            for j in (0, 1)
        ]
        BX = [XStage(f"B{j}", j, 4, rb1, rb2) for j in (0, 1)]

        def ax_end(j):
            AX[j].arrive()
            add2(gs.at[j, x], ra2.at[j, 0], ra2.at[j, 1], SLOTS)
            AY[j].start()

        def by_end(j, i):
            def go():
                @pl.when(d[j] == 0)
                def _():
                    BY[j][i].arrive()
                    add2(gs.at[j, 4 + order[i]], rz2.at[i, 0], rz2.at[i, 1], SLOTS)
                    if i < 3:
                        BX[j].start((i,))
            return go

        def bx_middle(j):
            @pl.when(d[j] == 0)
            def _():
                BX[j].middle()

        g_own = local("g", fin.at[k], wg_hbm)
        G = remote("G", fin.at[kk], wg_hbm, "p")

        def fin_out(half):
            @pl.when(k == half)
            def _():
                g_own.start()

            @pl.when(k != half)
            def _():
                G.start()

        def final_a(j):
            @pl.when(d[j] == 0)
            def _():
                AY[j].arrive()
                sum3(fin.at[0], gs.at[j, x], ry2.at[0], ry2.at[1], tabs[j, x, SLOTS])
                fin_out(0)

        def final_b(j):
            @pl.when(d[j] == 0)
            def _():
                BX[j].arrive()
                sum3(fin.at[1], gs.at[j, 4 + x], rb2.at[0], rb2.at[1], tabs[j, 4 + x, SLOTS])
                fin_out(1)

        def o_start(j, *which):
            def go():
                for i in which:
                    if i < 0:
                        o_own[j].start()
                    else:
                        o_sends[j][i].start()
            return go

        def o_hooks(j):
            return {0: [o_start(j, 0, 1)], 1: [o_start(j, 2, 3)], 2: [o_start(j, 4, 5)], 3: [o_start(j, 6, -1)]}

        def o_relay(j):
            O3r[j].wait_recv()
            O5[j].start()
            O4r[j].wait_recv()
            O6[j].start()

        def c_relay(j):
            C3r[j].wait_recv()
            C5[j].start()
            C4r[j].wait_recv()
            C6[j].start()

        def reduce_start(j):
            for i, q in enumerate(order):
                pick(j, q)
                if i < 3:
                    AX[j].start((i,))
                pick(j, 4 + q)
                BY[j][i].start()

        t_own.start()
        for copy in (T0, T1, T2):
            copy.start()
        tab_start()
        for copy in c_sends[0] + c_own:
            copy.start()
        w_first()
        wst[NSLOT] = jnp.zeros((BS, BS), BF16)
        tab_finish()
        w_second()
        w_third()
        T0r.wait_recv()
        T5.start()
        T3.start()
        T1r.wait_recv()
        T6.start()
        T4.start()
        inv = local("inv", invv, invs)
        inv.start()
        c_relay(0)
        for copy in c_sends[1]:
            copy.start()
        w_relay()
        w_fourth()
        T5r.wait_recv()
        T7.start()
        T6r.wait_recv()
        T8.start()
        t_own.wait()
        inv.wait()
        for copy in (T2r, T3r, T4r, T7r, T8r):
            copy.wait_recv()
        c_own[0].wait()
        for copy in c_recvs(0):
            copy.wait_recv()
        grads(0, {10: [lambda: c_relay(1)], 12: [lambda: w_load(0)]})
        reduce_start(0)
        w_ready(0)
        assemble(0)
        hooks = o_hooks(0)
        hooks[1] += [BY[0][0].middle, BY[0][1].middle]
        forward(0, 0, 2, hooks)
        c_own[1].wait()
        for copy in c_recvs(1):
            copy.wait_recv()
        grads(1, {4: [AX[0].middle, BY[0][2].middle], 8: [BY[0][3].middle]})
        reduce_start(1)
        assemble(0)
        w_load(1)
        hooks = o_hooks(0)
        hooks[2] += [lambda: ax_end(0)]
        hooks[3] += [AX[1].middle, BY[1][0].middle]
        forward(0, 2, 4, hooks)
        w_ready(1)
        assemble(1)
        AY[0].middle()
        o_relay(0)
        for i in range(4):
            by_end(0, i)()
        hooks = o_hooks(1)
        hooks[0] += [BY[1][1].middle]
        hooks[1] += [BY[1][2].middle]
        hooks[2] += [BY[1][3].middle]
        hooks[3] += [lambda: ax_end(1)]
        forward(1, 0, 4, hooks)
        by_end(1, 0)()
        by_end(1, 1)()
        AY[1].middle()
        bx_middle(0)
        by_end(1, 2)()
        o_relay(1)
        final_a(0)
        bx_middle(1)
        by_end(1, 3)()
        final_b(0)
        final_a(1)
        final_b(1)

        for j in (0, 1):
            for copy in o_recvs(j):
                copy.wait_recv()
            o_own[j].wait()

        own_final = (y // 2) == k

        @pl.when(own_final)
        def _():
            g_own.wait()
            G.wait_send()

        @pl.when(jnp.logical_not(own_final))
        def _():
            G.wait_recv()

        for copy in (T0, T1, T2, T3, T4, T5, T6, T7, T8):
            copy.wait_send()
        for j in (0, 1):
            for copy in c_sends[j] + [C5[j], C6[j]] + o_sends[j] + [O5[j], O6[j]] + AX[j].sends():
                copy.wait_send()
            AY[j].wait_sends()
            for i in range(4):
                BY[j][i].wait_sends()

            @pl.when(d[j] == 0)
            def _(j=j):
                for copy in [W0[j], W1[j], U0[j], U1[j]] + V[j] + BX[j].sends():
                    copy.wait_send()

            @pl.when(d[j] == 1)
            def _(j=j):
                W2[j].wait_send()
                U2[j].wait_send()

            @pl.when(d[j] == 3)
            def _(j=j):
                W3[j].wait_send()
                U3[j].wait_send()

            @pl.when(d[j] != 0)
            def _(j=j):
                for copy in (W4[j], W5[j], W6[j], W7[j]):
                    copy.wait_send()

    return kernel


def shards(tokens, cotangent, master, block_ids, live_count):
    owners, slots = block_ids.shape
    table = jnp.pad(block_ids, ((0, 0), (0, 128 - slots))) + jnp.pad(live_count, ((0, 0), (slots, 127 - slots)))
    vmem = pltpu.VMEM
    blk = (BS, BS)
    anyspec = pl.BlockSpec(memory_space=pl.ANY)
    outputs, w_grad, _ = pl.pallas_call(
        make_kernel(Names(), Names(), Names()),
        out_shape=(
            jax.ShapeDtypeStruct(cotangent.shape, BF16),
            jax.ShapeDtypeStruct((slots,) + blk, F32),
            jax.ShapeDtypeStruct((2, NSLOT) + blk, BF16),
        ),
        in_specs=[anyspec] * 4,
        out_specs=(anyspec,) * 3,
        scratch_shapes=[
            vmem((8 * TOK, ROWS * BS), BF16),
            vmem((2, 8 * TOK, WID), BF16),
            vmem((2, 2, TOK, WID), BF16),
            vmem((ROWS * COLS,) + blk, BF16),
            vmem((NSLOT + 1,) + blk, BF16),
            vmem((2, 8 * TOK, WID), BF16),
            vmem((2, 2, TOK, WID), BF16),
            vmem((2, OWN, SLOTS) + blk, BF16),
            vmem((2, 2, LO) + blk, BF16),
            vmem((2, 2, SLOTS) + blk, BF16),
            vmem((LO,) + blk, BF16),
            vmem((2, SLOTS) + blk, BF16),
            vmem((4, LO) + blk, BF16),
            vmem((4, 2, SLOTS) + blk, BF16),
            vmem((2, LO) + blk, BF16),
            vmem((2, SLOTS) + blk, BF16),
            vmem((2, SLOTS) + blk, F32),
            vmem((2, 8, 128), jnp.int32),
            pltpu.SMEM((2, 8, 128), jnp.int32),
            vmem((2, 8, 128), jnp.int32),
            pltpu.SMEM((2, 8, 128), jnp.int32),
            pltpu.SemaphoreType.DMA((184,)),
            pltpu.SemaphoreType.DMA((184,)),
            pltpu.SemaphoreType.DMA((20,)),
        ],
        compiler_params=pltpu.CompilerParams(
            collective_id=0, has_side_effects=True, vmem_limit_bytes=66 * 1024 * 1000
        ),
    )(tokens, cotangent, master.reshape(owners * slots, BS, BS), table)
    return finish(outputs, w_grad)


def finish(outputs, w_grad):
    n_o, n_g = 8, 3
    rows, each = outputs.shape[0] // n_o, SLOTS // n_g

    def body(o_ref, g_ref, o_out, g_out, o_v, g_v, in_sem, out_sem):
        loads, stores = [], []
        for i in range(n_o):
            part = pl.ds(i * rows, rows)
            loads.append(pltpu.make_async_copy(o_ref.at[part], o_v.at[part], in_sem.at[i]))
            stores.append(pltpu.make_async_copy(o_v.at[part], o_out.at[part], out_sem.at[i]))
        for i in range(n_g):
            part = pl.ds(i * each, each)
            loads.append(pltpu.make_async_copy(g_ref.at[part], g_v.at[part], in_sem.at[n_o + i]))
            stores.append(pltpu.make_async_copy(g_v.at[part], g_out.at[part], out_sem.at[n_o + i]))
        for load in loads:
            load.start()
        for load, store in zip(loads, stores):
            load.wait()
            store.start()
        for store in stores:
            store.wait()

    anyspec = pl.BlockSpec(memory_space=pl.ANY)
    outputs, w_grad = pl.pallas_call(
        body,
        out_shape=(
            jax.ShapeDtypeStruct(outputs.shape, outputs.dtype),
            jax.ShapeDtypeStruct(w_grad.shape, w_grad.dtype),
        ),
        in_specs=[anyspec] * 2,
        out_specs=(anyspec,) * 2,
        scratch_shapes=[
            pltpu.VMEM(outputs.shape, outputs.dtype),
            pltpu.VMEM(w_grad.shape, w_grad.dtype),
            pltpu.SemaphoreType.DMA((n_o + n_g,)),
            pltpu.SemaphoreType.DMA((n_o + n_g,)),
        ],
    )(outputs, w_grad)
    return outputs, w_grad[None]


def solution(mesh):
    return jax.shard_map(
        shards,
        mesh=mesh,
        in_specs=(
            P(("dp", "seq", "tensor"), None),
            P(("dp", "seq", "tensor"), None),
            P(None, "tensor", None, None),
            P(None, "tensor"),
            P(None, "tensor"),
        ),
        out_specs=(P(("dp", "seq", "tensor"), None), P(("dp", "seq"), "tensor", None, None)),
        check_vma=False,
    )
```

```python
import functools

import jax
import jax.numpy as jnp
from jax import lax
from jax.experimental import pallas as pl
from jax.experimental.pallas import tpu as pltpu
from jax.sharding import PartitionSpec as P

BS = 128
ROWS = 32
COLS = 7
OWN = 8
SLOTS = 21
NSLOT = OWN * SLOTS
QTR = 28
HALF = QTR // 2
YLO = 4 * QTR
YN = NSLOT - YLO
YH = YN // 2
LO, HI = 11, 10
WID = COLS * BS
TOK = 128
MESH = pl.DeviceIdType.MESH
F32 = jnp.float32
BF16 = jnp.bfloat16


class Names:
    def __init__(self):
        self.n = 0
        self.at = {}

    def get(self, key, width=1):
        if key not in self.at:
            self.at[key] = self.n
            self.n += width
        return self.at[key]


def make_kernel(names_s, names_r, names_l):
    def kernel(
        tok_hbm, cot_hbm, q_hbm, tab_hbm,
        out_hbm, wg_hbm, wc_hbm,
        tok_v, cb, crel, gw, wst, ob, orel, gs, ra1, ra2, ry1, ry2, rz1, rz2, rb1, rb2, fin,
        tabv, tabs, invv, invs, ssem, rsem, lsem,
    ):
        k = lax.axis_index("dp")
        x = lax.axis_index("seq")
        t_me = lax.axis_index("tensor")
        y, z = t_me // 4, t_me % 4
        xp, xm, xo = (x + 1) % 4, (x + 3) % 4, (x + 2) % 4
        yp, ym, yo = (y + 1) % 4, (y + 3) % 4, (y + 2) % 4
        zp, zm, zo = (z + 1) % 4, (z + 3) % 4, (z + 2) % 4
        kk = 1 - k

        def dev(k_=None, x_=None, y_=None, z_=None):
            kd = k if k_ is None else k_
            xd = x if x_ is None else x_
            yd = y if y_ is None else y_
            zd = z if z_ is None else z_
            return (kd, xd, yd * 4 + zd)

        partner = dev(k_=kk)
        devs = {
            "x+": dev(x_=xp), "x-": dev(x_=xm), "y+": dev(y_=yp), "y-": dev(y_=ym), "y2": dev(y_=yo),
            "z+": dev(z_=zp), "z-": dev(z_=zm), "p": partner,
            "z+0": dev(k_=0, z_=zp), "z+1": dev(k_=1, z_=zp), "z-0": dev(k_=0, z_=zm), "z-1": dev(k_=1, z_=zm),
        }

        def remote(key, src, dst, to, skey=None, rkey=None, roff=None, rwidth=1):
            si = names_s.get(skey or key)
            ri = names_r.get(rkey or key, rwidth)
            if roff is not None:
                ri = ri + roff
            assert max(si, names_r.n) < 184
            return pltpu.make_async_remote_copy(
                src_ref=src, dst_ref=dst, send_sem=ssem.at[si], recv_sem=rsem.at[ri],
                device_id=devs[to], device_id_type=MESH,
            )

        def local(key, src, dst):
            return pltpu.make_async_copy(src, dst, lsem.at[names_l.get(key)])

        def slot(z_, k_):
            return pl.ds(pl.multiple_of((z_ * 2 + k_) * TOK, TOK), TOK)

        def part(z_, k_, lo):
            return pl.ds(pl.multiple_of((z_ * 2 + k_) * TOK + lo, 64), 64)

        def cols(group_y, group_z):
            return pl.ds(pl.multiple_of((group_y * 4 + group_z) * WID, 128), WID)

        peers = [partner, devs["x+"], devs["x-"], devs["y+"], devs["y-"], devs["y2"],
                 devs["z+0"], devs["z+1"], devs["z-0"], devs["z-1"]]
        barrier = pltpu.get_barrier_semaphore()
        for peer in peers:
            pl.semaphore_signal(barrier, inc=1, device_id=peer, device_id_type=MESH)
        pl.semaphore_wait(barrier, len(peers))

        d = [(y + 4 - (2 * k + j)) % 4 for j in (0, 1)]
        tok2 = tok_hbm

        t_own = local("t", tok2, tok_v.at[slot(z, k)])
        T0 = remote("T0", tok2, tok_v.at[slot(z, k)], "z+")
        T1 = remote("T1", tok2, tok_v.at[slot(z, k)], "z-")
        T2 = remote("T2", tok2, tok_v.at[slot(z, k)], "p")
        T0r = remote("T0", tok2, tok_v.at[slot(zm, k)], "z+")
        T1r = remote("T1", tok2, tok_v.at[slot(zp, k)], "z-")
        T2r = remote("T2", tok2, tok_v.at[slot(z, kk)], "p")
        T3 = remote("T3", tok_v.at[slot(zm, k)], tok_v.at[slot(zm, k)], "p")
        T4 = remote("T4", tok_v.at[slot(zp, k)], tok_v.at[slot(zp, k)], "p")
        T3r = remote("T3", tok_v.at[slot(zm, kk)], tok_v.at[slot(zm, kk)], "p")
        T4r = remote("T4", tok_v.at[slot(zp, kk)], tok_v.at[slot(zp, kk)], "p")
        T5 = remote("T5", tok_v.at[part(zm, k, 0)], tok_v.at[part(zm, k, 0)], "z+")
        T6 = remote("T6", tok_v.at[part(zp, k, 64)], tok_v.at[part(zp, k, 64)], "z-")
        T5r = remote("T5", tok_v.at[part(zo, k, 0)], tok_v.at[part(zo, k, 0)], "z+")
        T6r = remote("T6", tok_v.at[part(zo, k, 64)], tok_v.at[part(zo, k, 64)], "z-")
        T7 = remote("T7", tok_v.at[part(zo, k, 0)], tok_v.at[part(zo, k, 0)], "p")
        T8 = remote("T8", tok_v.at[part(zo, k, 64)], tok_v.at[part(zo, k, 64)], "p")
        T7r = remote("T7", tok_v.at[part(zo, kk, 0)], tok_v.at[part(zo, kk, 0)], "p")
        T8r = remote("T8", tok_v.at[part(zo, kk, 64)], tok_v.at[part(zo, kk, 64)], "p")

        def cot(group_y, group_z):
            return cot_hbm.at[:, cols(group_y, group_z)]

        c_own = [local(f"c{j}", cot(2 * k + j, z), cb.at[j, slot(z, k)]) for j in (0, 1)]
        c_sends = []
        for j in (0, 1):
            row = []
            row.append(remote(f"C3{j}", cot(j, zo), crel.at[0, j], "z+"))
            row.append(remote(f"C4{j}", cot(2 + j, zo), crel.at[1, j], "z-"))
            for k_ in (0, 1):
                row.append(remote(f"C1{j}{k_}", cot(2 * k_ + j, zp), cb.at[j, slot(z, k)], f"z+{k_}",
                                  rkey=f"C1r{j}", roff=k, rwidth=2))
                row.append(remote(f"C2{j}{k_}", cot(2 * k_ + j, zm), cb.at[j, slot(z, k)], f"z-{k_}",
                                  rkey=f"C2r{j}", roff=k, rwidth=2))
            row.append(remote(f"C0{j}", cot(2 * kk + j, z), cb.at[j, slot(z, k)], "p"))
            c_sends.append(row)
        C3r = [remote(f"C3{j}", cot(j, zo), crel.at[0, j], "z+") for j in (0, 1)]
        C4r = [remote(f"C4{j}", cot(2 + j, zo), crel.at[1, j], "z-") for j in (0, 1)]
        C5 = [remote(f"C5{j}", crel.at[0, j], cb.at[j, slot(zm, k)], "z+0", rkey=f"C5r{j}", roff=k, rwidth=2) for j in (0, 1)]
        C6 = [remote(f"C6{j}", crel.at[1, j], cb.at[j, slot(zp, k)], "z-1", rkey=f"C5r{j}", roff=k, rwidth=2) for j in (0, 1)]

        def c_near(j):
            out = [remote(f"C0{j}", cot(j, z), cb.at[j, slot(z, kk)], "p")]
            for i in (0, 1):
                out.append(remote(f"C1{j}0", cot(j, z), cb.at[j, slot(zm, i)], "z+", rkey=f"C1r{j}", roff=i, rwidth=2))
                out.append(remote(f"C2{j}0", cot(j, z), cb.at[j, slot(zp, i)], "z-", rkey=f"C2r{j}", roff=i, rwidth=2))
            c_own[j].wait()
            for copy in out:
                copy.wait_recv()

        def c_far(j):
            for i in (0, 1):
                remote(f"C5{j}", cot(j, z), cb.at[j, slot(zo, i)], "z+", rkey=f"C5r{j}", roff=i, rwidth=2).wait_recv()

        def wq(j, q):
            return wc_hbm.at[j, pl.ds(q * QTR, QTR)]

        def wlo(j, q):
            return wc_hbm.at[j, pl.ds(q * QTR, HALF)]

        def whi(j, q):
            return wc_hbm.at[j, pl.ds(q * QTR + HALF, HALF)]

        def wu(j, lo=0, n=YN):
            return wc_hbm.at[j, pl.ds(YLO + lo, n)]

        JS = (0, 1)
        W0 = [remote(f"W0{j}", wq(j, x), wq(j, x), "y+") for j in JS]
        W1 = [remote(f"W1{j}", wq(j, x), wq(j, x), "y-") for j in JS]
        W2 = [remote(f"W2{j}", wlo(j, x), wlo(j, x), "y+") for j in JS]
        W3 = [remote(f"W3{j}", whi(j, x), whi(j, x), "y-") for j in JS]
        W4 = [remote(f"W4{j}", wq(j, x), wq(j, x), "x+") for j in JS]
        W5 = [remote(f"W5{j}", wq(j, x), wq(j, x), "x-") for j in JS]
        W4r = [remote(f"W4{j}", wq(j, xm), wq(j, xm), "x+") for j in JS]
        W5r = [remote(f"W5{j}", wq(j, xp), wq(j, xp), "x-") for j in JS]
        W6 = [remote(f"W6{j}", wlo(j, xm), wlo(j, xm), "x+") for j in JS]
        W7 = [remote(f"W7{j}", whi(j, xp), whi(j, xp), "x-") for j in JS]
        W6r = [remote(f"W6{j}", wlo(j, xo), wlo(j, xo), "x+") for j in JS]
        W7r = [remote(f"W7{j}", whi(j, xo), whi(j, xo), "x-") for j in JS]
        U0 = [remote(f"WU0{j}", wu(j), wu(j), "y+") for j in JS]
        U1 = [remote(f"WU1{j}", wu(j), wu(j), "y-") for j in JS]
        U2 = [remote(f"WU2{j}", wu(j, 0, YH), wu(j, 0, YH), "y+") for j in JS]
        U3 = [remote(f"WU3{j}", wu(j, YH, YH), wu(j, YH, YH), "y-") for j in JS]
        V = [[remote(f"V{j}{i}", tab_hbm, tabv.at[j], to) for i, to in enumerate(("y+", "y-", "y2"))] for j in (0, 1)]

        def tab_start():
            for j in (0, 1):
                @pl.when(d[j] == 0)
                def _(j=j):
                    for copy in V[j]:
                        copy.start()
                    local(f"v{j}", tab_hbm, tabv.at[j]).start()

        def tab_finish():
            for j in (0, 1):
                @pl.when(d[j] == 0)
                def _(j=j):
                    local(f"v{j}", tab_hbm, tabv.at[j]).wait()

                for i, dist in enumerate((1, 3, 2)):
                    @pl.when(d[j] == dist)
                    def _(j=j, i=i):
                        V[j][i].wait_recv()
            cp = local("tab", tabv, tabs)
            cp.start()
            cp.wait()
            spot = lax.broadcasted_iota(jnp.int32, (8, 128), 0) * 128 + lax.broadcasted_iota(jnp.int32, (8, 128), 1)
            spot = jnp.where((spot & 7) < COLS, (spot >> 3) * COLS + (spot & 7), -1)
            for j in (0, 1):
                def slot_step(s, inv, j=j):
                    for o in range(OWN):
                        named = jnp.where(s < tabs[j, o, SLOTS], tabs[j, o, s], -2)
                        inv = jnp.where(spot == named, o * SLOTS + s, inv)
                    return inv
                invv[j] = lax.fori_loop(0, SLOTS, slot_step, jnp.full((8, 128), NSLOT, jnp.int32))

        def quantize(j, start, n):
            @pl.loop(0, n // 4)
            def _(i):
                rows = pl.ds(start + i * 4, 4)
                wide = wst[rows].astype(F32)
                peak = jnp.max(jnp.abs(wide), axis=(1, 2), keepdims=True) + 1e-06
                levels = jnp.floor(wide * (7.0 / peak) + 0.5)
                wst[rows] = (levels * (peak / 7.0)).astype(BF16)

            cp = local("qw", wst.at[pl.ds(start, n)], wc_hbm.at[j, pl.ds(start, n)])
            cp.start()
            cp.wait()

        def w_first():
            for j in (0, 1):
                @pl.when(d[j] == 0)
                def _(j=j):
                    cp = local("q", q_hbm, wst.at[pl.ds(0, NSLOT)])
                    cp.start()
                    cp.wait()
                    quantize(j, x * QTR, QTR)
                    W0[j].start()
                    W1[j].start()
                    quantize(j, YLO, YN)
                    U0[j].start()
                    U1[j].start()
                    for q in (xp, xo, xm):
                        quantize(j, q * QTR, QTR)

        def w_second():
            for j in (0, 1):
                @pl.when(d[j] == 1)
                def _(j=j):
                    W0[j].wait_recv()
                    W2[j].start()
                    W4[j].start()
                    W5[j].start()

                @pl.when(d[j] == 3)
                def _(j=j):
                    W1[j].wait_recv()
                    W3[j].start()
                    W4[j].start()
                    W5[j].start()

        def w_third():
            for j in (0, 1):
                @pl.when(d[j] == 2)
                def _(j=j):
                    W2[j].wait_recv()
                    W3[j].wait_recv()
                    W4[j].start()
                    W5[j].start()

        def w_relay():
            for j in (0, 1):
                @pl.when(d[j] == 1)
                def _(j=j):
                    U0[j].wait_recv()
                    U2[j].start()

                @pl.when(d[j] == 3)
                def _(j=j):
                    U1[j].wait_recv()
                    U3[j].start()

        def w_fourth():
            for j in (0, 1):
                @pl.when(d[j] != 0)
                def _(j=j):
                    W4r[j].wait_recv()
                    W6[j].start()
                    W5r[j].wait_recv()
                    W7[j].start()

        def w_load(j):
            @pl.when(d[j] != 0)
            def _():
                W6r[j].wait_recv()
                W7r[j].wait_recv()

            @pl.when(d[j] == 2)
            def _():
                U2[j].wait_recv()
                U3[j].wait_recv()

            local("w", wc_hbm.at[j], wst.at[pl.ds(0, NSLOT)]).start()

        def w_ready(j):
            local("w", wc_hbm.at[j], wst.at[pl.ds(0, NSLOT)]).wait()

        def grads(j, chips, more, hooks):
            @pl.loop(0, 16)
            def _(r):
                rows = pl.ds(pl.multiple_of(r * 256, 256), 256)
                g = None
                for zz in chips:
                    ks = pl.ds(pl.multiple_of(zz * 256, 256), 256)
                    term = lax.dot_general(
                        tok_v[ks, rows], cb[j, ks, :], (((0,), (0,)), ((), ())), preferred_element_type=F32
                    )
                    g = term if g is None else g + term
                for h in (0, 1):
                    for c in range(COLS):
                        at = (r * 2 + h) * COLS + c
                        block = g[h * BS:(h + 1) * BS, c * BS:(c + 1) * BS]
                        if more:
                            block = block + gw[at].astype(F32)
                        gw[at] = block.astype(BF16)
                for at, steps in hooks.items():
                    @pl.when(r == at)
                    def _(steps=steps):
                        for step in steps:
                            step()

        def pick(j, o):
            @pl.loop(0, SLOTS)
            def _(s):
                gs[j, o, s] = gw[tabs[j, o, s]]

        def assemble(j):
            @pl.loop(0, ROWS)
            def _(r):
                for c in range(COLS):
                    gw[r * COLS + c] = wst[invs[j, r // 16, (r % 16) * 8 + c]]

        def forward(j, lo_m, hi_m, hooks):
            @pl.loop(lo_m, hi_m)
            def _(m):
                zz = (z + jnp.where(m == 0, 2, jnp.where(m == 1, 1, jnp.where(m == 2, 3, 0)))) % 4
                rows = pl.ds(pl.multiple_of(zz * 256, 256), 256)
                w = jnp.concatenate(
                    [jnp.concatenate([gw[r * COLS + c] for c in range(COLS)], axis=1) for r in range(ROWS)], axis=0
                )
                o = jnp.dot(tok_v[rows, :], w, preferred_element_type=F32)
                ob[j, rows, :] = o.astype(BF16)
                for at, steps in hooks.items():
                    @pl.when(m == at)
                    def _(steps=steps):
                        for step in steps:
                            step()

        o_own = [local(f"o{j}", ob.at[j, slot(z, k)], out_hbm.at[:, cols(2 * k + j, z)]) for j in (0, 1)]
        o_sends = []
        for j in (0, 1):
            dst = out_hbm.at[:, cols(2 * k + j, z)]
            row = []
            row.append(remote(f"O3{j}", ob.at[j, slot(zo, 0)], orel.at[0, j], "z+"))
            row.append(remote(f"O4{j}", ob.at[j, slot(zo, 1)], orel.at[1, j], "z-"))
            for i in (0, 1):
                row.append(remote(f"O1{j}{i}", ob.at[j, slot(zp, i)], dst, f"z+{i}", rkey=f"O1r{j}", roff=k, rwidth=2))
            for i in (0, 1):
                row.append(remote(f"O2{j}{i}", ob.at[j, slot(zm, i)], dst, f"z-{i}", rkey=f"O2r{j}", roff=k, rwidth=2))
            row.append(remote(f"O0{j}", ob.at[j, slot(z, kk)], dst, "p"))
            o_sends.append(row)
        O3r = [remote(f"O3{j}", orel.at[0, j], orel.at[0, j], "z+") for j in (0, 1)]
        O4r = [remote(f"O4{j}", orel.at[1, j], orel.at[1, j], "z-") for j in (0, 1)]
        O5 = [remote(f"O5{j}", orel.at[0, j], out_hbm.at[:, cols(2 * k + j, zm)], "z+0", rkey=f"O5r{j}", roff=k, rwidth=2) for j in (0, 1)]
        O6 = [remote(f"O6{j}", orel.at[1, j], out_hbm.at[:, cols(2 * k + j, zp)], "z-1", rkey=f"O5r{j}", roff=k, rwidth=2) for j in (0, 1)]

        def o_recvs(j):
            src = ob.at[j, slot(z, 0)]
            out = [remote(f"O0{j}", src, out_hbm.at[:, cols(2 * kk + j, z)], "p")]
            for i in (0, 1):
                out.append(remote(f"O1{j}0", src, out_hbm.at[:, cols(2 * i + j, zm)], "z+", rkey=f"O1r{j}", roff=i, rwidth=2))
                out.append(remote(f"O2{j}0", src, out_hbm.at[:, cols(2 * i + j, zp)], "z-", rkey=f"O2r{j}", roff=i, rwidth=2))
                out.append(remote(f"O5{j}", src, out_hbm.at[:, cols(2 * i + j, zo)], "z+", rkey=f"O5r{j}", roff=i, rwidth=2))
            return out

        def add1(dst, src, n):
            @pl.loop(0, n)
            def _(i):
                dst[i] = (dst[i].astype(F32) + src[i].astype(F32)).astype(BF16)

        def add2(dst, a, b, n):
            @pl.loop(0, n)
            def _(i):
                dst[i] = (dst[i].astype(F32) + a[i].astype(F32) + b[i].astype(F32)).astype(BF16)

        def sum3(out, dst, a, b, count):
            @pl.loop(0, SLOTS)
            def _(i):
                live = jnp.minimum(jnp.maximum(count - i, 0), 1).astype(F32)
                out[i] = (dst[i].astype(F32) + a[i].astype(F32) + b[i].astype(F32)) * live

        lo, hi = pl.ds(0, LO), pl.ds(LO, HI)

        class XStage:
            def __init__(self, name, j, base, first, second):
                self.j, self.base = j, base
                self.first = first
                self.c0 = remote(f"{name}0", gs.at[j, base + xo, lo], first.at[0], "x+")
                self.c1 = remote(f"{name}1", gs.at[j, base + xo, hi], first.at[1, pl.ds(0, HI)], "x-")
                self.c2l = remote(f"{name}2l", gs.at[j, base + xp, lo], second.at[0, lo], "x+")
                self.c2h = remote(f"{name}2h", gs.at[j, base + xp, hi], second.at[0, hi], "x+")
                self.c3l = remote(f"{name}3l", gs.at[j, base + xm, lo], second.at[1, lo], "x-")
                self.c3h = remote(f"{name}3h", gs.at[j, base + xm, hi], second.at[1, hi], "x-")

            def start(self, which=(0, 1, 2)):
                for i in which:
                    for copy in ((self.c0, self.c1), (self.c2h,), (self.c3l,))[i]:
                        copy.start()

            def middle(self):
                self.c0.wait_recv()
                add1(gs.at[self.j, self.base + xp, lo], self.first.at[0], LO)
                self.c2l.start()
                self.c1.wait_recv()
                add1(gs.at[self.j, self.base + xm, hi], self.first.at[1], HI)
                self.c3h.start()

            def arrive(self):
                for copy in (self.c2h, self.c3l, self.c2l, self.c3h):
                    copy.wait_recv()

            def sends(self):
                return [self.c0, self.c1, self.c2l, self.c2h, self.c3l, self.c3h]

        class YStage:
            def __init__(self, name, j, src, low, high, relay, high_relay, second, add):
                self.j, self.add, self.relay = j, add, relay
                self.low, self.high = src.at[low], src.at[high]
                self.c0 = remote(f"{name}0", self.low, relay, "y+")
                self.c1 = remote(f"{name}1", self.high, high_relay, "y-")
                self.c2l = remote(f"{name}2l", self.low, second.at[0].at[low], "y+")
                self.c2h = remote(f"{name}2h", self.high, second.at[0].at[high], "y+")
                self.c3l = remote(f"{name}3l", self.low, second.at[1].at[low], "y-")
                self.c3h = remote(f"{name}3h", self.high, second.at[1].at[high], "y-")

            def start(self):
                @pl.when(d[self.j] == 2)
                def _():
                    self.c0.start()
                    self.c1.start()

                @pl.when(d[self.j] == 3)
                def _():
                    self.c2h.start()

                @pl.when(d[self.j] == 1)
                def _():
                    self.c3l.start()

            def middle(self):
                @pl.when(d[self.j] == 3)
                def _():
                    self.c0.wait_recv()
                    self.add(self.low, self.relay, 0)
                    self.c2l.start()

                @pl.when(d[self.j] == 1)
                def _():
                    self.c1.wait_recv()
                    self.add(self.high, self.relay, 1)
                    self.c3h.start()

            def arrive(self):
                for copy in (self.c2h, self.c3l, self.c2l, self.c3h):
                    copy.wait_recv()

            def wait_sends(self):
                @pl.when(d[self.j] == 2)
                def _():
                    self.c0.wait_send()
                    self.c1.wait_send()

                @pl.when(d[self.j] == 3)
                def _():
                    self.c2h.wait_send()
                    self.c2l.wait_send()

                @pl.when(d[self.j] == 1)
                def _():
                    self.c3l.wait_send()
                    self.c3h.wait_send()

        AX = [XStage(f"A{j}", j, 0, ra1.at[j], ra2.at[j]) for j in (0, 1)]
        def add_ay(dst, src, half):
            add1(dst, src, (LO, HI)[half])

        AY = [YStage(f"Y{j}", j, gs.at[j, x], lo, hi, ry1, ry1.at[pl.ds(0, HI)], ry2, add_ay) for j in (0, 1)]
        order = (xo, xp, xm, x)
        BY = [
            [YStage(f"Z{j}{i}", j, gs.at[j, 4 + q], lo, hi, rz1.at[i], rz1.at[i, pl.ds(0, HI)], rz2.at[i], add_ay)
             for i, q in enumerate(order)]
            for j in (0, 1)
        ]
        BX = [XStage(f"B{j}", j, 4, rb1, rb2) for j in (0, 1)]

        def ax_end(j):
            AX[j].arrive()
            add2(gs.at[j, x], ra2.at[j, 0], ra2.at[j, 1], SLOTS)
            AY[j].start()

        def by_end(j, i):
            def go():
                @pl.when(d[j] == 0)
                def _():
                    BY[j][i].arrive()
                    add2(gs.at[j, 4 + order[i]], rz2.at[i, 0], rz2.at[i, 1], SLOTS)
                    if i < 3:
                        BX[j].start((i,))
            return go

        def bx_middle(j):
            @pl.when(d[j] == 0)
            def _():
                BX[j].middle()

        g_own = local("g", fin.at[k], wg_hbm)
        G = remote("G", fin.at[kk], wg_hbm, "p")

        def fin_out(half):
            @pl.when(k == half)
            def _():
                g_own.start()

            @pl.when(k != half)
            def _():
                G.start()

        def final_a(j):
            @pl.when(d[j] == 0)
            def _():
                AY[j].arrive()
                sum3(fin.at[0], gs.at[j, x], ry2.at[0], ry2.at[1], tabs[j, x, SLOTS])
                fin_out(0)

        def final_b(j):
            @pl.when(d[j] == 0)
            def _():
                BX[j].arrive()
                sum3(fin.at[1], gs.at[j, 4 + x], rb2.at[0], rb2.at[1], tabs[j, 4 + x, SLOTS])
                fin_out(1)

        def o_start(j, *which):
            def go():
                for i in which:
                    if i < 0:
                        o_own[j].start()
                    else:
                        o_sends[j][i].start()
            return go

        def o_hooks(j):
            return {0: [o_start(j, 0, 1)], 1: [o_start(j, 2, 3)], 2: [o_start(j, 4, 5)], 3: [o_start(j, 6, -1)]}

        def o_relay(j):
            O3r[j].wait_recv()
            O5[j].start()
            O4r[j].wait_recv()
            O6[j].start()

        def c_relay(j):
            C3r[j].wait_recv()
            C5[j].start()
            C4r[j].wait_recv()
            C6[j].start()

        def reduce_start(j):
            for i, q in enumerate(order):
                pick(j, q)
                if i < 3:
                    AX[j].start((i,))
                pick(j, 4 + q)
                BY[j][i].start()

        t_own.start()
        for copy in (T0, T1, T2):
            copy.start()
        tab_start()
        for copy in c_sends[0] + c_own:
            copy.start()
        w_first()
        wst[NSLOT] = jnp.zeros((BS, BS), BF16)
        tab_finish()
        w_second()
        w_third()
        T0r.wait_recv()
        T5.start()
        T3.start()
        T1r.wait_recv()
        T6.start()
        T4.start()
        inv = local("inv", invv, invs)
        inv.start()
        c_relay(0)
        for copy in c_sends[1]:
            copy.start()
        w_relay()
        t_own.wait()
        inv.wait()
        for copy in (T2r, T3r, T4r):
            copy.wait_recv()
        c_near(0)
        near, far = (z, zp, zm), (zo,)
        grads(0, near, False, {8: [w_fourth]})
        T5r.wait_recv()
        T7.start()
        T6r.wait_recv()
        T8.start()
        T7r.wait_recv()
        T8r.wait_recv()
        c_far(0)
        grads(0, far, True, {12: [lambda: c_relay(1)]})
        reduce_start(0)
        w_load(0)
        c_near(1)
        grads(1, near, False, {6: [BY[0][0].middle], 10: [BY[0][1].middle], 13: [AX[0].middle]})
        BY[0][2].middle()
        c_far(1)
        grads(1, far, True, {8: [BY[0][3].middle]})
        reduce_start(1)
        w_ready(0)
        assemble(0)
        w_load(1)
        hooks = o_hooks(0)
        hooks[0] += [lambda: ax_end(0)]
        hooks[3] += [AX[1].middle, AY[0].middle]
        forward(0, 0, 4, hooks)
        w_ready(1)
        assemble(1)
        for i in range(4):
            by_end(0, i)()
        BY[1][0].middle()
        o_relay(0)
        hooks = o_hooks(1)
        hooks[1] += [BY[1][1].middle]
        hooks[2] += [BY[1][2].middle]
        hooks[3] += [BY[1][3].middle]
        hooks[3] += [lambda: ax_end(1)]
        forward(1, 0, 4, hooks)
        by_end(1, 0)()
        by_end(1, 1)()
        AY[1].middle()
        bx_middle(0)
        by_end(1, 2)()
        o_relay(1)
        final_a(0)
        bx_middle(1)
        by_end(1, 3)()
        final_b(0)
        final_a(1)
        final_b(1)

        for j in (0, 1):
            for copy in o_recvs(j):
                copy.wait_recv()
            o_own[j].wait()

        own_final = (y // 2) == k

        @pl.when(own_final)
        def _():
            g_own.wait()
            G.wait_send()

        @pl.when(jnp.logical_not(own_final))
        def _():
            G.wait_recv()

        for copy in (T0, T1, T2, T3, T4, T5, T6, T7, T8):
            copy.wait_send()
        for j in (0, 1):
            for copy in c_sends[j] + [C5[j], C6[j]] + o_sends[j] + [O5[j], O6[j]] + AX[j].sends():
                copy.wait_send()
            AY[j].wait_sends()
            for i in range(4):
                BY[j][i].wait_sends()

            @pl.when(d[j] == 0)
            def _(j=j):
                for copy in [W0[j], W1[j], U0[j], U1[j]] + V[j] + BX[j].sends():
                    copy.wait_send()

            @pl.when(d[j] == 1)
            def _(j=j):
                W2[j].wait_send()
                U2[j].wait_send()

            @pl.when(d[j] == 3)
            def _(j=j):
                W3[j].wait_send()
                U3[j].wait_send()

            @pl.when(d[j] != 0)
            def _(j=j):
                for copy in (W4[j], W5[j], W6[j], W7[j]):
                    copy.wait_send()

    return kernel


def shards(tokens, cotangent, master, block_ids, live_count):
    owners, slots = block_ids.shape
    table = jnp.pad(block_ids, ((0, 0), (0, 128 - slots))) + jnp.pad(live_count, ((0, 0), (slots, 127 - slots)))
    vmem = pltpu.VMEM
    blk = (BS, BS)
    anyspec = pl.BlockSpec(memory_space=pl.ANY)
    outputs, w_grad, _ = pl.pallas_call(
        make_kernel(Names(), Names(), Names()),
        out_shape=(
            jax.ShapeDtypeStruct(cotangent.shape, BF16),
            jax.ShapeDtypeStruct((slots,) + blk, F32),
            jax.ShapeDtypeStruct((2, NSLOT) + blk, BF16),
        ),
        in_specs=[anyspec] * 4,
        out_specs=(anyspec,) * 3,
        scratch_shapes=[
            vmem((8 * TOK, ROWS * BS), BF16),
            vmem((2, 8 * TOK, WID), BF16),
            vmem((2, 2, TOK, WID), BF16),
            vmem((ROWS * COLS,) + blk, BF16),
            vmem((NSLOT + 1,) + blk, BF16),
            vmem((2, 8 * TOK, WID), BF16),
            vmem((2, 2, TOK, WID), BF16),
            vmem((2, OWN, SLOTS) + blk, BF16),
            vmem((2, 2, LO) + blk, BF16),
            vmem((2, 2, SLOTS) + blk, BF16),
            vmem((LO,) + blk, BF16),
            vmem((2, SLOTS) + blk, BF16),
            vmem((4, LO) + blk, BF16),
            vmem((4, 2, SLOTS) + blk, BF16),
            vmem((2, LO) + blk, BF16),
            vmem((2, SLOTS) + blk, BF16),
            vmem((2, SLOTS) + blk, F32),
            vmem((2, 8, 128), jnp.int32),
            pltpu.SMEM((2, 8, 128), jnp.int32),
            vmem((2, 8, 128), jnp.int32),
            pltpu.SMEM((2, 8, 128), jnp.int32),
            pltpu.SemaphoreType.DMA((184,)),
            pltpu.SemaphoreType.DMA((184,)),
            pltpu.SemaphoreType.DMA((20,)),
        ],
        compiler_params=pltpu.CompilerParams(
            collective_id=0, has_side_effects=True, vmem_limit_bytes=66 * 1024 * 1000
        ),
    )(tokens, cotangent, master.reshape(owners * slots, BS, BS), table)
    return finish(outputs, w_grad)


def finish(outputs, w_grad):
    n_o, n_g = 8, 3
    rows, each = outputs.shape[0] // n_o, SLOTS // n_g

    def body(o_ref, g_ref, o_out, g_out, o_v, g_v, in_sem, out_sem):
        loads, stores = [], []
        for i in range(n_o):
            part = pl.ds(i * rows, rows)
            loads.append(pltpu.make_async_copy(o_ref.at[part], o_v.at[part], in_sem.at[i]))
            stores.append(pltpu.make_async_copy(o_v.at[part], o_out.at[part], out_sem.at[i]))
        for i in range(n_g):
            part = pl.ds(i * each, each)
            loads.append(pltpu.make_async_copy(g_ref.at[part], g_v.at[part], in_sem.at[n_o + i]))
            stores.append(pltpu.make_async_copy(g_v.at[part], g_out.at[part], out_sem.at[n_o + i]))
        for load in loads:
            load.start()
        for load, store in zip(loads, stores):
            load.wait()
            store.start()
        for store in stores:
            store.wait()

    anyspec = pl.BlockSpec(memory_space=pl.ANY)
    outputs, w_grad = pl.pallas_call(
        body,
        out_shape=(
            jax.ShapeDtypeStruct(outputs.shape, outputs.dtype),
            jax.ShapeDtypeStruct(w_grad.shape, w_grad.dtype),
        ),
        in_specs=[anyspec] * 2,
        out_specs=(anyspec,) * 2,
        scratch_shapes=[
            pltpu.VMEM(outputs.shape, outputs.dtype),
            pltpu.VMEM(w_grad.shape, w_grad.dtype),
            pltpu.SemaphoreType.DMA((n_o + n_g,)),
            pltpu.SemaphoreType.DMA((n_o + n_g,)),
        ],
    )(outputs, w_grad)
    return outputs, w_grad[None]


def solution(mesh):
    return jax.shard_map(
        shards,
        mesh=mesh,
        in_specs=(
            P(("dp", "seq", "tensor"), None),
            P(("dp", "seq", "tensor"), None),
            P(None, "tensor", None, None),
            P(None, "tensor"),
            P(None, "tensor"),
        ),
        out_specs=(P(("dp", "seq", "tensor"), None), P(("dp", "seq"), "tensor", None, None)),
        check_vma=False,
    )
```

```python
import functools

import jax
import jax.numpy as jnp
from jax import lax
from jax.experimental import pallas as pl
from jax.experimental.pallas import tpu as pltpu
from jax.sharding import PartitionSpec as P

BS = 128
ROWS = 32
COLS = 7
OWN = 8
SLOTS = 21
NSLOT = OWN * SLOTS
QTR = 28
HALF = QTR // 2
YLO = 4 * QTR
YN = NSLOT - YLO
YH = YN // 2
LO, HI = 11, 10
WID = COLS * BS
TOK = 128
MESH = pl.DeviceIdType.MESH
F32 = jnp.float32
BF16 = jnp.bfloat16


class Names:
    def __init__(self):
        self.n = 0
        self.at = {}

    def get(self, key, width=1):
        if key not in self.at:
            self.at[key] = self.n
            self.n += width
        return self.at[key]


def make_kernel(names_s, names_r, names_l):
    def kernel(
        tok_hbm, cot_hbm, q_hbm, tab_hbm,
        out_hbm, wg_hbm, wc_hbm,
        tok_v, cb, crel, gw, wst, ob, orel, gs, ra1, ra2, ry1, ry2, rz1, rz2, rb1, rb2, fin,
        tabv, tabs, invv, invs, ssem, rsem, lsem,
    ):
        k = lax.axis_index("dp")
        x = lax.axis_index("seq")
        t_me = lax.axis_index("tensor")
        y, z = t_me // 4, t_me % 4
        xp, xm, xo = (x + 1) % 4, (x + 3) % 4, (x + 2) % 4
        yp, ym, yo = (y + 1) % 4, (y + 3) % 4, (y + 2) % 4
        zp, zm, zo = (z + 1) % 4, (z + 3) % 4, (z + 2) % 4
        kk = 1 - k

        def dev(k_=None, x_=None, y_=None, z_=None):
            kd = k if k_ is None else k_
            xd = x if x_ is None else x_
            yd = y if y_ is None else y_
            zd = z if z_ is None else z_
            return (kd, xd, yd * 4 + zd)

        partner = dev(k_=kk)
        devs = {
            "x+": dev(x_=xp), "x-": dev(x_=xm), "y+": dev(y_=yp), "y-": dev(y_=ym), "y2": dev(y_=yo),
            "z+": dev(z_=zp), "z-": dev(z_=zm), "p": partner,
            "z+0": dev(k_=0, z_=zp), "z+1": dev(k_=1, z_=zp), "z-0": dev(k_=0, z_=zm), "z-1": dev(k_=1, z_=zm),
        }

        def remote(key, src, dst, to, skey=None, rkey=None, roff=None, rwidth=1):
            si = names_s.get(skey or key)
            ri = names_r.get(rkey or key, rwidth)
            if roff is not None:
                ri = ri + roff
            assert max(si, names_r.n) < 184
            return pltpu.make_async_remote_copy(
                src_ref=src, dst_ref=dst, send_sem=ssem.at[si], recv_sem=rsem.at[ri],
                device_id=devs[to], device_id_type=MESH,
            )

        def local(key, src, dst):
            return pltpu.make_async_copy(src, dst, lsem.at[names_l.get(key)])

        def slot(z_, k_):
            return pl.ds(pl.multiple_of((z_ * 2 + k_) * TOK, TOK), TOK)

        def part(z_, k_, lo):
            return pl.ds(pl.multiple_of((z_ * 2 + k_) * TOK + lo, 64), 64)

        def cols(group_y, group_z):
            return pl.ds(pl.multiple_of((group_y * 4 + group_z) * WID, 128), WID)

        peers = [partner, devs["x+"], devs["x-"], devs["y+"], devs["y-"], devs["y2"],
                 devs["z+0"], devs["z+1"], devs["z-0"], devs["z-1"]]
        barrier = pltpu.get_barrier_semaphore()
        for peer in peers:
            pl.semaphore_signal(barrier, inc=1, device_id=peer, device_id_type=MESH)
        pl.semaphore_wait(barrier, len(peers))

        d = [(y + 4 - (2 * k + j)) % 4 for j in (0, 1)]
        tok2 = tok_hbm

        t_own = local("t", tok2, tok_v.at[slot(z, k)])
        T0 = remote("T0", tok2, tok_v.at[slot(z, k)], "z+")
        T1 = remote("T1", tok2, tok_v.at[slot(z, k)], "z-")
        T2 = remote("T2", tok2, tok_v.at[slot(z, k)], "p")
        T0r = remote("T0", tok2, tok_v.at[slot(zm, k)], "z+")
        T1r = remote("T1", tok2, tok_v.at[slot(zp, k)], "z-")
        T2r = remote("T2", tok2, tok_v.at[slot(z, kk)], "p")
        T3 = remote("T3", tok_v.at[slot(zm, k)], tok_v.at[slot(zm, k)], "p")
        T4 = remote("T4", tok_v.at[slot(zp, k)], tok_v.at[slot(zp, k)], "p")
        T3r = remote("T3", tok_v.at[slot(zm, kk)], tok_v.at[slot(zm, kk)], "p")
        T4r = remote("T4", tok_v.at[slot(zp, kk)], tok_v.at[slot(zp, kk)], "p")
        T5 = remote("T5", tok_v.at[part(zm, k, 0)], tok_v.at[part(zm, k, 0)], "z+")
        T6 = remote("T6", tok_v.at[part(zp, k, 64)], tok_v.at[part(zp, k, 64)], "z-")
        T5r = remote("T5", tok_v.at[part(zo, k, 0)], tok_v.at[part(zo, k, 0)], "z+")
        T6r = remote("T6", tok_v.at[part(zo, k, 64)], tok_v.at[part(zo, k, 64)], "z-")
        T7 = remote("T7", tok_v.at[part(zo, k, 0)], tok_v.at[part(zo, k, 0)], "p")
        T8 = remote("T8", tok_v.at[part(zo, k, 64)], tok_v.at[part(zo, k, 64)], "p")
        T7r = remote("T7", tok_v.at[part(zo, kk, 0)], tok_v.at[part(zo, kk, 0)], "p")
        T8r = remote("T8", tok_v.at[part(zo, kk, 64)], tok_v.at[part(zo, kk, 64)], "p")

        def cot(group_y, group_z):
            return cot_hbm.at[:, cols(group_y, group_z)]

        c_own = [local(f"c{j}", cot(2 * k + j, z), cb.at[j, slot(z, k)]) for j in (0, 1)]
        c_sends = []
        for j in (0, 1):
            row = []
            row.append(remote(f"C3{j}", cot(j, zo), crel.at[0, j], "z+"))
            row.append(remote(f"C4{j}", cot(2 + j, zo), crel.at[1, j], "z-"))
            for k_ in (0, 1):
                row.append(remote(f"C1{j}{k_}", cot(2 * k_ + j, zp), cb.at[j, slot(z, k)], f"z+{k_}",
                                  rkey=f"C1r{j}", roff=k, rwidth=2))
                row.append(remote(f"C2{j}{k_}", cot(2 * k_ + j, zm), cb.at[j, slot(z, k)], f"z-{k_}",
                                  rkey=f"C2r{j}", roff=k, rwidth=2))
            row.append(remote(f"C0{j}", cot(2 * kk + j, z), cb.at[j, slot(z, k)], "p"))
            c_sends.append(row)
        C3r = [remote(f"C3{j}", cot(j, zo), crel.at[0, j], "z+") for j in (0, 1)]
        C4r = [remote(f"C4{j}", cot(2 + j, zo), crel.at[1, j], "z-") for j in (0, 1)]
        C5 = [remote(f"C5{j}", crel.at[0, j], cb.at[j, slot(zm, k)], "z+0", rkey=f"C5r{j}", roff=k, rwidth=2) for j in (0, 1)]
        C6 = [remote(f"C6{j}", crel.at[1, j], cb.at[j, slot(zp, k)], "z-1", rkey=f"C5r{j}", roff=k, rwidth=2) for j in (0, 1)]

        def c_near(j):
            out = [remote(f"C0{j}", cot(j, z), cb.at[j, slot(z, kk)], "p")]
            for i in (0, 1):
                out.append(remote(f"C1{j}0", cot(j, z), cb.at[j, slot(zm, i)], "z+", rkey=f"C1r{j}", roff=i, rwidth=2))
                out.append(remote(f"C2{j}0", cot(j, z), cb.at[j, slot(zp, i)], "z-", rkey=f"C2r{j}", roff=i, rwidth=2))
            c_own[j].wait()
            for copy in out:
                copy.wait_recv()

        def c_far(j):
            for i in (0, 1):
                remote(f"C5{j}", cot(j, z), cb.at[j, slot(zo, i)], "z+", rkey=f"C5r{j}", roff=i, rwidth=2).wait_recv()

        def wq(j, q):
            return wc_hbm.at[j, pl.ds(q * QTR, QTR)]

        def wlo(j, q):
            return wc_hbm.at[j, pl.ds(q * QTR, HALF)]

        def whi(j, q):
            return wc_hbm.at[j, pl.ds(q * QTR + HALF, HALF)]

        def wu(j, lo=0, n=YN):
            return wc_hbm.at[j, pl.ds(YLO + lo, n)]

        JS = (0, 1)
        W0 = [remote(f"W0{j}", wq(j, x), wq(j, x), "y+") for j in JS]
        W1 = [remote(f"W1{j}", wq(j, x), wq(j, x), "y-") for j in JS]
        W2 = [remote(f"W2{j}", wlo(j, x), wlo(j, x), "y+") for j in JS]
        W3 = [remote(f"W3{j}", whi(j, x), whi(j, x), "y-") for j in JS]
        W4 = [remote(f"W4{j}", wq(j, x), wq(j, x), "x+") for j in JS]
        W5 = [remote(f"W5{j}", wq(j, x), wq(j, x), "x-") for j in JS]
        W4r = [remote(f"W4{j}", wq(j, xm), wq(j, xm), "x+") for j in JS]
        W5r = [remote(f"W5{j}", wq(j, xp), wq(j, xp), "x-") for j in JS]
        W6 = [remote(f"W6{j}", wlo(j, xm), wlo(j, xm), "x+") for j in JS]
        W7 = [remote(f"W7{j}", whi(j, xp), whi(j, xp), "x-") for j in JS]
        W6r = [remote(f"W6{j}", wlo(j, xo), wlo(j, xo), "x+") for j in JS]
        W7r = [remote(f"W7{j}", whi(j, xo), whi(j, xo), "x-") for j in JS]
        U0 = [remote(f"WU0{j}", wu(j), wu(j), "y+") for j in JS]
        U1 = [remote(f"WU1{j}", wu(j), wu(j), "y-") for j in JS]
        U2 = [remote(f"WU2{j}", wu(j, 0, YH), wu(j, 0, YH), "y+") for j in JS]
        U3 = [remote(f"WU3{j}", wu(j, YH, YH), wu(j, YH, YH), "y-") for j in JS]
        V = [[remote(f"V{j}{i}", tab_hbm, tabv.at[j], to) for i, to in enumerate(("y+", "y-", "y2"))] for j in (0, 1)]

        def tab_start():
            for j in (0, 1):
                @pl.when(d[j] == 0)
                def _(j=j):
                    for copy in V[j]:
                        copy.start()
                    local(f"v{j}", tab_hbm, tabv.at[j]).start()

        def tab_finish():
            for j in (0, 1):
                @pl.when(d[j] == 0)
                def _(j=j):
                    local(f"v{j}", tab_hbm, tabv.at[j]).wait()

                for i, dist in enumerate((1, 3, 2)):
                    @pl.when(d[j] == dist)
                    def _(j=j, i=i):
                        V[j][i].wait_recv()
            cp = local("tab", tabv, tabs)
            cp.start()
            cp.wait()
            spot = lax.broadcasted_iota(jnp.int32, (8, 128), 0) * 128 + lax.broadcasted_iota(jnp.int32, (8, 128), 1)
            spot = jnp.where((spot & 7) < COLS, (spot >> 3) * COLS + (spot & 7), -1)
            for j in (0, 1):
                def slot_step(s, inv, j=j):
                    for o in range(OWN):
                        named = jnp.where(s < tabs[j, 0, 32 + o], tabs[j, o, s], -2)
                        inv = jnp.where(spot == named, o * SLOTS + s, inv)
                    return inv
                invv[j] = lax.fori_loop(0, SLOTS, slot_step, jnp.full((8, 128), NSLOT, jnp.int32))

        def quantize(j, start, n):
            @pl.loop(0, n // 4)
            def _(i):
                rows = pl.ds(start + i * 4, 4)
                wide = wst[rows].astype(F32)
                peak = jnp.max(jnp.abs(wide), axis=(1, 2), keepdims=True) + 1e-06
                levels = jnp.floor(wide * (7.0 / peak) + 0.5)
                wst[rows] = (levels * (peak / 7.0)).astype(BF16)

            cp = local("qw", wst.at[pl.ds(start, n)], wc_hbm.at[j, pl.ds(start, n)])
            cp.start()
            cp.wait()

        def w_first():
            for j in (0, 1):
                @pl.when(d[j] == 0)
                def _(j=j):
                    cp = local("q", q_hbm, wst.at[pl.ds(0, NSLOT)])
                    cp.start()
                    cp.wait()
                    quantize(j, x * QTR, QTR)
                    W0[j].start()
                    W1[j].start()
                    quantize(j, YLO, YN)
                    U0[j].start()
                    U1[j].start()
                    for q in (xp, xo, xm):
                        quantize(j, q * QTR, QTR)

        def w_second():
            for j in (0, 1):
                @pl.when(d[j] == 1)
                def _(j=j):
                    W0[j].wait_recv()
                    W2[j].start()
                    W4[j].start()
                    W5[j].start()

                @pl.when(d[j] == 3)
                def _(j=j):
                    W1[j].wait_recv()
                    W3[j].start()
                    W4[j].start()
                    W5[j].start()

        def w_third():
            for j in (0, 1):
                @pl.when(d[j] == 2)
                def _(j=j):
                    W2[j].wait_recv()
                    W3[j].wait_recv()
                    W4[j].start()
                    W5[j].start()

        def w_relay():
            for j in (0, 1):
                @pl.when(d[j] == 1)
                def _(j=j):
                    U0[j].wait_recv()
                    U2[j].start()

                @pl.when(d[j] == 3)
                def _(j=j):
                    U1[j].wait_recv()
                    U3[j].start()

        def w_fourth():
            for j in (0, 1):
                @pl.when(d[j] != 0)
                def _(j=j):
                    W4r[j].wait_recv()
                    W6[j].start()
                    W5r[j].wait_recv()
                    W7[j].start()

        def w_load(j):
            @pl.when(d[j] != 0)
            def _():
                W6r[j].wait_recv()
                W7r[j].wait_recv()

            @pl.when(d[j] == 2)
            def _():
                U2[j].wait_recv()
                U3[j].wait_recv()

            local("w", wc_hbm.at[j], wst.at[pl.ds(0, NSLOT)]).start()

        def w_ready(j):
            local("w", wc_hbm.at[j], wst.at[pl.ds(0, NSLOT)]).wait()

        def grads(j, chips, more, hooks):
            @pl.loop(0, 16)
            def _(r):
                rows = pl.ds(pl.multiple_of(r * 256, 256), 256)
                g = None
                for zz in chips:
                    ks = pl.ds(pl.multiple_of(zz * 256, 256), 256)
                    term = lax.dot_general(
                        tok_v[ks, rows], cb[j, ks, :], (((0,), (0,)), ((), ())), preferred_element_type=F32
                    )
                    g = term if g is None else g + term
                for h in (0, 1):
                    for c in range(COLS):
                        at = (r * 2 + h) * COLS + c
                        block = g[h * BS:(h + 1) * BS, c * BS:(c + 1) * BS]
                        if more:
                            block = block + gw[at].astype(F32)
                        gw[at] = block.astype(BF16)
                for at, steps in hooks.items():
                    @pl.when(r == at)
                    def _(steps=steps):
                        for step in steps:
                            step()

        def pick(j, o):
            @pl.loop(0, SLOTS)
            def _(s):
                gs[j, o, s] = gw[tabs[j, o, s]]

        def assemble(j):
            @pl.loop(0, ROWS)
            def _(r):
                for c in range(COLS):
                    gw[r * COLS + c] = wst[invs[j, r // 16, (r % 16) * 8 + c]]

        def forward(j, lo_m, hi_m, hooks):
            @pl.loop(lo_m, hi_m)
            def _(m):
                zz = (z + jnp.where(m == 0, 2, jnp.where(m == 1, 1, jnp.where(m == 2, 3, 0)))) % 4
                rows = pl.ds(pl.multiple_of(zz * 256, 256), 256)
                w = jnp.concatenate(
                    [jnp.concatenate([gw[r * COLS + c] for c in range(COLS)], axis=1) for r in range(ROWS)], axis=0
                )
                o = jnp.dot(tok_v[rows, :], w, preferred_element_type=F32)
                ob[j, rows, :] = o.astype(BF16)
                for at, steps in hooks.items():
                    @pl.when(m == at)
                    def _(steps=steps):
                        for step in steps:
                            step()

        o_own = [local(f"o{j}", ob.at[j, slot(z, k)], out_hbm.at[:, cols(2 * k + j, z)]) for j in (0, 1)]
        o_sends = []
        for j in (0, 1):
            dst = out_hbm.at[:, cols(2 * k + j, z)]
            row = []
            row.append(remote(f"O3{j}", ob.at[j, slot(zo, 0)], orel.at[0, j], "z+"))
            row.append(remote(f"O4{j}", ob.at[j, slot(zo, 1)], orel.at[1, j], "z-"))
            for i in (0, 1):
                row.append(remote(f"O1{j}{i}", ob.at[j, slot(zp, i)], dst, f"z+{i}", rkey=f"O1r{j}", roff=k, rwidth=2))
            for i in (0, 1):
                row.append(remote(f"O2{j}{i}", ob.at[j, slot(zm, i)], dst, f"z-{i}", rkey=f"O2r{j}", roff=k, rwidth=2))
            row.append(remote(f"O0{j}", ob.at[j, slot(z, kk)], dst, "p"))
            o_sends.append(row)
        O3r = [remote(f"O3{j}", orel.at[0, j], orel.at[0, j], "z+") for j in (0, 1)]
        O4r = [remote(f"O4{j}", orel.at[1, j], orel.at[1, j], "z-") for j in (0, 1)]
        O5 = [remote(f"O5{j}", orel.at[0, j], out_hbm.at[:, cols(2 * k + j, zm)], "z+0", rkey=f"O5r{j}", roff=k, rwidth=2) for j in (0, 1)]
        O6 = [remote(f"O6{j}", orel.at[1, j], out_hbm.at[:, cols(2 * k + j, zp)], "z-1", rkey=f"O5r{j}", roff=k, rwidth=2) for j in (0, 1)]

        def o_recvs(j):
            src = ob.at[j, slot(z, 0)]
            out = [remote(f"O0{j}", src, out_hbm.at[:, cols(2 * kk + j, z)], "p")]
            for i in (0, 1):
                out.append(remote(f"O1{j}0", src, out_hbm.at[:, cols(2 * i + j, zm)], "z+", rkey=f"O1r{j}", roff=i, rwidth=2))
                out.append(remote(f"O2{j}0", src, out_hbm.at[:, cols(2 * i + j, zp)], "z-", rkey=f"O2r{j}", roff=i, rwidth=2))
                out.append(remote(f"O5{j}", src, out_hbm.at[:, cols(2 * i + j, zo)], "z+", rkey=f"O5r{j}", roff=i, rwidth=2))
            return out

        def add1(dst, src, n):
            @pl.loop(0, n)
            def _(i):
                dst[i] = (dst[i].astype(F32) + src[i].astype(F32)).astype(BF16)

        def add2(dst, a, b, n):
            @pl.loop(0, n)
            def _(i):
                dst[i] = (dst[i].astype(F32) + a[i].astype(F32) + b[i].astype(F32)).astype(BF16)

        def sum3(out, dst, a, b, count):
            @pl.loop(0, SLOTS)
            def _(i):
                live = jnp.minimum(jnp.maximum(count - i, 0), 1).astype(F32)
                out[i] = (dst[i].astype(F32) + a[i].astype(F32) + b[i].astype(F32)) * live

        lo, hi = pl.ds(0, LO), pl.ds(LO, HI)

        class XStage:
            def __init__(self, name, j, base, first, second):
                self.j, self.base = j, base
                self.first = first
                self.c0 = remote(f"{name}0", gs.at[j, base + xo, lo], first.at[0], "x+")
                self.c1 = remote(f"{name}1", gs.at[j, base + xo, hi], first.at[1, pl.ds(0, HI)], "x-")
                self.c2l = remote(f"{name}2l", gs.at[j, base + xp, lo], second.at[0, lo], "x+")
                self.c2h = remote(f"{name}2h", gs.at[j, base + xp, hi], second.at[0, hi], "x+")
                self.c3l = remote(f"{name}3l", gs.at[j, base + xm, lo], second.at[1, lo], "x-")
                self.c3h = remote(f"{name}3h", gs.at[j, base + xm, hi], second.at[1, hi], "x-")

            def start(self, which=(0, 1, 2)):
                for i in which:
                    for copy in ((self.c0, self.c1), (self.c2h,), (self.c3l,))[i]:
                        copy.start()

            def middle(self):
                self.c0.wait_recv()
                add1(gs.at[self.j, self.base + xp, lo], self.first.at[0], LO)
                self.c2l.start()
                self.c1.wait_recv()
                add1(gs.at[self.j, self.base + xm, hi], self.first.at[1], HI)
                self.c3h.start()

            def arrive(self):
                for copy in (self.c2h, self.c3l, self.c2l, self.c3h):
                    copy.wait_recv()

            def sends(self):
                return [self.c0, self.c1, self.c2l, self.c2h, self.c3l, self.c3h]

        class YStage:
            def __init__(self, name, j, src, low, high, relay, high_relay, second, add):
                self.j, self.add, self.relay = j, add, relay
                self.low, self.high = src.at[low], src.at[high]
                self.c0 = remote(f"{name}0", self.low, relay, "y+")
                self.c1 = remote(f"{name}1", self.high, high_relay, "y-")
                self.c2l = remote(f"{name}2l", self.low, second.at[0].at[low], "y+")
                self.c2h = remote(f"{name}2h", self.high, second.at[0].at[high], "y+")
                self.c3l = remote(f"{name}3l", self.low, second.at[1].at[low], "y-")
                self.c3h = remote(f"{name}3h", self.high, second.at[1].at[high], "y-")

            def start(self):
                @pl.when(d[self.j] == 2)
                def _():
                    self.c0.start()
                    self.c1.start()

                @pl.when(d[self.j] == 3)
                def _():
                    self.c2h.start()

                @pl.when(d[self.j] == 1)
                def _():
                    self.c3l.start()

            def middle(self):
                @pl.when(d[self.j] == 3)
                def _():
                    self.c0.wait_recv()
                    self.add(self.low, self.relay, 0)
                    self.c2l.start()

                @pl.when(d[self.j] == 1)
                def _():
                    self.c1.wait_recv()
                    self.add(self.high, self.relay, 1)
                    self.c3h.start()

            def arrive(self):
                for copy in (self.c2h, self.c3l, self.c2l, self.c3h):
                    copy.wait_recv()

            def wait_sends(self):
                @pl.when(d[self.j] == 2)
                def _():
                    self.c0.wait_send()
                    self.c1.wait_send()

                @pl.when(d[self.j] == 3)
                def _():
                    self.c2h.wait_send()
                    self.c2l.wait_send()

                @pl.when(d[self.j] == 1)
                def _():
                    self.c3l.wait_send()
                    self.c3h.wait_send()

        AX = [XStage(f"A{j}", j, 0, ra1.at[j], ra2.at[j]) for j in (0, 1)]
        def add_ay(dst, src, half):
            add1(dst, src, (LO, HI)[half])

        AY = [YStage(f"Y{j}", j, gs.at[j, x], lo, hi, ry1, ry1.at[pl.ds(0, HI)], ry2, add_ay) for j in (0, 1)]
        order = (xo, xp, xm, x)
        BY = [
            [YStage(f"Z{j}{i}", j, gs.at[j, 4 + q], lo, hi, rz1.at[i], rz1.at[i, pl.ds(0, HI)], rz2.at[i], add_ay)
             for i, q in enumerate(order)]
            for j in (0, 1)
        ]
        BX = [XStage(f"B{j}", j, 4, rb1, rb2) for j in (0, 1)]

        def ax_end(j):
            AX[j].arrive()
            add2(gs.at[j, x], ra2.at[j, 0], ra2.at[j, 1], SLOTS)
            AY[j].start()

        def by_end(j, i):
            def go():
                @pl.when(d[j] == 0)
                def _():
                    BY[j][i].arrive()
                    add2(gs.at[j, 4 + order[i]], rz2.at[i, 0], rz2.at[i, 1], SLOTS)
                    if i < 3:
                        BX[j].start((i,))
            return go

        def bx_middle(j):
            @pl.when(d[j] == 0)
            def _():
                BX[j].middle()

        g_own = local("g", fin.at[k], wg_hbm)
        G = remote("G", fin.at[kk], wg_hbm, "p")

        def fin_out(half):
            @pl.when(k == half)
            def _():
                g_own.start()

            @pl.when(k != half)
            def _():
                G.start()

        def final_a(j):
            @pl.when(d[j] == 0)
            def _():
                AY[j].arrive()
                sum3(fin.at[0], gs.at[j, x], ry2.at[0], ry2.at[1], tabs[j, 0, 32 + x])
                fin_out(0)

        def final_b(j):
            @pl.when(d[j] == 0)
            def _():
                BX[j].arrive()
                sum3(fin.at[1], gs.at[j, 4 + x], rb2.at[0], rb2.at[1], tabs[j, 0, 36 + x])
                fin_out(1)

        def o_start(j, *which):
            def go():
                for i in which:
                    if i < 0:
                        o_own[j].start()
                    else:
                        o_sends[j][i].start()
            return go

        def o_hooks(j):
            return {0: [o_start(j, 0, 1)], 1: [o_start(j, 2, 3)], 2: [o_start(j, 4, 5)], 3: [o_start(j, 6, -1)]}

        def o_relay(j):
            O3r[j].wait_recv()
            O5[j].start()
            O4r[j].wait_recv()
            O6[j].start()

        def c_relay(j):
            C3r[j].wait_recv()
            C5[j].start()
            C4r[j].wait_recv()
            C6[j].start()

        def reduce_start(j):
            for i, q in enumerate(order):
                pick(j, q)
                if i < 3:
                    AX[j].start((i,))
                pick(j, 4 + q)
                BY[j][i].start()

        t_own.start()
        for copy in (T0, T1, T2):
            copy.start()
        tab_start()
        for copy in c_sends[0] + c_own:
            copy.start()
        w_first()
        wst[NSLOT] = jnp.zeros((BS, BS), BF16)
        tab_finish()
        w_second()
        w_third()
        T0r.wait_recv()
        T5.start()
        T3.start()
        T1r.wait_recv()
        T6.start()
        T4.start()
        inv = local("inv", invv, invs)
        inv.start()
        c_relay(0)
        for copy in c_sends[1]:
            copy.start()
        w_relay()
        t_own.wait()
        inv.wait()
        for copy in (T2r, T3r, T4r):
            copy.wait_recv()
        c_near(0)
        near, far = (z, zp, zm), (zo,)
        grads(0, near, False, {8: [w_fourth]})
        T5r.wait_recv()
        T7.start()
        T6r.wait_recv()
        T8.start()
        T7r.wait_recv()
        T8r.wait_recv()
        c_far(0)
        grads(0, far, True, {12: [lambda: c_relay(1)]})
        reduce_start(0)
        w_load(0)
        c_near(1)
        grads(1, near, False, {6: [BY[0][0].middle], 10: [BY[0][1].middle], 13: [AX[0].middle]})
        BY[0][2].middle()
        c_far(1)
        grads(1, far, True, {8: [BY[0][3].middle]})
        reduce_start(1)
        w_ready(0)
        assemble(0)
        w_load(1)
        hooks = o_hooks(0)
        hooks[0] += [lambda: ax_end(0)]
        hooks[3] += [AX[1].middle, AY[0].middle]
        forward(0, 0, 4, hooks)
        w_ready(1)
        assemble(1)
        for i in range(4):
            by_end(0, i)()
        BY[1][0].middle()
        o_relay(0)
        hooks = o_hooks(1)
        hooks[1] += [BY[1][1].middle]
        hooks[2] += [BY[1][2].middle]
        hooks[3] += [BY[1][3].middle]
        hooks[3] += [lambda: ax_end(1)]
        forward(1, 0, 4, hooks)
        by_end(1, 0)()
        by_end(1, 1)()
        AY[1].middle()
        bx_middle(0)
        by_end(1, 2)()
        o_relay(1)
        final_a(0)
        bx_middle(1)
        by_end(1, 3)()
        final_b(0)
        final_a(1)
        final_b(1)

        for j in (0, 1):
            for copy in o_recvs(j):
                copy.wait_recv()
            o_own[j].wait()

        own_final = (y // 2) == k

        @pl.when(own_final)
        def _():
            g_own.wait()
            G.wait_send()

        @pl.when(jnp.logical_not(own_final))
        def _():
            G.wait_recv()

        for copy in (T0, T1, T2, T3, T4, T5, T6, T7, T8):
            copy.wait_send()
        for j in (0, 1):
            for copy in c_sends[j] + [C5[j], C6[j]] + o_sends[j] + [O5[j], O6[j]] + AX[j].sends():
                copy.wait_send()
            AY[j].wait_sends()
            for i in range(4):
                BY[j][i].wait_sends()

            @pl.when(d[j] == 0)
            def _(j=j):
                for copy in [W0[j], W1[j], U0[j], U1[j]] + V[j] + BX[j].sends():
                    copy.wait_send()

            @pl.when(d[j] == 1)
            def _(j=j):
                W2[j].wait_send()
                U2[j].wait_send()

            @pl.when(d[j] == 3)
            def _(j=j):
                W3[j].wait_send()
                U3[j].wait_send()

            @pl.when(d[j] != 0)
            def _(j=j):
                for copy in (W4[j], W5[j], W6[j], W7[j]):
                    copy.wait_send()

    return kernel


def shards(tokens, cotangent, master, block_ids, live_count):
    owners, slots = block_ids.shape
    table = jnp.pad(block_ids, ((0, 0), (0, 128 - slots))) + jnp.pad(live_count.reshape(1, owners), ((0, 7), (32, 96 - owners)))
    vmem = pltpu.VMEM
    blk = (BS, BS)
    anyspec = pl.BlockSpec(memory_space=pl.ANY)
    outputs, w_grad, _ = pl.pallas_call(
        make_kernel(Names(), Names(), Names()),
        out_shape=(
            jax.ShapeDtypeStruct(cotangent.shape, BF16),
            jax.ShapeDtypeStruct((slots,) + blk, F32),
            jax.ShapeDtypeStruct((2, NSLOT) + blk, BF16),
        ),
        in_specs=[anyspec] * 4,
        out_specs=(anyspec,) * 3,
        scratch_shapes=[
            vmem((8 * TOK, ROWS * BS), BF16),
            vmem((2, 8 * TOK, WID), BF16),
            vmem((2, 2, TOK, WID), BF16),
            vmem((ROWS * COLS,) + blk, BF16),
            vmem((NSLOT + 1,) + blk, BF16),
            vmem((2, 8 * TOK, WID), BF16),
            vmem((2, 2, TOK, WID), BF16),
            vmem((2, OWN, SLOTS) + blk, BF16),
            vmem((2, 2, LO) + blk, BF16),
            vmem((2, 2, SLOTS) + blk, BF16),
            vmem((LO,) + blk, BF16),
            vmem((2, SLOTS) + blk, BF16),
            vmem((4, LO) + blk, BF16),
            vmem((4, 2, SLOTS) + blk, BF16),
            vmem((2, LO) + blk, BF16),
            vmem((2, SLOTS) + blk, BF16),
            vmem((2, SLOTS) + blk, F32),
            vmem((2, 8, 128), jnp.int32),
            pltpu.SMEM((2, 8, 128), jnp.int32),
            vmem((2, 8, 128), jnp.int32),
            pltpu.SMEM((2, 8, 128), jnp.int32),
            pltpu.SemaphoreType.DMA((184,)),
            pltpu.SemaphoreType.DMA((184,)),
            pltpu.SemaphoreType.DMA((20,)),
        ],
        compiler_params=pltpu.CompilerParams(
            collective_id=0, has_side_effects=True, vmem_limit_bytes=66 * 1024 * 1000
        ),
    )(tokens, cotangent, master.reshape(owners * slots, BS, BS), table)
    return finish(outputs, w_grad)


def finish(outputs, w_grad):
    n_o, n_g = 8, 3
    rows, each = outputs.shape[0] // n_o, SLOTS // n_g

    def body(o_ref, g_ref, o_out, g_out, o_v, g_v, in_sem, out_sem):
        loads, stores = [], []
        for i in range(n_o):
            part = pl.ds(i * rows, rows)
            loads.append(pltpu.make_async_copy(o_ref.at[part], o_v.at[part], in_sem.at[i]))
            stores.append(pltpu.make_async_copy(o_v.at[part], o_out.at[part], out_sem.at[i]))
        for i in range(n_g):
            part = pl.ds(i * each, each)
            loads.append(pltpu.make_async_copy(g_ref.at[part], g_v.at[part], in_sem.at[n_o + i]))
            stores.append(pltpu.make_async_copy(g_v.at[part], g_out.at[part], out_sem.at[n_o + i]))
        for load in loads:
            load.start()
        for load, store in zip(loads, stores):
            load.wait()
            store.start()
        for store in stores:
            store.wait()

    anyspec = pl.BlockSpec(memory_space=pl.ANY)
    outputs, w_grad = pl.pallas_call(
        body,
        out_shape=(
            jax.ShapeDtypeStruct(outputs.shape, outputs.dtype),
            jax.ShapeDtypeStruct(w_grad.shape, w_grad.dtype),
        ),
        in_specs=[anyspec] * 2,
        out_specs=(anyspec,) * 2,
        scratch_shapes=[
            pltpu.VMEM(outputs.shape, outputs.dtype),
            pltpu.VMEM(w_grad.shape, w_grad.dtype),
            pltpu.SemaphoreType.DMA((n_o + n_g,)),
            pltpu.SemaphoreType.DMA((n_o + n_g,)),
        ],
    )(outputs, w_grad)
    return outputs, w_grad[None]


def solution(mesh):
    return jax.shard_map(
        shards,
        mesh=mesh,
        in_specs=(
            P(("dp", "seq", "tensor"), None),
            P(("dp", "seq", "tensor"), None),
            P(None, "tensor", None, None),
            P(None, "tensor"),
            P(None, "tensor"),
        ),
        out_specs=(P(("dp", "seq", "tensor"), None), P(("dp", "seq"), "tensor", None, None)),
        check_vma=False,
    )
```
